128 devices in a mesh: row: 4 (over y), col: 16 (over x_hi, z, core), rep: 2 (over x_lo).
Axes of the slice: x: 4 (x_hi: 2, x_lo: 2; x = x_hi * 2 + x_lo), y: 4, z: 4, core: 2. Of those that a mesh axis runs over, the one named last changes fastest.
Arguments:
- features: bfloat16 [2, 128, 512, 512], P('rep', 'row', 'col'), may hold values from -6 to 6
- cotangent: bfloat16 [2, 128, 512, 512], P('rep', 'row', 'col'), may hold values from -6 to 6
- depthwise_filters: float32 [2, 7, 7, 512], replicated, may hold values from -0.875 to 0.875
- depthwise_bias_vector: float32 [2, 512], replicated, may hold values from -1.5 to 1.5
- layernorm_gain: float32 [2, 512], replicated, may hold values from 0.5 to 1.5
- layernorm_shift: float32 [2, 512], replicated, may hold values from -1.5 to 1.5
- inner_frozen_weight: bfloat16 [2, 512, 2048], replicated, may hold values from -0.25 to 0.25
- outer_frozen_weight: bfloat16 [2, 2048, 512], replicated, may hold values from -0.125 to 0.125
- inner_down_factor: bfloat16 [2, 512, 16], replicated, may hold values from -0.25 to 0.25
- inner_up_factor: bfloat16 [2, 16, 2048], replicated, may hold values from -0.75 to 0.75
- outer_down_factor: bfloat16 [2, 2048, 16], replicated, may hold values from -0.125 to 0.125
- outer_up_factor: bfloat16 [2, 16, 512], replicated, may hold values from -0.75 to 0.75
- branch_channel_scale: float32 [2, 512], replicated, may hold values from 0.2 to 1
Outputs:
- features_out: bfloat16 [2, 128, 512, 512], P('rep', 'row', 'col')
- step_a_in: float32 [2, 512, 16], replicated
- step_b_in: float32 [2, 16, 2048], replicated
- step_a_out: float32 [2, 2048, 16], replicated
- step_b_out: float32 [2, 16, 512], replicated
The draws below stay inside these ranges and needn't reach their ends.
All inputs are finite; a program needn't handle non-finite values.
Results may differ from the reference program's by a relative error of at most 0.013.
Values may be sent and summed in bfloat16 or wider, within the bound.
No kernel may reach another device: no remote copies, remote signals or barrier semaphores. Data moves between devices by JAX's collectives and lax.ppermute only.
A program may use at most 128 MiB of HBM per device.

```python
import math
import jax
import jax.numpy as jnp
from jax import lax

CHANNEL_COUNT = 512
HIDDEN_UNITS = 2048
ADAPTER_RANK = 16
BLOCK_COUNT = 2
H = 128
W = 512
IMAGES = 2


def levels(stream_key, extent, pieces, smallest, top_value):
    def one(axis_at, parts):
        draws = jax.random.uniform(jax.random.fold_in(jax.random.fold_in(stream_key, 6), axis_at), (parts,), jnp.float32, smallest / len(pieces), top_value / len(pieces))
        return jnp.repeat(jnp.exp(draws), extent[axis_at] // parts).reshape((-1,) + (1,) * (len(extent) - axis_at - 1))

    loudness = one(*pieces[0])
    for cut in pieces[1:]:
        loudness = loudness * one(*cut)
    return loudness


def scatter_about(key, shape, width, limit, split=(), held_as=jnp.bfloat16):
    entries = width * jax.random.normal(key, shape, jnp.float32)
    if split:
        entries = entries * levels(key, shape, split, -0.22, 0.18)
    return jnp.clip(entries, -limit, limit).astype(held_as)


def setup_inputs(seed: int = 0) -> dict:
    seeds = jax.random.split(jax.random.key(seed), 14)
    features = scatter_about(seeds[0], (IMAGES, H, W, CHANNEL_COUNT), 1.0, 6.0, ((0, 2), (1, 4), (2, 16)))
    cotangent = scatter_about(seeds[1], (IMAGES, H, W, CHANNEL_COUNT), 1.0, 6.0, ((0, 2), (1, 4), (2, 16)))
    depthwise_filters = scatter_about(seeds[2], (BLOCK_COUNT, 7, 7, CHANNEL_COUNT), 49 ** -0.5, 0.875, (), jnp.float32)
    depthwise_bias_vector = scatter_about(seeds[3], (BLOCK_COUNT, CHANNEL_COUNT), 0.3, 1.5, (), jnp.float32)
    layernorm_gain = jnp.clip(1.0 + 0.1 * jax.random.normal(seeds[4], (BLOCK_COUNT, CHANNEL_COUNT), jnp.float32), 0.5, 1.5)
    layernorm_shift = scatter_about(seeds[5], (BLOCK_COUNT, CHANNEL_COUNT), 0.3, 1.5, (), jnp.float32)
    inner_frozen_weight = scatter_about(seeds[6], (BLOCK_COUNT, CHANNEL_COUNT, HIDDEN_UNITS), CHANNEL_COUNT ** -0.5, 0.25)
    outer_frozen_weight = scatter_about(seeds[7], (BLOCK_COUNT, HIDDEN_UNITS, CHANNEL_COUNT), HIDDEN_UNITS ** -0.5, 0.125)
    inner_down_factor = scatter_about(seeds[8], (BLOCK_COUNT, CHANNEL_COUNT, ADAPTER_RANK), CHANNEL_COUNT ** -0.5, 0.25)
    inner_up_factor = scatter_about(seeds[9], (BLOCK_COUNT, ADAPTER_RANK, HIDDEN_UNITS), (4 * ADAPTER_RANK) ** -0.5, 0.75)
    outer_down_factor = scatter_about(seeds[10], (BLOCK_COUNT, HIDDEN_UNITS, ADAPTER_RANK), HIDDEN_UNITS ** -0.5, 0.125)
    outer_up_factor = scatter_about(seeds[11], (BLOCK_COUNT, ADAPTER_RANK, CHANNEL_COUNT), (4 * ADAPTER_RANK) ** -0.5, 0.75)
    branch_channel_scale = jnp.clip(jnp.exp(jax.random.uniform(seeds[12], (BLOCK_COUNT, CHANNEL_COUNT), jnp.float32, math.log(0.2), math.log(1.0))), 0.2, 1.0)
    return {"features": features, "cotangent": cotangent, "depthwise_filters": depthwise_filters, "depthwise_bias_vector": depthwise_bias_vector, "layernorm_gain": layernorm_gain, "layernorm_shift": layernorm_shift, "inner_frozen_weight": inner_frozen_weight, "outer_frozen_weight": outer_frozen_weight, "inner_down_factor": inner_down_factor, "inner_up_factor": inner_up_factor, "outer_down_factor": outer_down_factor, "outer_up_factor": outer_up_factor, "branch_channel_scale": branch_channel_scale}


adapter_scale = 2.0
norm_eps = 1e-06
step_eps = 1e-06
gelu_coef = 0.7978845608

def depthwise(padded, kernel, bias, rows, cols):
    total = jnp.zeros(padded.shape[:1] + (rows, cols, padded.shape[3]), jnp.float32) + bias
    for first in range(7):
        for second in range(7):
            total = total + padded[:, first:first + rows, second:second + cols, :].astype(jnp.float32) * kernel[first, second]
    return total

def gelu_parts(preactivation):
    inner = gelu_coef * (preactivation + 0.044715 * preactivation * preactivation * preactivation)
    tangent = jnp.tanh(inner)
    value = 0.5 * preactivation * (1.0 + tangent)
    activation_slope = 0.5 * (1.0 + tangent) + 0.5 * preactivation * (1.0 - tangent * tangent) * gelu_coef * (1.0 + 3.0 * 0.044715 * preactivation * preactivation)
    return (value, activation_slope)

def multiply_matrices(left, right):
    return jnp.dot(left, right, preferred_element_type=jnp.float32)

def pointwise_forward(flat_block, weights):
    inner_frozen, outer_frozen, inner_down, inner_up, outer_down, outer_up = weights
    inner_middle = multiply_matrices(flat_block, inner_down).astype(jnp.bfloat16)
    preactivation = multiply_matrices(flat_block, inner_frozen) + adapter_scale * multiply_matrices(inner_middle, inner_up)
    value, activation_slope = gelu_parts(preactivation)
    hidden_activation = value.astype(jnp.bfloat16)
    outer_middle = multiply_matrices(hidden_activation, outer_down).astype(jnp.bfloat16)
    branch = multiply_matrices(hidden_activation, outer_frozen) + adapter_scale * multiply_matrices(outer_middle, outer_up)
    return (branch, inner_middle, activation_slope, hidden_activation, outer_middle)

def pointwise_backward(flat_block, output_gradient, weights):
    inner_frozen, outer_frozen, inner_down, inner_up, outer_down, outer_up = weights
    unused_branch, inner_middle, activation_slope, hidden_activation, outer_middle = pointwise_forward(flat_block, weights)
    outer_up_gradient = adapter_scale * multiply_matrices(outer_middle.T, output_gradient)
    outer_mid_gradient = (adapter_scale * multiply_matrices(output_gradient, outer_up.T)).astype(jnp.bfloat16)
    grad_a_out = multiply_matrices(hidden_activation.T, outer_mid_gradient)
    hidden_gradient = multiply_matrices(output_gradient, outer_frozen.T) + multiply_matrices(outer_mid_gradient, outer_down.T)
    preact_gradient = (hidden_gradient * activation_slope).astype(jnp.bfloat16)
    inner_up_gradient = adapter_scale * multiply_matrices(inner_middle.T, preact_gradient)
    inner_mid_gradient = (adapter_scale * multiply_matrices(preact_gradient, inner_up.T)).astype(jnp.bfloat16)
    grad_a_in = multiply_matrices(flat_block.T, inner_mid_gradient)
    normed_gradient = multiply_matrices(preact_gradient, inner_frozen.T) + multiply_matrices(inner_mid_gradient, inner_down.T)
    return (normed_gradient, (grad_a_in, inner_up_gradient, grad_a_out, outer_up_gradient))

def picture_forward_backward(image_tensor, cotangent, depthwise_filters, depthwise_bias_vector, layernorm_gain, layernorm_shift, inner_frozen_weight, outer_frozen_weight, inner_down_factor, inner_up_factor, outer_down_factor, outer_up_factor, branch_channel_scale):
    rows, cols, chans = (image_tensor.shape[1], image_tensor.shape[2], image_tensor.shape[3])
    pixel_total = rows * cols
    group_rows = math.gcd(pixel_total, 2048)
    group_count = pixel_total // group_rows
    current = image_tensor
    saved_activations = []
    for block_layer in range(BLOCK_COUNT):
        weights = (inner_frozen_weight[block_layer], outer_frozen_weight[block_layer], inner_down_factor[block_layer], inner_up_factor[block_layer], outer_down_factor[block_layer], outer_up_factor[block_layer])
        padded = jnp.pad(current, ((0, 0), (3, 3), (3, 3), (0, 0)))
        conv = depthwise(padded, depthwise_filters[block_layer], depthwise_bias_vector[block_layer], rows, cols)
        channel_mean = lax.optimization_barrier(jnp.mean(conv, -1, keepdims=True))
        centered_input = conv - channel_mean
        inverse_deviation = lax.rsqrt(lax.optimization_barrier(jnp.mean(centered_input * centered_input, -1, keepdims=True)) + norm_eps)
        standardized_input = centered_input * inverse_deviation
        normed_features = (standardized_input * layernorm_gain[block_layer] + layernorm_shift[block_layer]).astype(jnp.bfloat16)
        grouped_pixels = normed_features.reshape(group_count, group_rows, chans)
        residual_branch = lax.map(lambda flat_block: pointwise_forward(flat_block, weights)[0], grouped_pixels)
        current = (current.astype(jnp.float32) + branch_channel_scale[block_layer] * residual_branch.reshape(current.shape)).astype(jnp.bfloat16)
        saved_activations.append((grouped_pixels, standardized_input, inverse_deviation))
    grad_x = cotangent.astype(jnp.float32)
    adapter_gradients = [None] * BLOCK_COUNT
    for block_layer in range(BLOCK_COUNT - 1, -1, -1):
        weights = (inner_frozen_weight[block_layer], outer_frozen_weight[block_layer], inner_down_factor[block_layer], inner_up_factor[block_layer], outer_down_factor[block_layer], outer_up_factor[block_layer])
        grouped_pixels, standardized_input, inverse_deviation = saved_activations[block_layer]
        output_gradient = (grad_x * branch_channel_scale[block_layer]).astype(jnp.bfloat16).reshape(group_count, group_rows, chans)
        initial = (jnp.zeros(inner_down_factor.shape[1:], jnp.float32), jnp.zeros(inner_up_factor.shape[1:], jnp.float32), jnp.zeros(outer_down_factor.shape[1:], jnp.float32), jnp.zeros(outer_up_factor.shape[1:], jnp.float32))

        def accumulate(carry, inputs):
            normed_gradient, gradients = pointwise_backward(inputs[0], inputs[1], weights)
            return (tuple((carry[which] + gradients[which] for which in range(4))), normed_gradient)
        totals, normed_gradient = lax.scan(accumulate, initial, (grouped_pixels, output_gradient))
        adapter_gradients[block_layer] = totals
        if block_layer > 0:
            scaled_branch = normed_gradient.reshape(standardized_input.shape) * layernorm_gain[block_layer]
            conv_gradient = inverse_deviation * (scaled_branch - lax.optimization_barrier(jnp.mean(scaled_branch, -1, keepdims=True)) - standardized_input * lax.optimization_barrier(jnp.mean(scaled_branch * standardized_input, -1, keepdims=True)))
            conv_gradient = conv_gradient.astype(jnp.bfloat16)
            padded = jnp.pad(conv_gradient, ((0, 0), (3, 3), (3, 3), (0, 0)))
            flipped = depthwise_filters[block_layer][::-1, ::-1, :]
            grad_x = grad_x + depthwise(padded, flipped, jnp.zeros((chans,), jnp.float32), rows, cols)
    return (current, adapter_gradients)

def normalize(stacked):
    channel_mean = lax.optimization_barrier(jnp.mean(stacked * stacked, axis=(1, 2), keepdims=True))
    return stacked * lax.rsqrt(channel_mean + step_eps)

def reference(features, cotangent, depthwise_filters, depthwise_bias_vector, layernorm_gain, layernorm_shift, inner_frozen_weight, outer_frozen_weight, inner_down_factor, inner_up_factor, outer_down_factor, outer_up_factor, branch_channel_scale):
    outputs = []
    totals = None
    for picture_index in range(IMAGES):
        step_result, adapter_gradients = picture_forward_backward(features[picture_index:picture_index + 1], cotangent[picture_index:picture_index + 1], depthwise_filters, depthwise_bias_vector, layernorm_gain, layernorm_shift, inner_frozen_weight, outer_frozen_weight, inner_down_factor, inner_up_factor, outer_down_factor, outer_up_factor, branch_channel_scale)
        outputs.append(step_result)
        stacked = [jnp.stack([adapter_gradients[block_layer][which] for block_layer in range(BLOCK_COUNT)]) for which in range(4)]
        totals = stacked if totals is None else [totals[which] + stacked[which] for which in range(4)]
    features_out = jnp.concatenate(outputs, 0)
    return (features_out, normalize(totals[0]), normalize(totals[1]), normalize(totals[2]), normalize(totals[3]))
```

```python
import jax
import jax.numpy as jnp
from jax import lax
from jax.experimental import pallas as pl
from jax.experimental.pallas import tpu as pltpu
from jax.sharding import PartitionSpec as P

BLOCK_COUNT = 2
ROWS, COLS, CHANS, HIDDEN, RANK = 32, 32, 512, 2048, 16
PIXELS = ROWS * COLS
GROUPS = CHANS // 128
HALF = COLS // 2
SPAN = 32
OFFSET = 5
TILE = 256
CHUNK = 512

adapter_scale = 2.0
norm_eps = 1e-06
step_eps = 1e-06
gelu_coef = 0.7978845608
f32, bf16 = jnp.float32, jnp.bfloat16


def dot(a, b):
    return jnp.dot(a, b, preferred_element_type=f32)


def dot_t(a, b):
    return lax.dot_general(a, b, (((1,), (1,)), ((), ())), preferred_element_type=f32)


def t_dot(a, b):
    return lax.dot_general(a, b, (((0,), (0,)), ((), ())), preferred_element_type=f32)


def spread(xs, row, values, blocks):
    for k, g, half, at in blocks:
        start = (row * SPAN + at) * 8 + half * GROUPS + g
        xs[pl.ds(start, 8, stride=8), :] = values[8 * k : 8 * k + 8, 128 * g : 128 * g + 128]


CENTRE = [(k, g, 0, 8 * k + 8) for k in (0, 1, 2) for g in range(GROUPS)] + [
    (k, g, 1, 8 * k - 8) for k in (1, 2, 3) for g in range(GROUPS)
]


def fill(xs, x_ref, n_ref, s_ref, w_ref, e_ref):
    def centre(i, c):
        spread(xs, i + 3, x_ref[i].astype(f32), CENTRE)
        return c

    lax.fori_loop(0, ROWS, centre, 0)
    for i in range(3):
        spread(xs, i, n_ref[i].astype(f32), CENTRE)
        spread(xs, ROWS + 3 + i, s_ref[i].astype(f32), CENTRE)
    for side, half, at in ((w_ref, 0, OFFSET), (e_ref, 1, 3 + 16 + OFFSET)):
        for c in range(3):
            v = side[c].astype(f32)
            for r in range(0, 40, 8):
                for g in range(GROUPS):
                    start = (r * SPAN + at + c) * 8 + half * GROUPS + g
                    xs[pl.ds(start, 8, stride=8 * SPAN), :] = v[r : r + 8, 128 * g : 128 * g + 128]


def conv_row(xs, cv, taps, first, i):
    totals = [first] * HALF
    for a in range(7):
        base = pl.multiple_of((i + a) * (SPAN * 8), SPAN * 8)
        line = [xs[pl.ds(base + (OFFSET + c) * 8, 8), :] for c in range(HALF + 6)]
        for b in range(7):
            tap = taps[a * 7 + b]
            for c in range(HALF):
                totals[c] = totals[c] + line[c + b] * tap
    base = pl.multiple_of(i * (HALF * 8), HALF * 8)
    for c in range(HALF):
        cv[pl.ds(base + c * 8, 8), :] = totals[c]
    parts = []
    for k in range(4):
        start = base + (k % 2) * 64 + (k // 2) * GROUPS
        parts.append(
            jnp.concatenate([cv[pl.ds(start + g, 8, stride=8), :] for g in range(GROUPS)], axis=1)
        )
    return jnp.concatenate(parts, axis=0)


def gelu_parts(v):
    square = v * v
    t = jnp.tanh(v * (gelu_coef + (gelu_coef * 0.044715) * square))
    h = 0.5 * t + 0.5
    value = v * h
    slope = h + value * (1.0 - t) * (gelu_coef + (3.0 * 0.044715 * gelu_coef) * square)
    return value, slope


def row_of(i):
    return pl.ds(pl.multiple_of(i * COLS, COLS), COLS)


def norm_rows(xs, cv, taps, bias, gain, shift, nrm, xh=None, rs=None):
    def body(i, c):
        conv = conv_row(xs, cv, taps, bias[...], i)
        centred = conv - jnp.mean(conv, -1, keepdims=True)
        inverse = lax.rsqrt(jnp.mean(centred * centred, -1, keepdims=True) + norm_eps)
        standard = centred * inverse
        nrm[row_of(i), :] = (standard * gain[...] + shift[...]).astype(bf16)
        if xh is not None:
            xh[row_of(i), :] = standard
            rs[row_of(i), :] = jnp.broadcast_to(inverse, (COLS, 128))
        return c

    lax.fori_loop(0, ROWS, body, 0)


def tiles(body):
    def step(t, c):
        body(pl.ds(pl.multiple_of(t * TILE, TILE), TILE))
        return c

    lax.fori_loop(0, PIXELS // TILE, step, 0)


def fold_kernel(win, ain, bin_, wout, aout, bout, win_out, wout_out):
    win_out[0] = (win[0].astype(f32) + adapter_scale * dot(ain[0], bin_[0])).astype(bf16)
    wout_out[0] = (wout[0].astype(f32) + adapter_scale * dot(aout[0], bout[0])).astype(bf16)


def first_kernel(
    x, n, s, w, e, taps, bias, gain, shift, win, wout, ain, aout, scale,
    y, nrm, hid, slope, mid_in, mid_out, xs, cv,
):
    fill(xs, x, n, s, w, e)
    norm_rows(xs, cv, taps, bias, gain, shift, nrm)
    xf = x.reshape(PIXELS, CHANS)
    yf = y.reshape(PIXELS, CHANS)

    def body(at):
        nb = nrm[at, :]
        mid_in[at, :] = dot(nb, ain[...]).astype(bf16)
        out = jnp.zeros((TILE, CHANS), f32)
        mid = jnp.zeros((TILE, RANK), f32)
        for c in range(0, HIDDEN, CHUNK):
            cs = slice(c, c + CHUNK)
            value, sl = gelu_parts(dot(nb, win[:, cs]))
            h = value.astype(bf16)
            hid[at, cs] = h
            slope[at, cs] = sl.astype(bf16)
            out = out + dot(h, wout[cs, :])
            mid = mid + dot(h, aout[cs, :])
        mid_out[at, :] = mid.astype(bf16)
        yf[at, :] = (xf[at, :].astype(f32) + scale[...] * out).astype(bf16)

    tiles(body)


def second_kernel(
    x, n, s, w, e, cot, taps, bias, gain, shift, win, wout, ain, bin_, aout, bout, scale,
    y, gc, grads, xs, cv, nrm, xh, rs,
):
    fill(xs, x, n, s, w, e)
    norm_rows(xs, cv, taps, bias, gain, shift, nrm, xh, rs)
    xf = x.reshape(PIXELS, CHANS)
    yf = y.reshape(PIXELS, CHANS)
    cf = cot.reshape(PIXELS, CHANS)
    gf = gc.reshape(PIXELS, CHANS)
    grads[...] = jnp.zeros_like(grads)

    def body(at):
        nb = nrm[at, :]
        go = (cf[at, :].astype(f32) * scale[...]).astype(bf16)
        mid_in = dot(nb, ain[...]).astype(bf16)
        gm_out = (adapter_scale * dot_t(go, bout[...])).astype(bf16)
        out = jnp.zeros((TILE, CHANS), f32)
        gn = jnp.zeros((TILE, CHANS), f32)
        mid = jnp.zeros((TILE, RANK), f32)
        gm_in = jnp.zeros((TILE, RANK), f32)
        for c in range(0, HIDDEN, CHUNK):
            cs = slice(c, c + CHUNK)
            value, sl = gelu_parts(dot(nb, win[:, cs]))
            h = value.astype(bf16)
            gpre = (dot_t(go, wout[cs, :]) * sl).astype(bf16)
            out = out + dot(h, wout[cs, :])
            mid = mid + dot(h, aout[cs, :])
            gn = gn + dot_t(gpre, win[:, cs])
            gm_in = gm_in + dot_t(gpre, bin_[:, cs])
            grads[:, 512 + c : 512 + c + CHUNK] += t_dot(mid_in, gpre)
            grads[:, 2560 + c : 2560 + c + CHUNK] += t_dot(gm_out, h)
        gm_in = (adapter_scale * gm_in).astype(bf16)
        grads[:, 0:512] += t_dot(gm_in, nb)
        grads[:, 4608:5120] += t_dot(mid.astype(bf16), go)
        yf[at, :] = (xf[at, :].astype(f32) + scale[...] * out).astype(bf16)
        u = gn * gain[...]
        standard = xh[at, :]
        m1 = jnp.mean(u, -1, keepdims=True)
        m2 = jnp.mean(u * standard, -1, keepdims=True)
        inverse = jnp.concatenate([rs[at, :]] * GROUPS, axis=1)
        gf[at, :] = (inverse * (u - m1 - standard * m2)).astype(bf16)

    tiles(body)


def third_kernel(
    x, n, s, w, e, cot, taps, scale, wout, bin_, bout, nrm, hid, slope, mid_in, mid_out,
    grads, xs, cv, gos,
):
    fill(xs, x, n, s, w, e)
    zero = jnp.zeros((8, 128), f32)

    def rows(i, c):
        g = cot[i].astype(f32) + conv_row(xs, cv, taps, zero, i)
        gos[row_of(i), :] = (g * scale[...]).astype(bf16)
        return c

    lax.fori_loop(0, ROWS, rows, 0)
    grads[...] = jnp.zeros_like(grads)

    def body(at):
        nb = nrm[at, :]
        go = gos[at, :]
        mi = mid_in[at, :]
        gm_out = (adapter_scale * dot_t(go, bout[...])).astype(bf16)
        gm_in = jnp.zeros((TILE, RANK), f32)
        for c in range(0, HIDDEN, CHUNK):
            cs = slice(c, c + CHUNK)
            gpre = (dot_t(go, wout[cs, :]) * slope[at, cs].astype(f32)).astype(bf16)
            gm_in = gm_in + dot_t(gpre, bin_[:, cs])
            grads[:, 512 + c : 512 + c + CHUNK] += t_dot(mi, gpre)
            grads[:, 2560 + c : 2560 + c + CHUNK] += t_dot(gm_out, hid[at, cs])
        gm_in = (adapter_scale * gm_in).astype(bf16)
        grads[:, 0:512] += t_dot(gm_in, nb)
        grads[:, 4608:5120] += t_dot(mid_out[at, :], go)

    tiles(body)


VMEM = pl.BlockSpec(memory_space=pltpu.VMEM)
PARAMS = dict(compiler_params=pltpu.CompilerParams(vmem_limit_bytes=60 * 2**20))
XS = pltpu.VMEM((40 * SPAN * 8, 128), f32)
CV = pltpu.VMEM((ROWS * HALF * 8, 128), f32)


def call(kernel, outs, scratch, args, name):
    return pl.pallas_call(
        kernel,
        out_shape=[jax.ShapeDtypeStruct(shape, dtype) for shape, dtype in outs],
        in_specs=[VMEM] * len(args),
        out_specs=[VMEM] * len(outs),
        scratch_shapes=scratch,
        name=name,
        **PARAMS,
    )(*args)


def halo(x):
    def shift(v, axis):
        devices = lax.axis_size(axis)
        up = [(i, i + 1) for i in range(devices - 1)]
        return lambda first, last: (
            lax.ppermute(last, axis, up),
            lax.ppermute(first, axis, [(j, i) for i, j in up]),
        )

    north, south = shift(x, "row")(x[:3], x[-3:])
    zeros = jnp.zeros((2, 3, CHANS), x.dtype)

    def strip(cut):
        parts = [north[:, cut], x[:, cut], south[:, cut], zeros]
        return jnp.concatenate(parts, axis=0).transpose(1, 0, 2)

    west, east = shift(x, "col")(strip(slice(0, 3)), strip(slice(COLS - 3, COLS)))
    return x, north, south, west, east


def pair_swap(v, axis, mask):
    n = lax.axis_size(axis)
    return lax.ppermute(v, axis, [(i, i ^ mask) for i in range(n)])


def total(first, second):
    core = lax.axis_index("col") % 2
    mine = jnp.where(core == 0, first, second)
    other = jnp.where(core == 0, second, first).astype(bf16)
    part = (mine + pair_swap(other, "col", 1).astype(f32)).astype(bf16)
    for axis, mask in (("row", 1), ("row", 2), ("col", 2), ("col", 4), ("rep", 1), ("col", 8)):
        part = (part.astype(f32) + pair_swap(part, axis, mask).astype(f32)).astype(bf16)
    back = pair_swap(part, "col", 1)
    return jnp.stack([jnp.where(core == 0, part, back), jnp.where(core == 0, back, part)]).astype(f32)


def normalize(stacked):
    mean = jnp.mean(stacked * stacked, axis=(1, 2), keepdims=True)
    return stacked * lax.rsqrt(mean + step_eps)


def body(
    features,
    cotangent,
    depthwise_filters,
    depthwise_bias_vector,
    layernorm_gain,
    layernorm_shift,
    inner_frozen_weight,
    outer_frozen_weight,
    inner_down_factor,
    inner_up_factor,
    outer_down_factor,
    outer_up_factor,
    branch_channel_scale,
):
    x0 = features.reshape(ROWS, COLS, CHANS)
    cot = cotangent.reshape(ROWS, COLS, CHANS)
    taps = depthwise_filters.reshape(2, 49, GROUPS, 128)
    taps = jnp.concatenate([taps, taps], axis=2)
    bias = depthwise_bias_vector.reshape(2, GROUPS, 128)
    bias = jnp.concatenate([bias, bias], axis=1)
    gain, shift, scale = (
        v.reshape(2, 1, CHANS) for v in (layernorm_gain, layernorm_shift, branch_channel_scale)
    )
    halo0 = halo(x0)

    def whole(*shape):
        return pl.BlockSpec((1,) + shape, lambda i: (i, 0, 0))

    win, wout = pl.pallas_call(
        fold_kernel,
        grid=(2,),
        out_shape=[
            jax.ShapeDtypeStruct((2, CHANS, HIDDEN), bf16),
            jax.ShapeDtypeStruct((2, HIDDEN, CHANS), bf16),
        ],
        in_specs=[
            whole(CHANS, HIDDEN), whole(CHANS, RANK), whole(RANK, HIDDEN),
            whole(HIDDEN, CHANS), whole(HIDDEN, RANK), whole(RANK, CHANS),
        ],
        out_specs=[whole(CHANS, HIDDEN), whole(HIDDEN, CHANS)],
        name="fold",
        **PARAMS,
    )(
        inner_frozen_weight, inner_down_factor, inner_up_factor,
        outer_frozen_weight, outer_down_factor, outer_up_factor,
    )
    ain, bin_, aout, bout = inner_down_factor, inner_up_factor, outer_down_factor, outer_up_factor

    x1, nrm, hid, slope, mid_in, mid_out = call(
        first_kernel,
        [
            ((ROWS, COLS, CHANS), bf16),
            ((PIXELS, CHANS), bf16),
            ((PIXELS, HIDDEN), bf16),
            ((PIXELS, HIDDEN), bf16),
            ((PIXELS, RANK), bf16),
            ((PIXELS, RANK), bf16),
        ],
        [XS, CV],
        [*halo0, taps[0], bias[0], gain[0], shift[0], win[0], wout[0], ain[0], aout[0], scale[0]],
        "first",
    )
    out, gconv, grads1 = call(
        second_kernel,
        [((ROWS, COLS, CHANS), bf16), ((ROWS, COLS, CHANS), bf16), ((RANK, 5120), f32)],
        [
            XS,
            CV,
            pltpu.VMEM((PIXELS, CHANS), bf16),
            pltpu.VMEM((PIXELS, CHANS), f32),
            pltpu.VMEM((PIXELS, 128), f32),
        ],
        [
            *halo(x1), cot, taps[1], bias[1], gain[1], shift[1], win[1], wout[1],
            ain[1], bin_[1], aout[1], bout[1], scale[1],
        ],
        "second",
    )
    (grads0,) = call(
        third_kernel,
        [((RANK, 5120), f32)],
        [XS, CV, pltpu.VMEM((PIXELS, CHANS), bf16)],
        [
            *halo(gconv), cot, taps[1, ::-1], scale[0], wout[0], bin_[0], bout[0],
            nrm, hid, slope, mid_in, mid_out,
        ],
        "third",
    )
    sums = total(grads0, grads1)
    return (
        out[None],
        normalize(sums[:, :, 0:512].transpose(0, 2, 1)),
        normalize(adapter_scale * sums[:, :, 512:2560]),
        normalize(sums[:, :, 2560:4608].transpose(0, 2, 1)),
        normalize(adapter_scale * sums[:, :, 4608:5120]),
    )


def solution(mesh):
    tile = P("rep", "row", "col", None)
    return jax.shard_map(
        body,
        mesh=mesh,
        in_specs=(tile, tile) + (P(),) * 11,
        out_specs=(tile, P(), P(), P(), P()),
        check_vma=False,
    )
```

```python
import functools

import jax
import jax.numpy as jnp
from jax import lax
from jax.experimental import pallas as pl
from jax.experimental.pallas import tpu as pltpu
from jax.sharding import PartitionSpec as P

BLOCK_COUNT = 2
ROWS, COLS, CHANS, HIDDEN, RANK = 32, 32, 512, 2048, 16
PIXELS = ROWS * COLS
GROUPS = CHANS // 128
HALF = COLS // 2
SPAN = 32
OFFSET = 5
TROWS = 8
TILE = TROWS * COLS
CHUNK = 512
STRIP = 48
GRADS = 2 * (CHANS + HIDDEN)

adapter_scale = 2.0
norm_eps = 1e-06
step_eps = 1e-06
gelu_coef = 0.7978845608
f32, bf16 = jnp.float32, jnp.bfloat16


def dot(a, b):
    return jnp.dot(a, b, preferred_element_type=f32)


def dot_t(a, b):
    return lax.dot_general(a, b, (((1,), (1,)), ((), ())), preferred_element_type=f32)


def t_dot(a, b):
    return lax.dot_general(a, b, (((0,), (0,)), ((), ())), preferred_element_type=f32)


CENTRE = [(k, g, 0, 8 * k + 8) for k in (0, 1, 2) for g in range(GROUPS)] + [
    (k, g, 1, 8 * k - 8) for k in (1, 2, 3) for g in range(GROUPS)
]


def spread(xs, row, values):
    for k, g, half, at in CENTRE:
        start = (row * SPAN + at) * 8 + half * GROUPS + g
        xs[pl.ds(start, 8, stride=8), :] = values[8 * k : 8 * k + 8, 128 * g : 128 * g + 128]


def conv_kernel(sources, flip, flags, *refs):
    xrefs, (n, s, taps, bias, cv, xs) = refs[: len(sources)], refs[len(sources) :]
    step = pl.program_id(0)

    @pl.when(step == 0)
    def _():
        zero = jnp.zeros((8, 128), f32)
        for ref, pieces in zip(xrefs, sources):
            for at, row, count in pieces:

                def centre(i, c, ref=ref, at=at, row=row):
                    spread(xs, row + 3 + i, ref[at + i].astype(f32))
                    return c

                lax.fori_loop(0, count, centre, 0)
        for i in range(3):
            spread(xs, i, n[i].astype(f32) * flags[0])
            spread(xs, ROWS + 3 + i, s[i].astype(f32) * flags[1])
        left = lax.broadcasted_iota(jnp.int32, (8, 128), 0) < GROUPS

        def edge(r, c):
            for k in (5, 6, 7):
                at = pl.ds(pl.multiple_of((r * SPAN + k) * 8, 8), 8)
                xs[at, :] = jnp.where(left, zero, xs[at, :])
            for k in (24, 25, 26):
                at = pl.ds(pl.multiple_of((r * SPAN + k) * 8, 8), 8)
                xs[at, :] = jnp.where(left, xs[at, :], zero)
            return c

        lax.fori_loop(0, ROWS + 6, edge, 0)

    def row(i, c):
        first = jnp.zeros((8, 128), f32) if flip else bias[...]
        totals = [first] * HALF
        for a in range(7):
            base = pl.multiple_of((step * TROWS + i + a) * (SPAN * 8), SPAN * 8)
            line = [xs[pl.ds(base + (OFFSET + k) * 8, 8), :] for k in range(HALF + 6)]
            for b in range(7):
                tap = taps[48 - (a * 7 + b) if flip else a * 7 + b]
                for k in range(HALF):
                    totals[k] = totals[k] + line[k + b] * tap
        base = pl.multiple_of(i * (HALF * 8), HALF * 8)
        for k in range(HALF):
            cv[pl.ds(base + k * 8, 8), :] = totals[k]
        return c

    lax.fori_loop(0, TROWS, row, 0)


def hold_strips(he, w, e, flags):
    he[...] = jnp.zeros_like(he)
    for side, ref in ((0, w), (1, e)):
        for c in range(3):
            for block, row in ((4, 0), (5, 35), (0, 3), (2, 11), (3, 19), (1, 27)):
                v = ref[c, 8 * block : 8 * block + 8, :].astype(f32) * flags[2 + side]
                if block >= 4:
                    v = v * flags[block - 4]
                if block == 5:
                    v = v[0:3]
                for g in range(GROUPS):
                    start = (row * 6 + side * 3 + c) * 8 + side * GROUPS + g
                    he[pl.ds(start, v.shape[0], stride=48), :] = v[:, 128 * g : 128 * g + 128]


def whole_row(cv, he, taps, flip, line, tile, i):
    base = pl.multiple_of(i * (HALF * 8), HALF * 8)
    totals = [cv[pl.ds(base + k * 8, 8), :] for k in range(HALF)]
    for a in range(7):
        at = pl.multiple_of((tile * TROWS + i + a) * 48, 48)
        edge = [he[pl.ds(at + 8 * k, 8), :] for k in range(6)]
        pairs = [(k, h, h - k) for k in range(3) for h in range(k, 3)]
        pairs += [(k, 3 + h, 19 + h - k) for k in (13, 14, 15) for h in range(k - 12)]
        for k, h, b in pairs:
            totals[k] = totals[k] + edge[h] * taps[48 - (a * 7 + b) if flip else a * 7 + b]
    for k in range(HALF):
        line[k * 8 : k * 8 + 8, :] = totals[k]
    parts = []
    for k in range(4):
        start = (k % 2) * 64 + (k // 2) * GROUPS
        parts.append(
            jnp.concatenate([line[pl.ds(start + g, 8, stride=8), :] for g in range(GROUPS)], axis=1)
        )
    return jnp.concatenate(parts, axis=0)


def gelu_parts(v):
    square = v * v
    t = jnp.tanh(v * (gelu_coef + (gelu_coef * 0.044715) * square))
    h = 0.5 * t + 0.5
    value = v * h
    slope = h + value * (1.0 - t) * (gelu_coef + (3.0 * 0.044715 * gelu_coef) * square)
    return value, slope


def row_of(i):
    return pl.ds(pl.multiple_of(i * COLS, COLS), COLS)


def norm_rows(cv, he, taps, line, tile, gain, shift, nrm, xh=None, rs=None):
    def body(i, c):
        conv = whole_row(cv, he, taps, False, line, tile, i)
        centred = conv - jnp.mean(conv, -1, keepdims=True)
        inverse = lax.rsqrt(jnp.mean(centred * centred, -1, keepdims=True) + norm_eps)
        standard = centred * inverse
        nrm[row_of(i), :] = (standard * gain[...] + shift[...]).astype(bf16)
        if xh is not None:
            xh[row_of(i), :] = standard
            rs[row_of(i), :] = jnp.broadcast_to(inverse, (COLS, 128))
        return c

    lax.fori_loop(0, TROWS, body, 0)


def put_edges(edge, value, refs, step, inner):
    west, east = refs[-2:]
    if not inner:
        top, bottom = refs[:2]

        @pl.when(step == 0)
        def _():
            top[...] = value[: 3 * COLS].reshape(3, COLS, CHANS).astype(bf16)

        @pl.when(step == 1)
        def _():
            bottom[...] = value[5 * COLS :].reshape(3, COLS, CHANS).astype(bf16)

    for g in range(GROUPS):
        cs = slice(128 * g, 128 * g + 128)
        edge[...] = value[:, cs]
        for c in range(3):
            at = pl.ds(pl.multiple_of(step * 8, 8), 8)
            west[c, at, cs] = edge[pl.ds(c, 8, stride=COLS), :].astype(bf16)
            east[c, at, cs] = edge[pl.ds(COLS - 3 + c, 8, stride=COLS), :].astype(bf16)


def fold_kernel(win, ain, bin_, wout, aout, bout, win_out, wout_out):
    win_out[...] = (win[...].astype(f32) + adapter_scale * dot(ain[...], bin_[...])).astype(bf16)
    wout_out[...] = (wout[...].astype(f32) + adapter_scale * dot(aout[...], bout[...])).astype(bf16)


def first_kernel(inner, flags, x, cv, w, e, taps, gain, shift, win, wout, ain, aout, scale, *refs):
    refs = refs[5 if inner else 0 :]
    nrm, hid, slope, mid_in, mid_out, y = refs[:6]
    edges, (he, line, edge) = refs[6:-3], refs[-3:]
    step = pl.program_id(0)
    tile = step + 1 if inner else 3 * step

    @pl.when(step == 0)
    def _():
        hold_strips(he, w, e, flags)

    norm_rows(cv, he, taps, line, tile, gain, shift, nrm)
    nb = nrm[...]
    mid_in[...] = dot(nb, ain[...]).astype(bf16)
    out = jnp.zeros((TILE, CHANS), f32)
    mid = jnp.zeros((TILE, RANK), f32)
    for c in range(0, HIDDEN, CHUNK):
        cs = slice(c, c + CHUNK)
        value, sl = gelu_parts(dot(nb, win[:, cs]))
        h = value.astype(bf16)
        hid[:, cs] = h
        slope[:, cs] = sl.astype(bf16)
        out = out + dot(h, wout[cs, :])
        mid = mid + dot(h, aout[cs, :])
    mid_out[...] = mid.astype(bf16)
    result = x[...].reshape(TILE, CHANS).astype(f32) + scale[...] * out
    y[...] = result.reshape(TROWS, COLS, CHANS).astype(bf16)
    put_edges(edge, result, edges, step, inner)


def second_kernel(
    inner, flags, x, cv, w, e, taps, gain, shift, win, wout, ain, bin_, aout, bout, scale, cot, *refs
):
    if inner:
        before, refs = refs[1], refs[2:]
    out_ref, grads, gc = refs[:3]
    edges, (he, line, edge, nrm, xh, rs) = refs[3:-6], refs[-6:]
    step = pl.program_id(0)
    tile = step + 1 if inner else 3 * step

    @pl.when(step == 0)
    def _():
        hold_strips(he, w, e, flags)
        grads[...] = before[...] if inner else jnp.zeros_like(grads)

    norm_rows(cv, he, taps, line, tile, gain, shift, nrm, xh, rs)
    nb = nrm[...]
    go = (cot[...].reshape(TILE, CHANS).astype(f32) * scale[...]).astype(bf16)
    mid_in = dot(nb, ain[...]).astype(bf16)
    gm_out = (adapter_scale * dot_t(go, bout[...])).astype(bf16)
    out = jnp.zeros((TILE, CHANS), f32)
    gn = jnp.zeros((TILE, CHANS), f32)
    mid = jnp.zeros((TILE, RANK), f32)
    gm_in = jnp.zeros((TILE, RANK), f32)
    for c in range(0, HIDDEN, CHUNK):
        cs = slice(c, c + CHUNK)
        value, sl = gelu_parts(dot(nb, win[:, cs]))
        h = value.astype(bf16)
        gpre = (dot_t(go, wout[cs, :]) * sl).astype(bf16)
        out = out + dot(h, wout[cs, :])
        mid = mid + dot(h, aout[cs, :])
        gn = gn + dot_t(gpre, win[:, cs])
        gm_in = gm_in + dot_t(gpre, bin_[:, cs])
        grads[:, 512 + c : 512 + c + CHUNK] += t_dot(mid_in, gpre)
        grads[:, 2560 + c : 2560 + c + CHUNK] += t_dot(gm_out, h)
    gm_in = (adapter_scale * gm_in).astype(bf16)
    grads[:, 0:512] += t_dot(gm_in, nb)
    grads[:, 4608:5120] += t_dot(mid.astype(bf16), go)
    result = x[...].reshape(TILE, CHANS).astype(f32) + scale[...] * out
    out_ref[...] = result.reshape(TROWS, COLS, CHANS).astype(bf16)
    u = gn * gain[...]
    standard = xh[...]
    m1 = jnp.mean(u, -1, keepdims=True)
    m2 = jnp.mean(u * standard, -1, keepdims=True)
    inverse = jnp.concatenate([rs[...]] * GROUPS, axis=1)
    result = inverse * (u - m1 - standard * m2)
    gc[...] = result.reshape(TROWS, COLS, CHANS).astype(bf16)
    put_edges(edge, result, edges, step, inner)


def third_kernel(
    flags, cot, cv, w, e, taps, scale, wout, bin_, bout, nrm, hid, slope, mid_in, mid_out,
    grads, he, line, gos,
):
    step = pl.program_id(0)

    @pl.when(step == 0)
    def _():
        hold_strips(he, w, e, flags)
        grads[...] = jnp.zeros_like(grads)

    def rows(i, c):
        g = cot[i].astype(f32) + whole_row(cv, he, taps, True, line, step, i)
        gos[row_of(i), :] = (g * scale[...]).astype(bf16)
        return c

    lax.fori_loop(0, TROWS, rows, 0)
    nb = nrm[...]
    go = gos[...]
    mi = mid_in[...]
    gm_out = (adapter_scale * dot_t(go, bout[...])).astype(bf16)
    gm_in = jnp.zeros((TILE, RANK), f32)
    for c in range(0, HIDDEN, CHUNK):
        cs = slice(c, c + CHUNK)
        gpre = (dot_t(go, wout[cs, :]) * slope[:, cs].astype(f32)).astype(bf16)
        gm_in = gm_in + dot_t(gpre, bin_[:, cs])
        grads[:, 512 + c : 512 + c + CHUNK] += t_dot(mi, gpre)
        grads[:, 2560 + c : 2560 + c + CHUNK] += t_dot(gm_out, hid[:, cs])
    gm_in = (adapter_scale * gm_in).astype(bf16)
    grads[:, 0:512] += t_dot(gm_in, nb)
    grads[:, 4608:5120] += t_dot(mid_out[...], go)


PARAMS = dict(compiler_params=pltpu.CompilerParams(vmem_limit_bytes=60 * 2**20))
SMEM = pl.BlockSpec(memory_space=pltpu.SMEM)
ANY = pl.BlockSpec(memory_space=pl.ANY)
HE = pltpu.VMEM((40 * 48, 128), f32)
LINE = pltpu.VMEM((HALF * 8, 128), f32)
EDGE = pltpu.VMEM((TILE, 128), f32)


def fixed(*shape):
    return pl.BlockSpec(shape, lambda t: (0,) * len(shape))


def layer(l, *shape):
    return pl.BlockSpec((None,) + shape, lambda t: (l,) + (0,) * len(shape))


def tiled(place, *shape):
    return pl.BlockSpec(shape, lambda t: (place(t),) + (0,) * (len(shape) - 1))


def call(kernel, name, grid, ins, outs, scratch, aliases={}):
    return pl.pallas_call(
        kernel,
        grid=(grid,),
        out_shape=[jax.ShapeDtypeStruct(shape, dtype) for shape, dtype, _ in outs],
        in_specs=[spec for _, spec in ins],
        out_specs=[spec for _, _, spec in outs],
        scratch_shapes=scratch,
        input_output_aliases=aliases,
        name=name,
        **PARAMS,
    )(*[array for array, _ in ins])


def conv(arrays, sources, n, s, taps, bias, l, flip, flags):
    return call(
        functools.partial(conv_kernel, sources, flip),
        "conv",
        4,
        [(flags, SMEM)]
        + [(a, fixed(*a.shape)) for a in arrays]
        + [(n, fixed(3, COLS, CHANS)), (s, fixed(3, COLS, CHANS))]
        + [(taps, layer(l, 49, 8, 128)), (bias, layer(l, 8, 128))],
        [((PIXELS * 4, 128), f32, tiled(lambda t: t, TILE * 4, 128))],
        [pltpu.VMEM((40 * SPAN * 8, 128), f32)],
    )[0]


def swap(v, axis):
    n = lax.axis_size(axis)
    after = [(i, (i + 1) % n) for i in range(n)]
    before = [(j, i) for i, j in after]
    return lax.ppermute(v[1], axis, after), lax.ppermute(v[0], axis, before)


def strips(outer, inner, north, south):
    sent = []
    for side, cut in ((0, slice(0, 3)), (1, slice(COLS - 3, COLS))):
        corners = [
            jnp.pad(v[:, cut].transpose(1, 0, 2), ((0, 0), (0, 5), (0, 0))) for v in (north, south)
        ]
        sent.append(jnp.concatenate([outer[side], inner[side], *corners], axis=1))
    return swap(sent, "col")


def total(first, second):
    core = lax.axis_index("col") % 2
    mine = jnp.where(core == 0, first, second)
    other = jnp.where(core == 0, second, first).astype(bf16)
    pair = [(i, i ^ 1) for i in range(16)]
    part = (mine + lax.ppermute(other, "col", pair).astype(f32)).astype(bf16)
    for even, odd in ((32, 4), (64, 8), (4, 1), (8, 16), (1, 32), (16, 64)):
        pairs = [(i, i ^ (odd if i & 2 else even)) for i in range(128)]
        other = lax.ppermute(part, ("row", "col", "rep"), pairs)
        part = (part.astype(f32) + other.astype(f32)).astype(bf16)
    back = lax.ppermute(part, "col", pair)
    return jnp.stack([jnp.where(core == 0, part, back), jnp.where(core == 0, back, part)]).astype(f32)


def normalize(stacked):
    mean = jnp.mean(stacked * stacked, axis=(1, 2), keepdims=True)
    return stacked * lax.rsqrt(mean + step_eps)


def body(
    features,
    cotangent,
    depthwise_filters,
    depthwise_bias_vector,
    layernorm_gain,
    layernorm_shift,
    inner_frozen_weight,
    outer_frozen_weight,
    inner_down_factor,
    inner_up_factor,
    outer_down_factor,
    outer_up_factor,
    branch_channel_scale,
):
    x0 = features.reshape(ROWS, COLS, CHANS)
    cot = cotangent.reshape(ROWS, COLS, CHANS)
    ain, bin_, aout, bout = inner_down_factor, inner_up_factor, outer_down_factor, outer_up_factor
    taps = depthwise_filters.reshape(2, 49, GROUPS, 128)
    taps = jnp.concatenate([taps, taps], axis=2)
    bias = depthwise_bias_vector.reshape(2, GROUPS, 128)
    bias = jnp.concatenate([bias, bias], axis=1)
    gain, shift, scale = (
        v.reshape(2, 1, CHANS) for v in (layernorm_gain, layernorm_shift, branch_channel_scale)
    )
    row, col = lax.axis_index("row"), lax.axis_index("col")
    flags = jnp.stack(
        [row > 0, row < lax.axis_size("row") - 1, col > 0, col < lax.axis_size("col") - 1]
    ).astype(f32)

    def by_block(*shape):
        return pl.BlockSpec((None,) + shape, lambda t: (t, 0, 0))

    north, south = swap((x0[:3], x0[-3:]), "row")
    win, wout = call(
        fold_kernel,
        "fold",
        2,
        [
            (inner_frozen_weight, by_block(CHANS, HIDDEN)),
            (ain, by_block(CHANS, RANK)),
            (bin_, by_block(RANK, HIDDEN)),
            (outer_frozen_weight, by_block(HIDDEN, CHANS)),
            (aout, by_block(HIDDEN, RANK)),
            (bout, by_block(RANK, CHANS)),
        ],
        [
            ((2, CHANS, HIDDEN), bf16, by_block(CHANS, HIDDEN)),
            ((2, HIDDEN, CHANS), bf16, by_block(HIDDEN, CHANS)),
        ],
        [],
    )
    ends = [x0[:, :3].transpose(1, 0, 2), x0[:, -3:].transpose(1, 0, 2)]
    west, east = strips(
        [jnp.concatenate([v[:, :8], v[:, 24:]], axis=1) for v in ends],
        [v[:, 8:24] for v in ends],
        north,
        south,
    )
    cv = conv([x0], [[(0, 0, 32)]], north, south, taps, bias, 0, False, flags)

    pixels = tiled
    strip_spec = fixed(3, STRIP, CHANS)

    def common(l, place, x, x_place):
        return [
            (flags, SMEM),
            (x, tiled(x_place, TROWS, COLS, CHANS)),
            (cv, tiled(place, TILE * 4, 128)),
            (west, strip_spec),
            (east, strip_spec),
            (taps, layer(l, 49, 8, 128)),
            (gain, layer(l, 1, CHANS)),
            (shift, layer(l, 1, CHANS)),
            (win, layer(l, CHANS, HIDDEN)),
            (wout, layer(l, HIDDEN, CHANS)),
            (ain, layer(l, CHANS, RANK)),
        ]

    def outer_place(t):
        return 3 * t

    def inner_place(t):
        return t + 1

    def same(t):
        return t

    row_edges = [((3, COLS, CHANS), bf16, fixed(3, COLS, CHANS))] * 2
    col_edges = [((3, 16, CHANS), bf16, fixed(3, 16, CHANS))] * 2
    half = ((16, COLS, CHANS), bf16, tiled(same, TROWS, COLS, CHANS))

    def kept(place):
        return [
            ((PIXELS, width), bf16, tiled(place, TILE, width))
            for width in (CHANS, HIDDEN, HIDDEN, RANK, RANK)
        ]

    last = [(aout, layer(0, HIDDEN, RANK)), (scale, layer(0, 1, CHANS))]
    *saved, outer, top, bottom, west_a, east_a = call(
        functools.partial(first_kernel, False),
        "first_outer",
        2,
        common(0, outer_place, x0, outer_place) + last,
        kept(outer_place) + [half] + row_edges + col_edges,
        [HE, LINE, EDGE],
    )
    north, south = swap((top, bottom), "row")
    ins = common(0, inner_place, x0, inner_place) + last
    *saved, inner, west_b, east_b = call(
        functools.partial(first_kernel, True),
        "first_inner",
        2,
        ins + [(v, ANY) for v in saved],
        kept(inner_place) + [half] + col_edges,
        [HE, LINE, EDGE],
        {len(ins) + i: i for i in range(5)},
    )
    split = [[(0, 0, 8), (8, 24, 8)], [(0, 8, 16)]]
    west, east = strips([west_a, east_a], [west_b, east_b], north, south)
    cv = conv([outer, inner], split, north, south, taps, bias, 1, False, flags)

    def second(place):
        return [
            (bin_, layer(1, RANK, HIDDEN)),
            (aout, layer(1, HIDDEN, RANK)),
            (bout, layer(1, RANK, CHANS)),
            (scale, layer(1, 1, CHANS)),
            (cot, tiled(place, TROWS, COLS, CHANS)),
        ]

    def results(place):
        return [
            ((ROWS, COLS, CHANS), bf16, tiled(place, TROWS, COLS, CHANS)),
            ((RANK, GRADS), f32, fixed(RANK, GRADS)),
            half,
        ]

    work = [
        HE,
        LINE,
        EDGE,
        pltpu.VMEM((TILE, CHANS), bf16),
        pltpu.VMEM((TILE, CHANS), f32),
        pltpu.VMEM((TILE, 128), f32),
    ]
    out, grads1, outer_g, top, bottom, west_a, east_a = call(
        functools.partial(second_kernel, False),
        "second_outer",
        2,
        common(1, outer_place, outer, same) + second(outer_place),
        results(outer_place) + row_edges + col_edges,
        work,
    )
    north, south = swap((top, bottom), "row")
    ins = common(1, inner_place, inner, same) + second(inner_place)
    out, grads1, inner_g, west_b, east_b = call(
        functools.partial(second_kernel, True),
        "second_inner",
        2,
        ins + [(out, ANY), (grads1, fixed(RANK, GRADS))],
        results(inner_place) + col_edges,
        work,
        {len(ins): 0},
    )
    west, east = strips([west_a, east_a], [west_b, east_b], north, south)
    cv = conv([outer_g, inner_g], split, north, south, taps, bias, 1, True, flags)
    (grads0,) = call(
        third_kernel,
        "third",
        4,
        [
            (flags, SMEM),
            (cot, tiled(same, TROWS, COLS, CHANS)),
            (cv, tiled(same, TILE * 4, 128)),
            (west, strip_spec),
            (east, strip_spec),
            (taps, layer(1, 49, 8, 128)),
            (scale, layer(0, 1, CHANS)),
            (wout, layer(0, HIDDEN, CHANS)),
            (bin_, layer(0, RANK, HIDDEN)),
            (bout, layer(0, RANK, CHANS)),
        ]
        + [(v, tiled(same, TILE, v.shape[1])) for v in saved],
        [((RANK, GRADS), f32, fixed(RANK, GRADS))],
        [HE, LINE, pltpu.VMEM((TILE, CHANS), bf16)],
    )
    sums = total(grads0, grads1)
    return (
        out[None],
        normalize(sums[:, :, 0:512].transpose(0, 2, 1)),
        normalize(adapter_scale * sums[:, :, 512:2560]),
        normalize(sums[:, :, 2560:4608].transpose(0, 2, 1)),
        normalize(adapter_scale * sums[:, :, 4608:5120]),
    )


def solution(mesh):
    tile = P("rep", "row", "col", None)
    return jax.shard_map(
        body,
        mesh=mesh,
        in_specs=(tile, tile) + (P(),) * 11,
        out_specs=(tile, P(), P(), P(), P()),
        check_vma=False,
    )
```

```python
import functools

import jax
import jax.numpy as jnp
from jax import lax
from jax.experimental import pallas as pl
from jax.experimental.pallas import tpu as pltpu
from jax.sharding import PartitionSpec as P

BLOCK_COUNT = 2
ROWS, COLS, CHANS, HIDDEN, RANK = 32, 32, 512, 2048, 16
PIXELS = ROWS * COLS
GROUPS = CHANS // 128
HALF = COLS // 2
SPAN = 32
OFFSET = 5
TROWS = 8
TILE = TROWS * COLS
CHUNK = 2048
STRIP = 48
GRADS = 2 * (CHANS + HIDDEN)

adapter_scale = 2.0
norm_eps = 1e-06
step_eps = 1e-06
gelu_coef = 0.7978845608
f32, bf16 = jnp.float32, jnp.bfloat16


def dot(a, b):
    return jnp.dot(a, b, preferred_element_type=f32)


def dot_t(a, b):
    return lax.dot_general(a, b, (((1,), (1,)), ((), ())), preferred_element_type=f32)


def t_dot(a, b):
    return lax.dot_general(a, b, (((0,), (0,)), ((), ())), preferred_element_type=f32)


CENTRE = [(k, g, 0, 8 * k + 8) for k in (0, 1, 2) for g in range(GROUPS)] + [
    (k, g, 1, 8 * k - 8) for k in (1, 2, 3) for g in range(GROUPS)
]


def spread(xs, row, values):
    for k, g, half, at in CENTRE:
        start = (row * SPAN + at) * 8 + half * GROUPS + g
        xs[pl.ds(start, 8, stride=8), :] = values[8 * k : 8 * k + 8, 128 * g : 128 * g + 128]


def conv_kernel(sources, flip, flags, *refs):
    xrefs, (n, s, taps, bias, cv, xs) = refs[: len(sources)], refs[len(sources) :]
    step = pl.program_id(0)

    @pl.when(step == 0)
    def _():
        zero = jnp.zeros((8, 128), f32)
        for ref, pieces in zip(xrefs, sources):
            for at, row, count in pieces:

                def centre(i, c, ref=ref, at=at, row=row):
                    spread(xs, row + 3 + i, ref[at + i].astype(f32))
                    return c

                lax.fori_loop(0, count, centre, 0)
        for i in range(3):
            spread(xs, i, n[i].astype(f32) * flags[0])
            spread(xs, ROWS + 3 + i, s[i].astype(f32) * flags[1])
        left = lax.broadcasted_iota(jnp.int32, (8, 128), 0) < GROUPS

        def edge(r, c):
            for k in (5, 6, 7):
                at = pl.ds(pl.multiple_of((r * SPAN + k) * 8, 8), 8)
                xs[at, :] = jnp.where(left, zero, xs[at, :])
            for k in (24, 25, 26):
                at = pl.ds(pl.multiple_of((r * SPAN + k) * 8, 8), 8)
                xs[at, :] = jnp.where(left, xs[at, :], zero)
            return c

        lax.fori_loop(0, ROWS + 6, edge, 0)

    def row(i, c):
        first = jnp.zeros((8, 128), f32) if flip else bias[...]
        totals = [first] * HALF
        for a in range(7):
            base = pl.multiple_of((step * TROWS + i + a) * (SPAN * 8), SPAN * 8)
            line = [xs[pl.ds(base + (OFFSET + k) * 8, 8), :] for k in range(HALF + 6)]
            for b in range(7):
                tap = taps[48 - (a * 7 + b) if flip else a * 7 + b]
                for k in range(HALF):
                    totals[k] = totals[k] + line[k + b] * tap
        base = pl.multiple_of(i * (HALF * 8), HALF * 8)
        for k in range(HALF):
            cv[pl.ds(base + k * 8, 8), :] = totals[k]
        return c

    lax.fori_loop(0, TROWS, row, 0)


def hold_strips(he, w, e, flags):
    he[...] = jnp.zeros_like(he)
    for side, ref in ((0, w), (1, e)):
        for c in range(3):
            for block, row in ((4, 0), (5, 35), (0, 3), (2, 11), (3, 19), (1, 27)):
                v = ref[c, 8 * block : 8 * block + 8, :].astype(f32) * flags[2 + side]
                if block >= 4:
                    v = v * flags[block - 4]
                if block == 5:
                    v = v[0:3]
                for g in range(GROUPS):
                    start = (row * 6 + side * 3 + c) * 8 + side * GROUPS + g
                    he[pl.ds(start, v.shape[0], stride=48), :] = v[:, 128 * g : 128 * g + 128]


def whole_row(cv, he, taps, flip, line, tile, i):
    base = pl.multiple_of(i * (HALF * 8), HALF * 8)
    totals = [cv[pl.ds(base + k * 8, 8), :] for k in range(HALF)]
    for a in range(7):
        at = pl.multiple_of((tile * TROWS + i + a) * 48, 48)
        edge = [he[pl.ds(at + 8 * k, 8), :] for k in range(6)]
        pairs = [(k, h, h - k) for k in range(3) for h in range(k, 3)]
        pairs += [(k, 3 + h, 19 + h - k) for k in (13, 14, 15) for h in range(k - 12)]
        for k, h, b in pairs:
            totals[k] = totals[k] + edge[h] * taps[48 - (a * 7 + b) if flip else a * 7 + b]
    for k in range(HALF):
        line[k * 8 : k * 8 + 8, :] = totals[k]
    parts = []
    for k in range(4):
        start = (k % 2) * 64 + (k // 2) * GROUPS
        parts.append(
            jnp.concatenate([line[pl.ds(start + g, 8, stride=8), :] for g in range(GROUPS)], axis=1)
        )
    return jnp.concatenate(parts, axis=0)


def gelu_parts(v):
    square = v * v
    t = jnp.tanh(v * (gelu_coef + (gelu_coef * 0.044715) * square))
    h = 0.5 * t + 0.5
    value = v * h
    slope = h + value * (1.0 - t) * (gelu_coef + (3.0 * 0.044715 * gelu_coef) * square)
    return value, slope


def row_of(i):
    return pl.ds(pl.multiple_of(i * COLS, COLS), COLS)


def norm_rows(cv, he, taps, line, tile, gain, shift, nrm, xh=None, rs=None):
    def body(i, c):
        conv = whole_row(cv, he, taps, False, line, tile, i)
        centred = conv - jnp.mean(conv, -1, keepdims=True)
        inverse = lax.rsqrt(jnp.mean(centred * centred, -1, keepdims=True) + norm_eps)
        standard = centred * inverse
        nrm[row_of(i), :] = (standard * gain[...] + shift[...]).astype(bf16)
        if xh is not None:
            xh[row_of(i), :] = standard
            rs[row_of(i), :] = jnp.broadcast_to(inverse, (COLS, 128))
        return c

    lax.fori_loop(0, TROWS, body, 0, unroll=8)


def put_edges(edge, value, refs, step, inner):
    west, east = refs[-2:]
    if not inner:
        top, bottom = refs[:2]

        @pl.when(step == 0)
        def _():
            top[...] = value[: 3 * COLS].reshape(3, COLS, CHANS).astype(bf16)

        @pl.when(step == 1)
        def _():
            bottom[...] = value[5 * COLS :].reshape(3, COLS, CHANS).astype(bf16)

    for g in range(GROUPS):
        cs = slice(128 * g, 128 * g + 128)
        edge[...] = value[:, cs]
        for c in range(3):
            at = pl.ds(pl.multiple_of(step * 8, 8), 8)
            west[c, at, cs] = edge[pl.ds(c, 8, stride=COLS), :].astype(bf16)
            east[c, at, cs] = edge[pl.ds(COLS - 3 + c, 8, stride=COLS), :].astype(bf16)


def fold_kernel(win, ain, bin_, wout, aout, bout, win_out, wout_out):
    win_out[...] = (win[...].astype(f32) + adapter_scale * dot(ain[...], bin_[...])).astype(bf16)
    wout_out[...] = (wout[...].astype(f32) + adapter_scale * dot(aout[...], bout[...])).astype(bf16)


def first_kernel(inner, flags, x, cv, w, e, taps, gain, shift, win, wout, ain, aout, scale, *refs):
    refs = refs[5 if inner else 0 :]
    nrm, hid, slope, mid_in, mid_out, y = refs[:6]
    edges, (he, line, edge) = refs[6:-3], refs[-3:]
    step = pl.program_id(0)
    tile = step + 1 if inner else 3 * step

    @pl.when(step == 0)
    def _():
        hold_strips(he, w, e, flags)

    norm_rows(cv, he, taps, line, tile, gain, shift, nrm)
    nb = nrm[...]
    mid_in[...] = dot(nb, ain[...]).astype(bf16)
    out = jnp.zeros((TILE, CHANS), f32)
    mid = jnp.zeros((TILE, RANK), f32)
    for c in range(0, HIDDEN, CHUNK):
        cs = slice(c, c + CHUNK)
        value, sl = gelu_parts(dot(nb, win[:, cs]))
        h = value.astype(bf16)
        hid[:, cs] = h
        slope[:, cs] = sl.astype(bf16)
        out = out + dot(h, wout[cs, :])
        mid = mid + dot(h, aout[cs, :])
    mid_out[...] = mid.astype(bf16)
    result = x[...].reshape(TILE, CHANS).astype(f32) + scale[...] * out
    y[...] = result.reshape(TROWS, COLS, CHANS).astype(bf16)
    put_edges(edge, result, edges, step, inner)


def second_kernel(
    inner, flags, x, cv, w, e, taps, gain, shift, win, wout, ain, bin_, aout, bout, scale, cot, *refs
):
    if inner:
        before, refs = refs[1], refs[2:]
    out_ref, grads, gc = refs[:3]
    edges, (he, line, edge, nrm, xh, rs) = refs[3:-6], refs[-6:]
    step = pl.program_id(0)
    tile = step + 1 if inner else 3 * step

    @pl.when(step == 0)
    def _():
        hold_strips(he, w, e, flags)
        grads[...] = before[...] if inner else jnp.zeros_like(grads)

    norm_rows(cv, he, taps, line, tile, gain, shift, nrm, xh, rs)
    nb = nrm[...]
    go = (cot[...].reshape(TILE, CHANS).astype(f32) * scale[...]).astype(bf16)
    mid_in = dot(nb, ain[...]).astype(bf16)
    gm_out = (adapter_scale * dot_t(go, bout[...])).astype(bf16)
    out = jnp.zeros((TILE, CHANS), f32)
    gn = jnp.zeros((TILE, CHANS), f32)
    mid = jnp.zeros((TILE, RANK), f32)
    gm_in = jnp.zeros((TILE, RANK), f32)
    for c in range(0, HIDDEN, CHUNK):
        cs = slice(c, c + CHUNK)
        value, sl = gelu_parts(dot(nb, win[:, cs]))
        h = value.astype(bf16)
        gpre = (dot_t(go, wout[cs, :]) * sl).astype(bf16)
        out = out + dot(h, wout[cs, :])
        mid = mid + dot(h, aout[cs, :])
        gn = gn + dot_t(gpre, win[:, cs])
        gm_in = gm_in + dot_t(gpre, bin_[:, cs])
        grads[:, 512 + c : 512 + c + CHUNK] += t_dot(mid_in, gpre)
        grads[:, 2560 + c : 2560 + c + CHUNK] += t_dot(gm_out, h)
    gm_in = (adapter_scale * gm_in).astype(bf16)
    grads[:, 0:512] += t_dot(gm_in, nb)
    grads[:, 4608:5120] += t_dot(mid.astype(bf16), go)
    result = x[...].reshape(TILE, CHANS).astype(f32) + scale[...] * out
    out_ref[...] = result.reshape(TROWS, COLS, CHANS).astype(bf16)
    u = gn * gain[...]
    standard = xh[...]
    m1 = jnp.mean(u, -1, keepdims=True)
    m2 = jnp.mean(u * standard, -1, keepdims=True)
    inverse = jnp.concatenate([rs[...]] * GROUPS, axis=1)
    result = inverse * (u - m1 - standard * m2)
    gc[...] = result.reshape(TROWS, COLS, CHANS).astype(bf16)
    put_edges(edge, result, edges, step, inner)


def third_kernel(
    flags, cot, cv, w, e, taps, scale, wout, bin_, bout, nrm, hid, slope, mid_in, mid_out,
    grads, he, line, gos,
):
    step = pl.program_id(0)

    @pl.when(step == 0)
    def _():
        hold_strips(he, w, e, flags)
        grads[...] = jnp.zeros_like(grads)

    def rows(i, c):
        g = cot[i].astype(f32) + whole_row(cv, he, taps, True, line, step, i)
        gos[row_of(i), :] = (g * scale[...]).astype(bf16)
        return c

    lax.fori_loop(0, TROWS, rows, 0, unroll=8)
    nb = nrm[...]
    go = gos[...]
    mi = mid_in[...]
    gm_out = (adapter_scale * dot_t(go, bout[...])).astype(bf16)
    gm_in = jnp.zeros((TILE, RANK), f32)
    for c in range(0, HIDDEN, CHUNK):
        cs = slice(c, c + CHUNK)
        gpre = (dot_t(go, wout[cs, :]) * slope[:, cs].astype(f32)).astype(bf16)
        gm_in = gm_in + dot_t(gpre, bin_[:, cs])
        grads[:, 512 + c : 512 + c + CHUNK] += t_dot(mi, gpre)
        grads[:, 2560 + c : 2560 + c + CHUNK] += t_dot(gm_out, hid[:, cs])
    gm_in = (adapter_scale * gm_in).astype(bf16)
    grads[:, 0:512] += t_dot(gm_in, nb)
    grads[:, 4608:5120] += t_dot(mid_out[...], go)


PARAMS = dict(compiler_params=pltpu.CompilerParams(vmem_limit_bytes=26 * 2**20))
SMEM = pl.BlockSpec(memory_space=pltpu.SMEM)
ANY = pl.BlockSpec(memory_space=pl.ANY)
HE = pltpu.VMEM((40 * 48, 128), f32)
LINE = pltpu.VMEM((HALF * 8, 128), f32)
EDGE = pltpu.VMEM((TILE, 128), f32)


def fixed(*shape):
    return pl.BlockSpec(shape, lambda t: (0,) * len(shape), pipeline_mode=pl.Buffered(1))


def layer(l, *shape):
    return pl.BlockSpec((None,) + shape, lambda t: (l,) + (0,) * len(shape), pipeline_mode=pl.Buffered(1))


def tiled(place, *shape):
    return pl.BlockSpec(shape, lambda t: (place(t),) + (0,) * (len(shape) - 1))


def call(kernel, name, grid, ins, outs, scratch, aliases={}):
    return pl.pallas_call(
        kernel,
        grid=(grid,),
        out_shape=[jax.ShapeDtypeStruct(shape, dtype) for shape, dtype, _ in outs],
        in_specs=[spec for _, spec in ins],
        out_specs=[spec for _, _, spec in outs],
        scratch_shapes=scratch,
        input_output_aliases=aliases,
        name=name,
        **PARAMS,
    )(*[array for array, _ in ins])


def conv(arrays, sources, n, s, taps, bias, l, flip, flags):
    return call(
        functools.partial(conv_kernel, sources, flip),
        "conv",
        4,
        [(flags, SMEM)]
        + [(a, fixed(*a.shape)) for a in arrays]
        + [(n, fixed(3, COLS, CHANS)), (s, fixed(3, COLS, CHANS))]
        + [(taps, layer(l, 49, 8, 128)), (bias, layer(l, 8, 128))],
        [((PIXELS * 4, 128), f32, tiled(lambda t: t, TILE * 4, 128))],
        [pltpu.VMEM((40 * SPAN * 8, 128), f32)],
    )[0]


def swap(v, axis):
    n = lax.axis_size(axis)
    after = [(i, (i + 1) % n) for i in range(n)]
    before = [(j, i) for i, j in after]
    return lax.ppermute(v[1], axis, after), lax.ppermute(v[0], axis, before)


def strips(outer, inner, north, south):
    sent = []
    for side, cut in ((0, slice(0, 3)), (1, slice(COLS - 3, COLS))):
        corners = [
            jnp.pad(v[:, cut].transpose(1, 0, 2), ((0, 0), (0, 5), (0, 0))) for v in (north, south)
        ]
        sent.append(jnp.concatenate([outer[side], inner[side], *corners], axis=1))
    return swap(sent, "col")


def total(first, second):
    core = lax.axis_index("col") % 2
    mine = jnp.where(core == 0, first, second)
    other = jnp.where(core == 0, second, first).astype(bf16)
    pair = [(i, i ^ 1) for i in range(16)]
    part = (mine + lax.ppermute(other, "col", pair).astype(f32)).astype(bf16)
    for even, odd in ((32, 4), (64, 8), (4, 1), (8, 16), (1, 32), (16, 64)):
        pairs = [(i, i ^ (odd if i & 2 else even)) for i in range(128)]
        other = lax.ppermute(part, ("row", "col", "rep"), pairs)
        part = (part.astype(f32) + other.astype(f32)).astype(bf16)
    back = lax.ppermute(part, "col", pair)
    return jnp.stack([jnp.where(core == 0, part, back), jnp.where(core == 0, back, part)]).astype(f32)


def normalize(stacked):
    mean = jnp.mean(stacked * stacked, axis=(1, 2), keepdims=True)
    return stacked * lax.rsqrt(mean + step_eps)


def body(
    features,
    cotangent,
    depthwise_filters,
    depthwise_bias_vector,
    layernorm_gain,
    layernorm_shift,
    inner_frozen_weight,
    outer_frozen_weight,
    inner_down_factor,
    inner_up_factor,
    outer_down_factor,
    outer_up_factor,
    branch_channel_scale,
):
    x0 = features.reshape(ROWS, COLS, CHANS)
    cot = cotangent.reshape(ROWS, COLS, CHANS)
    ain, bin_, aout, bout = inner_down_factor, inner_up_factor, outer_down_factor, outer_up_factor
    taps = depthwise_filters.reshape(2, 49, GROUPS, 128)
    taps = jnp.concatenate([taps, taps], axis=2)
    bias = depthwise_bias_vector.reshape(2, GROUPS, 128)
    bias = jnp.concatenate([bias, bias], axis=1)
    gain, shift, scale = (
        v.reshape(2, 1, CHANS) for v in (layernorm_gain, layernorm_shift, branch_channel_scale)
    )
    row, col = lax.axis_index("row"), lax.axis_index("col")
    flags = jnp.stack(
        [row > 0, row < lax.axis_size("row") - 1, col > 0, col < lax.axis_size("col") - 1]
    ).astype(f32)

    def by_block(*shape):
        return pl.BlockSpec((None,) + shape, lambda t: (t, 0, 0))

    north, south = swap((x0[:3], x0[-3:]), "row")
    win, wout = call(
        fold_kernel,
        "fold",
        2,
        [
            (inner_frozen_weight, by_block(CHANS, HIDDEN)),
            (ain, by_block(CHANS, RANK)),
            (bin_, by_block(RANK, HIDDEN)),
            (outer_frozen_weight, by_block(HIDDEN, CHANS)),
            (aout, by_block(HIDDEN, RANK)),
            (bout, by_block(RANK, CHANS)),
        ],
        [
            ((2, CHANS, HIDDEN), bf16, by_block(CHANS, HIDDEN)),
            ((2, HIDDEN, CHANS), bf16, by_block(HIDDEN, CHANS)),
        ],
        [],
    )
    ends = [x0[:, :3].transpose(1, 0, 2), x0[:, -3:].transpose(1, 0, 2)]
    west, east = strips(
        [jnp.concatenate([v[:, :8], v[:, 24:]], axis=1) for v in ends],
        [v[:, 8:24] for v in ends],
        north,
        south,
    )
    cv = conv([x0], [[(0, 0, 32)]], north, south, taps, bias, 0, False, flags)

    pixels = tiled
    strip_spec = fixed(3, STRIP, CHANS)

    def common(l, place, x, x_place):
        return [
            (flags, SMEM),
            (x, tiled(x_place, TROWS, COLS, CHANS)),
            (cv, tiled(place, TILE * 4, 128)),
            (west, strip_spec),
            (east, strip_spec),
            (taps, layer(l, 49, 8, 128)),
            (gain, layer(l, 1, CHANS)),
            (shift, layer(l, 1, CHANS)),
            (win, layer(l, CHANS, HIDDEN)),
            (wout, layer(l, HIDDEN, CHANS)),
            (ain, layer(l, CHANS, RANK)),
        ]

    def outer_place(t):
        return 3 * t

    def inner_place(t):
        return t + 1

    def same(t):
        return t

    row_edges = [((3, COLS, CHANS), bf16, fixed(3, COLS, CHANS))] * 2
    col_edges = [((3, 16, CHANS), bf16, fixed(3, 16, CHANS))] * 2
    half = ((16, COLS, CHANS), bf16, tiled(same, TROWS, COLS, CHANS))

    def kept(place):
        return [
            ((PIXELS, width), bf16, tiled(place, TILE, width))
            for width in (CHANS, HIDDEN, HIDDEN, RANK, RANK)
        ]

    last = [(aout, layer(0, HIDDEN, RANK)), (scale, layer(0, 1, CHANS))]
    *saved, outer, top, bottom, west_a, east_a = call(
        functools.partial(first_kernel, False),
        "first_outer",
        2,
        common(0, outer_place, x0, outer_place) + last,
        kept(outer_place) + [half] + row_edges + col_edges,
        [HE, LINE, EDGE],
    )
    north, south = swap((top, bottom), "row")
    ins = common(0, inner_place, x0, inner_place) + last
    *saved, inner, west_b, east_b = call(
        functools.partial(first_kernel, True),
        "first_inner",
        2,
        ins + [(v, ANY) for v in saved],
        kept(inner_place) + [half] + col_edges,
        [HE, LINE, EDGE],
        {len(ins) + i: i for i in range(5)},
    )
    split = [[(0, 0, 8), (8, 24, 8)], [(0, 8, 16)]]
    west, east = strips([west_a, east_a], [west_b, east_b], north, south)
    cv = conv([outer, inner], split, north, south, taps, bias, 1, False, flags)

    def second(place):
        return [
            (bin_, layer(1, RANK, HIDDEN)),
            (aout, layer(1, HIDDEN, RANK)),
            (bout, layer(1, RANK, CHANS)),
            (scale, layer(1, 1, CHANS)),
            (cot, tiled(place, TROWS, COLS, CHANS)),
        ]

    def results(place):
        return [
            ((ROWS, COLS, CHANS), bf16, tiled(place, TROWS, COLS, CHANS)),
            ((RANK, GRADS), f32, fixed(RANK, GRADS)),
            half,
        ]

    work = [
        HE,
        LINE,
        EDGE,
        pltpu.VMEM((TILE, CHANS), bf16),
        pltpu.VMEM((TILE, CHANS), f32),
        pltpu.VMEM((TILE, 128), f32),
    ]
    out, grads1, outer_g, top, bottom, west_a, east_a = call(
        functools.partial(second_kernel, False),
        "second_outer",
        2,
        common(1, outer_place, outer, same) + second(outer_place),
        results(outer_place) + row_edges + col_edges,
        work,
    )
    north, south = swap((top, bottom), "row")
    ins = common(1, inner_place, inner, same) + second(inner_place)
    out, grads1, inner_g, west_b, east_b = call(
        functools.partial(second_kernel, True),
        "second_inner",
        2,
        ins + [(out, ANY), (grads1, fixed(RANK, GRADS))],
        results(inner_place) + col_edges,
        work,
        {len(ins): 0},
    )
    west, east = strips([west_a, east_a], [west_b, east_b], north, south)
    cv = conv([outer_g, inner_g], split, north, south, taps, bias, 1, True, flags)
    (grads0,) = call(
        third_kernel,
        "third",
        4,
        [
            (flags, SMEM),
            (cot, tiled(same, TROWS, COLS, CHANS)),
            (cv, tiled(same, TILE * 4, 128)),
            (west, strip_spec),
            (east, strip_spec),
            (taps, layer(1, 49, 8, 128)),
            (scale, layer(0, 1, CHANS)),
            (wout, layer(0, HIDDEN, CHANS)),
            (bin_, layer(0, RANK, HIDDEN)),
            (bout, layer(0, RANK, CHANS)),
        ]
        + [(v, tiled(same, TILE, v.shape[1])) for v in saved],
        [((RANK, GRADS), f32, fixed(RANK, GRADS))],
        [HE, LINE, pltpu.VMEM((TILE, CHANS), bf16)],
    )
    sums = total(grads0, grads1)
    return (
        out[None],
        normalize(sums[:, :, 0:512].transpose(0, 2, 1)),
        normalize(adapter_scale * sums[:, :, 512:2560]),
        normalize(sums[:, :, 2560:4608].transpose(0, 2, 1)),
        normalize(adapter_scale * sums[:, :, 4608:5120]),
    )


def solution(mesh):
    tile = P("rep", "row", "col", None)
    return jax.shard_map(
        body,
        mesh=mesh,
        in_specs=(tile, tile) + (P(),) * 11,
        out_specs=(tile, P(), P(), P(), P()),
        check_vma=False,
    )
```

```python
import functools

import jax
import jax.numpy as jnp
from jax import lax
from jax.experimental import pallas as pl
from jax.experimental.pallas import tpu as pltpu
from jax.sharding import PartitionSpec as P

BLOCK_COUNT = 2
ROWS, COLS, CHANS, HIDDEN, RANK = 32, 32, 512, 2048, 16
PIXELS = ROWS * COLS
GROUPS = CHANS // 128
HALF = COLS // 2
SPAN = 32
OFFSET = 5
WIDE = HALF + 6
TROWS = 8
TILE = TROWS * COLS
CHUNK = 2048
STRIP = 48
GRADS = 2 * (CHANS + HIDDEN)

adapter_scale = 2.0
norm_eps = 1e-06
step_eps = 1e-06
gelu_coef = 0.7978845608
f32, bf16 = jnp.float32, jnp.bfloat16


def dot(a, b):
    return jnp.dot(a, b, preferred_element_type=f32)


def dot_t(a, b):
    return lax.dot_general(a, b, (((1,), (1,)), ((), ())), preferred_element_type=f32)


def t_dot(a, b):
    return lax.dot_general(a, b, (((0,), (0,)), ((), ())), preferred_element_type=f32)


CENTRE = [(k, g, 0, 8 * k + 8) for k in (0, 1, 2) for g in range(GROUPS)] + [
    (k, g, 1, 8 * k - 8) for k in (1, 2, 3) for g in range(GROUPS)
]


def spread(xs, row, values):
    for k, g, half, at in CENTRE:
        start = (row * SPAN + at) * 8 + half * GROUPS + g
        xs[pl.ds(start, 8, stride=8), :] = values[8 * k : 8 * k + 8, 128 * g : 128 * g + 128]


def conv_kernel(sources, flip, flags, *refs):
    xrefs, (n, s, taps, cv, held, spans, lines) = refs[: len(sources)], refs[len(sources) :]
    step = pl.program_id(0)
    zero = jnp.zeros((8, 128), f32)
    left = lax.broadcasted_iota(jnp.int32, (8, 128), 0) < GROUPS

    def take(row):
        spread(spans, 0, held[row].astype(f32))
        base = pl.multiple_of(row * (WIDE * 8), WIDE * 8)
        for k in range(WIDE):
            reg = spans[(OFFSET + k) * 8 : (OFFSET + k) * 8 + 8, :]
            if k < 3:
                reg = jnp.where(left, zero, reg)
            if k >= HALF + 3:
                reg = jnp.where(left, reg, zero)
            lines[pl.ds(base + k * 8, 8), :] = reg

    @pl.when(step == 0)
    def _():
        for ref, pieces in zip(xrefs, sources):
            for at, row, count in pieces:
                held[row + 3 : row + 3 + count] = ref[at : at + count]
        held[0:3] = (n[...].astype(f32) * flags[0]).astype(bf16)
        held[ROWS + 3 : ROWS + 6] = (s[...].astype(f32) * flags[1]).astype(bf16)
        held[ROWS + 6 :] = jnp.zeros((2, COLS, CHANS), bf16)
        lax.fori_loop(0, 38, lambda r, c: (take(r), c)[1], 0)

    def row(i, c):
        at = step * TROWS + i
        totals = [zero] * HALF
        for a in range(7):
            base = pl.multiple_of((at + a) * (WIDE * 8), WIDE * 8)
            line = [lines[pl.ds(base + k * 8, 8), :] for k in range(WIDE)]
            for b in range(7):
                tap = taps[48 - (a * 7 + b) if flip else a * 7 + b]
                for k in range(HALF):
                    totals[k] = totals[k] + line[k + b] * tap
        base = pl.multiple_of(i * (HALF * 8), HALF * 8)
        for k in range(HALF):
            cv[pl.ds(base + k * 8, 8), :] = totals[k]
        return c

    lax.fori_loop(0, TROWS, row, 0)


def hold_strips(he, w, e, flags):
    he[...] = jnp.zeros_like(he)
    for side, ref in ((0, w), (1, e)):
        for c in range(3):
            for block, row in ((4, 0), (5, 35), (0, 3), (2, 11), (3, 19), (1, 27)):
                v = ref[c, 8 * block : 8 * block + 8, :].astype(f32) * flags[2 + side]
                if block >= 4:
                    v = v * flags[block - 4]
                if block == 5:
                    v = v[0:3]
                for g in range(GROUPS):
                    start = (row * 6 + side * 3 + c) * 8 + side * GROUPS + g
                    he[pl.ds(start, v.shape[0], stride=48), :] = v[:, 128 * g : 128 * g + 128]


def whole_row(cv, he, taps, flip, line, tile, i):
    base = pl.multiple_of(i * (HALF * 8), HALF * 8)
    totals = [cv[pl.ds(base + k * 8, 8), :] for k in range(HALF)]
    for a in range(7):
        at = pl.multiple_of((tile * TROWS + i + a) * 48, 48)
        edge = [he[pl.ds(at + 8 * k, 8), :] for k in range(6)]
        pairs = [(k, h, h - k) for k in range(3) for h in range(k, 3)]
        pairs += [(k, 3 + h, 19 + h - k) for k in (13, 14, 15) for h in range(k - 12)]
        for k, h, b in pairs:
            totals[k] = totals[k] + edge[h] * taps[48 - (a * 7 + b) if flip else a * 7 + b]
    for k in range(HALF):
        line[k * 8 : k * 8 + 8, :] = totals[k]
    parts = []
    for k in range(4):
        start = (k % 2) * 64 + (k // 2) * GROUPS
        parts.append(
            jnp.concatenate([line[pl.ds(start + g, 8, stride=8), :] for g in range(GROUPS)], axis=1)
        )
    return jnp.concatenate(parts, axis=0)


def gelu_parts(v):
    square = v * v
    t = jnp.tanh(v * (gelu_coef + (gelu_coef * 0.044715) * square))
    h = 0.5 * t + 0.5
    value = v * h
    slope = h + value * (1.0 - t) * (gelu_coef + (3.0 * 0.044715 * gelu_coef) * square)
    return value, slope


def row_of(i):
    return pl.ds(pl.multiple_of(i * COLS, COLS), COLS)


def norm_rows(cv, he, taps, line, tile, bias, gain, shift, nrm, xh=None, rs=None):
    def body(i, c):
        conv = whole_row(cv, he, taps, False, line, tile, i) + bias
        centred = conv - jnp.mean(conv, -1, keepdims=True)
        inverse = lax.rsqrt(jnp.mean(centred * centred, -1, keepdims=True) + norm_eps)
        standard = centred * inverse
        nrm[row_of(i), :] = (standard * gain + shift).astype(bf16)
        if xh is not None:
            xh[row_of(i), :] = standard
            rs[row_of(i), :] = jnp.broadcast_to(inverse, (COLS, 128))
        return c

    lax.fori_loop(0, TROWS, body, 0, unroll=8)


def put_edges(edge, value, refs, step, inner):
    west, east = refs[-2:]
    if not inner:
        top, bottom = refs[:2]

        @pl.when(step == 0)
        def _():
            top[...] = value[: 3 * COLS].reshape(3, COLS, CHANS).astype(bf16)

        @pl.when(step == 1)
        def _():
            bottom[...] = value[5 * COLS :].reshape(3, COLS, CHANS).astype(bf16)

    for g in range(GROUPS):
        cs = slice(128 * g, 128 * g + 128)
        edge[...] = value[:, cs]
        for c in range(3):
            at = pl.ds(pl.multiple_of(step * 8, 8), 8)
            west[c, at, cs] = edge[pl.ds(c, 8, stride=COLS), :].astype(bf16)
            east[c, at, cs] = edge[pl.ds(COLS - 3 + c, 8, stride=COLS), :].astype(bf16)


def edge_kernel(first, last, west, east, edge):
    for ref, out, at in ((first, west, 0), (last, east, 5)):
        for g in range(GROUPS):
            cs = slice(128 * g, 128 * g + 128)
            edge[...] = ref[:, :, cs].reshape(ROWS * 8, 128).astype(f32)
            for c in range(3):
                out[c, :, cs] = edge[pl.ds(at + c, ROWS, stride=8), :].astype(bf16)


def pack_kernel(split, *refs):
    pieces, (n, s, west, east) = refs[:-4], refs[-4:]
    for side, out in ((0, west), (1, east)):
        if split:
            out[:, 0:16] = pieces[2 * side][...]
            out[:, 16:32] = pieces[2 * side + 1][...]
        else:
            v = pieces[side]
            for block, row in enumerate((0, 24, 8, 16)):
                out[:, 8 * block : 8 * block + 8] = v[:, row : row + 8]
        for at, ref in ((32, n), (40, s)):
            cut = slice(COLS - 8, COLS) if side else slice(0, 8)
            v = [ref[r, cut, :].astype(f32) for r in range(3)]
            for c in range(3):
                k = c + 5 if side else c
                rows = [v[r][k : k + 1] for r in range(3)] + [jnp.zeros((5, CHANS), f32)]
                out[c, at : at + 8] = jnp.concatenate(rows, axis=0).astype(bf16)


def fold_kernel(win, ain, bin_, wout, aout, bout, filters, win_out, wout_out, taps):
    @pl.when((pl.program_id(0) == 0) & (pl.program_id(1) == 0))
    def _():
        for t in range(49):
            v = filters[t]
            for l in range(2):
                for g in range(8):
                    at = 128 * (g % GROUPS)
                    taps[l, t, g : g + 1, :] = v[l : l + 1, at : at + 128]

    win_out[...] = (win[...].astype(f32) + adapter_scale * t_dot(ain[...], bin_[...])).astype(bf16)
    wout_out[...] = (wout[...].astype(f32) + adapter_scale * t_dot(aout[...], bout[...])).astype(bf16)


def first_kernel(inner, flags, x, cv, w, e, taps, bias, gain, shift, scale, win, wout, ain, aout, *refs):
    refs = refs[5 if inner else 0 :]
    bias, gain, shift, scale = (v[0:1, :] for v in (bias, gain, shift, scale))
    nrm, hid, slope, mid_in, mid_out, y = refs[:6]
    edges, (he, line, edge) = refs[6:-3], refs[-3:]
    step = pl.program_id(0)
    tile = step + 1 if inner else 3 * step

    @pl.when(step == 0)
    def _():
        hold_strips(he, w, e, flags)

    norm_rows(cv, he, taps, line, tile, bias, gain, shift, nrm)
    nb = nrm[...]
    mid_in[...] = dot_t(nb, ain[...]).astype(bf16)
    out = jnp.zeros((TILE, CHANS), f32)
    mid = jnp.zeros((TILE, RANK), f32)
    for c in range(0, HIDDEN, CHUNK):
        cs = slice(c, c + CHUNK)
        value, sl = gelu_parts(dot(nb, win[:, cs]))
        h = value.astype(bf16)
        hid[:, cs] = h
        slope[:, cs] = sl.astype(bf16)
        out = out + dot(h, wout[cs, :])
        mid = mid + dot_t(h, aout[:, cs])
    mid_out[...] = mid.astype(bf16)
    result = x[...].reshape(TILE, CHANS).astype(f32) + scale * out
    y[...] = result.reshape(TROWS, COLS, CHANS).astype(bf16)
    put_edges(edge, result, edges, step, inner)


def second_kernel(
    inner, flags, x, cv, w, e, taps, bias, gain, shift, scale, win, wout, ain, aout, bin_, bout, cot, *refs
):
    bias, gain, shift, scale = (v[1:2, :] for v in (bias, gain, shift, scale))
    if inner:
        before, refs = refs[1], refs[2:]
    out_ref, grads, gc = refs[:3]
    edges, (he, line, edge, nrm, xh, rs) = refs[3:-6], refs[-6:]
    step = pl.program_id(0)
    tile = step + 1 if inner else 3 * step

    @pl.when(step == 0)
    def _():
        hold_strips(he, w, e, flags)
        grads[...] = before[...] if inner else jnp.zeros_like(grads)

    norm_rows(cv, he, taps, line, tile, bias, gain, shift, nrm, xh, rs)
    nb = nrm[...]
    go = (cot[...].reshape(TILE, CHANS).astype(f32) * scale).astype(bf16)
    mid_in = dot_t(nb, ain[...]).astype(bf16)
    gm_out = (adapter_scale * dot_t(go, bout[...])).astype(bf16)
    out = jnp.zeros((TILE, CHANS), f32)
    gn = jnp.zeros((TILE, CHANS), f32)
    mid = jnp.zeros((TILE, RANK), f32)
    gm_in = jnp.zeros((TILE, RANK), f32)
    for c in range(0, HIDDEN, CHUNK):
        cs = slice(c, c + CHUNK)
        value, sl = gelu_parts(dot(nb, win[:, cs]))
        h = value.astype(bf16)
        gpre = (dot_t(go, wout[cs, :]) * sl).astype(bf16)
        out = out + dot(h, wout[cs, :])
        mid = mid + dot_t(h, aout[:, cs])
        gn = gn + dot_t(gpre, win[:, cs])
        gm_in = gm_in + dot_t(gpre, bin_[:, cs])
        grads[:, 512 + c : 512 + c + CHUNK] += t_dot(mid_in, gpre)
        grads[:, 2560 + c : 2560 + c + CHUNK] += t_dot(gm_out, h)
    gm_in = (adapter_scale * gm_in).astype(bf16)
    grads[:, 0:512] += t_dot(gm_in, nb)
    grads[:, 4608:5120] += t_dot(mid.astype(bf16), go)
    result = x[...].reshape(TILE, CHANS).astype(f32) + scale * out
    out_ref[...] = result.reshape(TROWS, COLS, CHANS).astype(bf16)
    u = gn * gain
    standard = xh[...]
    m1 = jnp.mean(u, -1, keepdims=True)
    m2 = jnp.mean(u * standard, -1, keepdims=True)
    inverse = jnp.concatenate([rs[...]] * GROUPS, axis=1)
    result = inverse * (u - m1 - standard * m2)
    gc[...] = result.reshape(TROWS, COLS, CHANS).astype(bf16)
    put_edges(edge, result, edges, step, inner)


def third_kernel(
    flags, cot, cv, w, e, taps, scale, wout, bin_, bout, mid_in, mid_out, nrm_far, hid_far, slope_far,
    grads, he, line, gos, nrm, hid, slope, sems,
):
    step = pl.program_id(0)
    scale = scale[0:1, :]

    def copies(t):
        at = pl.ds(pl.multiple_of(t * TILE, TILE), TILE)
        return [
            pltpu.make_async_copy(far.at[at, :], near.at[t], sems.at[k, t])
            for k, (far, near) in enumerate(((nrm_far, nrm), (hid_far, hid), (slope_far, slope)))
        ]

    @pl.when(step == 0)
    def _():
        for t in range(PIXELS // TILE):
            for copy in copies(t):
                copy.start()
        hold_strips(he, w, e, flags)
        grads[...] = jnp.zeros_like(grads)

    def rows(i, c):
        g = cot[i].astype(f32) + whole_row(cv, he, taps, True, line, step, i)
        gos[row_of(i), :] = (g * scale).astype(bf16)
        return c

    lax.fori_loop(0, TROWS, rows, 0, unroll=8)
    for copy in copies(step):
        copy.wait()
    nb = nrm[step]
    go = gos[...]
    mi = mid_in[...]
    gm_out = (adapter_scale * dot_t(go, bout[...])).astype(bf16)
    gm_in = jnp.zeros((TILE, RANK), f32)
    for c in range(0, HIDDEN, CHUNK):
        cs = slice(c, c + CHUNK)
        gpre = (dot_t(go, wout[cs, :]) * slope[step, :, cs].astype(f32)).astype(bf16)
        gm_in = gm_in + dot_t(gpre, bin_[:, cs])
        grads[:, 512 + c : 512 + c + CHUNK] += t_dot(mi, gpre)
        grads[:, 2560 + c : 2560 + c + CHUNK] += t_dot(gm_out, hid[step, :, cs])
    gm_in = (adapter_scale * gm_in).astype(bf16)
    grads[:, 0:512] += t_dot(gm_in, nb)
    grads[:, 4608:5120] += t_dot(mid_out[...], go)


SMEM = pl.BlockSpec(memory_space=pltpu.SMEM)
ANY = pl.BlockSpec(memory_space=pl.ANY)
HE = pltpu.VMEM((40 * 48, 128), f32)
LINE = pltpu.VMEM((HALF * 8, 128), f32)
EDGE = pltpu.VMEM((TILE, 128), f32)


def fixed(*shape):
    return pl.BlockSpec(shape, lambda *t: (0,) * len(shape), pipeline_mode=pl.Buffered(1))


def layer(l, *shape):
    return pl.BlockSpec((None,) + shape, lambda t: (l,) + (0,) * len(shape), pipeline_mode=pl.Buffered(1))


def tiled(place, *shape):
    return pl.BlockSpec(shape, lambda t: (place(t),) + (0,) * (len(shape) - 1))


def call(kernel, name, grid, ins, outs, scratch, aliases={}, limit=26):
    return pl.pallas_call(
        kernel,
        grid=grid if isinstance(grid, tuple) else (grid,),
        out_shape=[jax.ShapeDtypeStruct(shape, dtype) for shape, dtype, _ in outs],
        in_specs=[spec for _, spec in ins],
        out_specs=[spec for _, _, spec in outs],
        scratch_shapes=scratch,
        input_output_aliases=aliases,
        name=name,
        compiler_params=pltpu.CompilerParams(vmem_limit_bytes=limit * 2**20),
    )(*[array for array, _ in ins])


def conv(arrays, sources, n, s, taps, l, flip, flags):
    return call(
        functools.partial(conv_kernel, sources, flip),
        "conv",
        4,
        [(flags, SMEM)]
        + [(a, fixed(*a.shape)) for a in arrays]
        + [(n, fixed(3, COLS, CHANS)), (s, fixed(3, COLS, CHANS))]
        + [(taps, layer(l, 49, 8, 128))],
        [((PIXELS * 4, 128), f32, tiled(lambda t: t, TILE * 4, 128))],
        [
            pltpu.VMEM((40, COLS, CHANS), bf16),
            pltpu.VMEM((SPAN * 8, 128), f32),
            pltpu.VMEM((40 * WIDE * 8, 128), f32),
        ],
        limit=12,
    )[0]


def swap(v, axis):
    n = lax.axis_size(axis)
    after = [(i, (i + 1) % n) for i in range(n)]
    before = [(j, i) for i, j in after]
    return lax.ppermute(v[1], axis, after), lax.ppermute(v[0], axis, before)


def strips(columns, north, south):
    sent = call(
        functools.partial(pack_kernel, len(columns) == 4),
        "pack",
        1,
        [(v, fixed(*v.shape)) for v in (*columns, north, south)],
        [((3, STRIP, CHANS), bf16, fixed(3, STRIP, CHANS))] * 2,
        [],
        limit=6,
    )
    return swap(sent, "col")


def total(first, second):
    core = lax.axis_index("col") % 2
    mine = jnp.where(core == 0, first, second)
    other = jnp.where(core == 0, second, first).astype(bf16)
    pair = [(i, i ^ 1) for i in range(16)]
    part = (mine + lax.ppermute(other, "col", pair).astype(f32)).astype(bf16)
    for even, odd in ((32, 4), (64, 8), (4, 1), (8, 16), (1, 32), (16, 64)):
        pairs = [(i, i ^ (odd if i & 2 else even)) for i in range(128)]
        other = lax.ppermute(part, ("row", "col", "rep"), pairs)
        part = (part.astype(f32) + other.astype(f32)).astype(bf16)
    back = lax.ppermute(part, "col", pair)
    return jnp.stack([jnp.where(core == 0, part, back), jnp.where(core == 0, back, part)]).astype(f32)


def normalize(stacked):
    mean = jnp.mean(stacked * stacked, axis=(1, 2), keepdims=True)
    return stacked * lax.rsqrt(mean + step_eps)


def body(
    features,
    cotangent,
    depthwise_filters,
    depthwise_bias_vector,
    layernorm_gain,
    layernorm_shift,
    inner_frozen_weight,
    outer_frozen_weight,
    inner_down_factor,
    inner_up_factor,
    outer_down_factor,
    outer_up_factor,
    branch_channel_scale,
):
    x0 = features.reshape(ROWS, COLS, CHANS)
    cot = cotangent.reshape(ROWS, COLS, CHANS)
    ain, bin_ = inner_down_factor.transpose(0, 2, 1), inner_up_factor
    aout, bout = outer_down_factor.transpose(0, 2, 1), outer_up_factor
    filters = depthwise_filters.transpose(1, 2, 0, 3).reshape(49, 2, CHANS)
    bias, gain, shift, scale = (
        depthwise_bias_vector, layernorm_gain, layernorm_shift, branch_channel_scale
    )
    row, col = lax.axis_index("row"), lax.axis_index("col")
    flags = jnp.stack(
        [row > 0, row < lax.axis_size("row") - 1, col > 0, col < lax.axis_size("col") - 1]
    ).astype(f32)

    west, east = call(
        edge_kernel,
        "edges",
        1,
        [(x0, pl.BlockSpec((ROWS, 8, CHANS), lambda t, k=k: (0, k, 0))) for k in (0, 3)],
        [((3, ROWS, CHANS), bf16, fixed(3, ROWS, CHANS))] * 2,
        [pltpu.VMEM((ROWS * 8, 128), f32)],
        limit=6,
    )
    north, south = swap((x0[:3], x0[-3:]), "row")
    part = HIDDEN // 4
    wide = (None, CHANS, part), lambda l, c: (l, 0, c)
    tall = (None, part, CHANS), lambda l, c: (l, c, 0)
    flat = (None, RANK, part), lambda l, c: (l, 0, c)
    full = (None, RANK, CHANS), lambda l, c: (l, 0, 0)
    win, wout, taps = call(
        fold_kernel,
        "fold",
        (2, 4),
        [
            (inner_frozen_weight, pl.BlockSpec(*wide)),
            (ain, pl.BlockSpec(*full)),
            (bin_, pl.BlockSpec(*flat)),
            (outer_frozen_weight, pl.BlockSpec(*tall)),
            (aout, pl.BlockSpec(*flat)),
            (bout, pl.BlockSpec(*full)),
            (filters, fixed(49, 2, CHANS)),
        ],
        [
            ((2, CHANS, HIDDEN), bf16, pl.BlockSpec(*wide)),
            ((2, HIDDEN, CHANS), bf16, pl.BlockSpec(*tall)),
            ((2, 49, 8, 128), f32, fixed(2, 49, 8, 128)),
        ],
        [],
        limit=12,
    )
    west, east, win, wout = lax.optimization_barrier((west, east, win, wout))
    west, east = strips([west, east], north, south)
    cv = conv([x0], [[(0, 0, 32)]], north, south, taps, 0, False, flags)

    strip_spec = fixed(3, STRIP, CHANS)

    def common(l, place, x, x_place):
        return [
            (flags, SMEM),
            (x, tiled(x_place, TROWS, COLS, CHANS)),
            (cv, tiled(place, TILE * 4, 128)),
            (west, strip_spec),
            (east, strip_spec),
            (taps, layer(l, 49, 8, 128)),
            (bias, fixed(2, CHANS)),
            (gain, fixed(2, CHANS)),
            (shift, fixed(2, CHANS)),
            (scale, fixed(2, CHANS)),
            (win, layer(l, CHANS, HIDDEN)),
            (wout, layer(l, HIDDEN, CHANS)),
            (ain, layer(l, RANK, CHANS)),
            (aout, layer(l, RANK, HIDDEN)),
        ]

    def outer_place(t):
        return 3 * t

    def inner_place(t):
        return t + 1

    def same(t):
        return t

    row_edges = [((3, COLS, CHANS), bf16, fixed(3, COLS, CHANS))] * 2
    col_edges = [((3, 16, CHANS), bf16, fixed(3, 16, CHANS))] * 2
    half = ((16, COLS, CHANS), bf16, tiled(same, TROWS, COLS, CHANS))

    def kept(place):
        return [
            ((PIXELS, width), bf16, tiled(place, TILE, width))
            for width in (CHANS, HIDDEN, HIDDEN, RANK, RANK)
        ]

    *saved, outer, top, bottom, west_a, east_a = call(
        functools.partial(first_kernel, False),
        "first_outer",
        2,
        common(0, outer_place, x0, outer_place),
        kept(outer_place) + [half] + row_edges + col_edges,
        [HE, LINE, EDGE],
    )
    north, south = swap((top, bottom), "row")
    ins = common(0, inner_place, x0, inner_place)
    *saved, inner, west_b, east_b = call(
        functools.partial(first_kernel, True),
        "first_inner",
        2,
        ins + [(v, ANY) for v in saved],
        kept(inner_place) + [half] + col_edges,
        [HE, LINE, EDGE],
        {len(ins) + i: i for i in range(5)},
    )
    split = [[(0, 0, 8), (8, 24, 8)], [(0, 8, 16)]]
    west, east = strips([west_a, west_b, east_a, east_b], north, south)
    cv = conv([outer, inner], split, north, south, taps, 1, False, flags)

    def second(place):
        return [
            (bin_, layer(1, RANK, HIDDEN)),
            (bout, layer(1, RANK, CHANS)),
            (cot, tiled(place, TROWS, COLS, CHANS)),
        ]

    def results(place):
        return [
            ((ROWS, COLS, CHANS), bf16, tiled(place, TROWS, COLS, CHANS)),
            ((RANK, GRADS), f32, fixed(RANK, GRADS)),
            half,
        ]

    work = [
        HE,
        LINE,
        EDGE,
        pltpu.VMEM((TILE, CHANS), bf16),
        pltpu.VMEM((TILE, CHANS), f32),
        pltpu.VMEM((TILE, 128), f32),
    ]
    out, grads1, outer_g, top, bottom, west_a, east_a = call(
        functools.partial(second_kernel, False),
        "second_outer",
        2,
        common(1, outer_place, outer, same) + second(outer_place),
        results(outer_place) + row_edges + col_edges,
        work,
    )
    north, south = swap((top, bottom), "row")
    ins = common(1, inner_place, inner, same) + second(inner_place)
    out, grads1, inner_g, west_b, east_b = call(
        functools.partial(second_kernel, True),
        "second_inner",
        2,
        ins + [(out, ANY), (grads1, fixed(RANK, GRADS))],
        results(inner_place) + col_edges,
        work,
        {len(ins): 0},
    )
    west, east = strips([west_a, west_b, east_a, east_b], north, south)
    cv = conv([outer_g, inner_g], split, north, south, taps, 1, True, flags)
    (grads0,) = call(
        third_kernel,
        "third",
        4,
        [
            (flags, SMEM),
            (cot, tiled(same, TROWS, COLS, CHANS)),
            (cv, tiled(same, TILE * 4, 128)),
            (west, strip_spec),
            (east, strip_spec),
            (taps, layer(1, 49, 8, 128)),
            (scale, fixed(2, CHANS)),
            (wout, layer(0, HIDDEN, CHANS)),
            (bin_, layer(0, RANK, HIDDEN)),
            (bout, layer(0, RANK, CHANS)),
        ]
        + [(v, tiled(same, TILE, RANK)) for v in saved[3:]]
        + [(v, pl.BlockSpec(memory_space=pltpu.HBM)) for v in saved[:3]],
        [((RANK, GRADS), f32, fixed(RANK, GRADS))],
        [HE, LINE, pltpu.VMEM((TILE, CHANS), bf16)]
        + [pltpu.VMEM((4, TILE, width), bf16) for width in (CHANS, HIDDEN, HIDDEN)]
        + [pltpu.SemaphoreType.DMA((3, 4))],
    )
    sums = total(grads0, grads1)
    return (
        out[None],
        normalize(sums[:, :, 0:512].transpose(0, 2, 1)),
        normalize(adapter_scale * sums[:, :, 512:2560]),
        normalize(sums[:, :, 2560:4608].transpose(0, 2, 1)),
        normalize(adapter_scale * sums[:, :, 4608:5120]),
    )


def solution(mesh):
    tile = P("rep", "row", "col", None)
    return jax.shard_map(
        body,
        mesh=mesh,
        in_specs=(tile, tile) + (P(),) * 11,
        out_specs=(tile, P(), P(), P(), P()),
        check_vma=False,
    )
```

```python
import functools

import jax
import jax.numpy as jnp
from jax import lax
from jax.experimental import pallas as pl
from jax.experimental.pallas import tpu as pltpu
from jax.sharding import PartitionSpec as P

BLOCK_COUNT = 2
ROWS, COLS, CHANS, HIDDEN, RANK = 32, 32, 512, 2048, 16
PIXELS = ROWS * COLS
GROUPS = CHANS // 128
HALF = COLS // 2
SPAN = 32
OFFSET = 5
WIDE = HALF + 6
TROWS = 8
TILE = TROWS * COLS
CHUNK = 2048
STRIP = 48
GRADS = 2 * (CHANS + HIDDEN)

adapter_scale = 2.0
norm_eps = 1e-06
step_eps = 1e-06
gelu_coef = 0.7978845608
f32, bf16 = jnp.float32, jnp.bfloat16


def dot(a, b):
    return jnp.dot(a, b, preferred_element_type=f32)


def dot_t(a, b):
    return lax.dot_general(a, b, (((1,), (1,)), ((), ())), preferred_element_type=f32)


def t_dot(a, b):
    return lax.dot_general(a, b, (((0,), (0,)), ((), ())), preferred_element_type=f32)


CENTRE = [(k, g, 0, 8 * k + 8) for k in (0, 1, 2) for g in range(GROUPS)] + [
    (k, g, 1, 8 * k - 8) for k in (1, 2, 3) for g in range(GROUPS)
]


def spread(xs, row, values):
    for k, g, half, at in CENTRE:
        start = (row * SPAN + at) * 8 + half * GROUPS + g
        xs[pl.ds(start, 8, stride=8), :] = values[8 * k : 8 * k + 8, 128 * g : 128 * g + 128]


def conv_kernel(sources, flip, flags, *refs):
    xrefs, (n, s, taps, cv, held, spans, lines) = refs[: len(sources)], refs[len(sources) :]
    step = pl.program_id(0)
    zero = jnp.zeros((8, 128), f32)
    left = lax.broadcasted_iota(jnp.int32, (8, 128), 0) < GROUPS

    def take(row):
        spread(spans, 0, held[row].astype(f32))
        base = pl.multiple_of(row * (WIDE * 8), WIDE * 8)
        for k in range(WIDE):
            reg = spans[(OFFSET + k) * 8 : (OFFSET + k) * 8 + 8, :]
            if k < 3:
                reg = jnp.where(left, zero, reg)
            if k >= HALF + 3:
                reg = jnp.where(left, reg, zero)
            lines[pl.ds(base + k * 8, 8), :] = reg

    @pl.when(step == 0)
    def _():
        for ref, pieces in zip(xrefs, sources):
            for at, row, count in pieces:
                held[row + 3 : row + 3 + count] = ref[at : at + count]
        held[0:3] = (n[...].astype(f32) * flags[0]).astype(bf16)
        held[ROWS + 3 : ROWS + 6] = (s[...].astype(f32) * flags[1]).astype(bf16)
        held[ROWS + 6 :] = jnp.zeros((2, COLS, CHANS), bf16)
        lax.fori_loop(0, 38, lambda r, c: (take(r), c)[1], 0)

    def row(i, c):
        at = step * TROWS + i
        totals = [zero] * HALF
        for a in range(7):
            base = pl.multiple_of((at + a) * (WIDE * 8), WIDE * 8)
            line = [lines[pl.ds(base + k * 8, 8), :] for k in range(WIDE)]
            for b in range(7):
                tap = taps[48 - (a * 7 + b) if flip else a * 7 + b]
                for k in range(HALF):
                    totals[k] = totals[k] + line[k + b] * tap
        base = pl.multiple_of(i * (HALF * 8), HALF * 8)
        for k in range(HALF):
            cv[pl.ds(base + k * 8, 8), :] = totals[k]
        return c

    lax.fori_loop(0, TROWS, row, 0)


def hold_strips(he, w, e, flags):
    he[...] = jnp.zeros_like(he)
    for side, ref in ((0, w), (1, e)):
        for c in range(3):
            for block, row in ((4, 0), (5, 35), (0, 3), (2, 11), (3, 19), (1, 27)):
                v = ref[c, 8 * block : 8 * block + 8, :].astype(f32) * flags[2 + side]
                if block >= 4:
                    v = v * flags[block - 4]
                if block == 5:
                    v = v[0:3]
                for g in range(GROUPS):
                    start = (row * 6 + side * 3 + c) * 8 + side * GROUPS + g
                    he[pl.ds(start, v.shape[0], stride=48), :] = v[:, 128 * g : 128 * g + 128]


def whole_row(cv, he, taps, flip, line, tile, i):
    base = pl.multiple_of(i * (HALF * 8), HALF * 8)
    totals = [cv[pl.ds(base + k * 8, 8), :] for k in range(HALF)]
    for a in range(7):
        at = pl.multiple_of((tile * TROWS + i + a) * 48, 48)
        edge = [he[pl.ds(at + 8 * k, 8), :] for k in range(6)]
        pairs = [(k, h, h - k) for k in range(3) for h in range(k, 3)]
        pairs += [(k, 3 + h, 19 + h - k) for k in (13, 14, 15) for h in range(k - 12)]
        for k, h, b in pairs:
            totals[k] = totals[k] + edge[h] * taps[48 - (a * 7 + b) if flip else a * 7 + b]
    for k in range(HALF):
        line[k * 8 : k * 8 + 8, :] = totals[k]
    parts = []
    for k in range(4):
        start = (k % 2) * 64 + (k // 2) * GROUPS
        parts.append(
            jnp.concatenate([line[pl.ds(start + g, 8, stride=8), :] for g in range(GROUPS)], axis=1)
        )
    return jnp.concatenate(parts, axis=0)


def gelu_parts(v):
    square = v * v
    t = jnp.tanh(v * (gelu_coef + (gelu_coef * 0.044715) * square))
    h = 0.5 * t + 0.5
    value = v * h
    slope = h + value * (1.0 - t) * (gelu_coef + (3.0 * 0.044715 * gelu_coef) * square)
    return value, slope


def row_of(i):
    return pl.ds(pl.multiple_of(i * COLS, COLS), COLS)


def norm_rows(cv, he, taps, line, tile, bias, gain, shift, nrm, xh=None, rs=None):
    def body(i, c):
        conv = whole_row(cv, he, taps, False, line, tile, i) + bias
        centred = conv - jnp.mean(conv, -1, keepdims=True)
        inverse = lax.rsqrt(jnp.mean(centred * centred, -1, keepdims=True) + norm_eps)
        standard = centred * inverse
        nrm[row_of(i), :] = (standard * gain + shift).astype(bf16)
        if xh is not None:
            xh[row_of(i), :] = standard
            rs[row_of(i), :] = jnp.broadcast_to(inverse, (COLS, 128))
        return c

    lax.fori_loop(0, TROWS, body, 0, unroll=8)


def put_edges(edge, value, refs, step, inner):
    west, east = refs[-2:]
    if not inner:
        top, bottom = refs[:2]

        @pl.when(step == 0)
        def _():
            top[...] = value[: 3 * COLS].reshape(3, COLS, CHANS).astype(bf16)

        @pl.when(step == 1)
        def _():
            bottom[...] = value[5 * COLS :].reshape(3, COLS, CHANS).astype(bf16)

    for g in range(GROUPS):
        cs = slice(128 * g, 128 * g + 128)
        edge[...] = value[:, cs]
        for c in range(3):
            at = pl.ds(pl.multiple_of(step * 8, 8), 8)
            west[c, at, cs] = edge[pl.ds(c, 8, stride=COLS), :].astype(bf16)
            east[c, at, cs] = edge[pl.ds(COLS - 3 + c, 8, stride=COLS), :].astype(bf16)


def edge_kernel(first, last, west, east, edge):
    for ref, out, at in ((first, west, 0), (last, east, 5)):
        for g in range(GROUPS):
            cs = slice(128 * g, 128 * g + 128)
            edge[...] = ref[:, :, cs].reshape(ROWS * 8, 128).astype(f32)
            for c in range(3):
                out[c, :, cs] = edge[pl.ds(at + c, ROWS, stride=8), :].astype(bf16)


def pack_kernel(split, *refs):
    pieces, (n, s, west, east) = refs[:-4], refs[-4:]
    for side, out in ((0, west), (1, east)):
        if split:
            out[:, 0:16] = pieces[2 * side][...]
            out[:, 16:32] = pieces[2 * side + 1][...]
        else:
            v = pieces[side]
            for block, row in enumerate((0, 24, 8, 16)):
                out[:, 8 * block : 8 * block + 8] = v[:, row : row + 8]
        for at, ref in ((32, n), (40, s)):
            cut = slice(COLS - 8, COLS) if side else slice(0, 8)
            v = [ref[r, cut, :].astype(f32) for r in range(3)]
            for c in range(3):
                k = c + 5 if side else c
                rows = [v[r][k : k + 1] for r in range(3)] + [jnp.zeros((5, CHANS), f32)]
                out[c, at : at + 8] = jnp.concatenate(rows, axis=0).astype(bf16)


def fold_kernel(win, ain, bin_, wout, aout, bout, filters, win_out, wout_out, taps):
    @pl.when((pl.program_id(0) == 0) & (pl.program_id(1) == 0))
    def _():
        for t in range(49):
            v = filters[t]
            for l in range(2):
                for g in range(8):
                    at = 128 * (g % GROUPS)
                    taps[l, t, g : g + 1, :] = v[l : l + 1, at : at + 128]

    win_out[...] = (win[...].astype(f32) + adapter_scale * t_dot(ain[...], bin_[...])).astype(bf16)
    wout_out[...] = (wout[...].astype(f32) + adapter_scale * t_dot(aout[...], bout[...])).astype(bf16)


def first_kernel(inner, flags, x, cv, w, e, taps, bias, gain, shift, scale, win, wout, ain, aout, *refs):
    refs = refs[5 if inner else 0 :]
    bias, gain, shift, scale = (v[0:1, :] for v in (bias, gain, shift, scale))
    nrm, hid, slope, mid_in, mid_out, y = refs[:6]
    edges, (he, line, edge) = refs[6:-3], refs[-3:]
    step = pl.program_id(0)
    tile = step + 1 if inner else 3 * step

    @pl.when(step == 0)
    def _():
        hold_strips(he, w, e, flags)

    norm_rows(cv, he, taps, line, tile, bias, gain, shift, nrm)
    nb = nrm[...]
    mid_in[...] = dot_t(nb, ain[...]).astype(bf16)
    out = jnp.zeros((TILE, CHANS), f32)
    mid = jnp.zeros((TILE, RANK), f32)
    for c in range(0, HIDDEN, CHUNK):
        cs = slice(c, c + CHUNK)
        value, sl = gelu_parts(dot(nb, win[:, cs]))
        h = value.astype(bf16)
        hid[:, cs] = h
        slope[:, cs] = sl.astype(bf16)
        out = out + dot(h, wout[cs, :])
        mid = mid + dot_t(h, aout[:, cs])
    mid_out[...] = mid.astype(bf16)
    result = x[...].reshape(TILE, CHANS).astype(f32) + scale * out
    y[...] = result.reshape(TROWS, COLS, CHANS).astype(bf16)
    put_edges(edge, result, edges, step, inner)


def second_kernel(
    inner, flags, x, cv, w, e, taps, bias, gain, shift, scale, win, wout, ain, aout, bin_, bout, cot, *refs
):
    bias, gain, shift, scale = (v[1:2, :] for v in (bias, gain, shift, scale))
    if inner:
        before, refs = refs[1], refs[2:]
    out_ref, grads, gc = refs[:3]
    edges, (he, line, edge, nrm, xh, rs) = refs[3:-6], refs[-6:]
    step = pl.program_id(0)
    tile = step + 1 if inner else 3 * step

    @pl.when(step == 0)
    def _():
        hold_strips(he, w, e, flags)
        grads[...] = before[...] if inner else jnp.zeros_like(grads)

    norm_rows(cv, he, taps, line, tile, bias, gain, shift, nrm, xh, rs)
    nb = nrm[...]
    go = (cot[...].reshape(TILE, CHANS).astype(f32) * scale).astype(bf16)
    mid_in = dot_t(nb, ain[...]).astype(bf16)
    gm_out = (adapter_scale * dot_t(go, bout[...])).astype(bf16)
    out = jnp.zeros((TILE, CHANS), f32)
    gn = jnp.zeros((TILE, CHANS), f32)
    mid = jnp.zeros((TILE, RANK), f32)
    gm_in = jnp.zeros((TILE, RANK), f32)
    for c in range(0, HIDDEN, CHUNK):
        cs = slice(c, c + CHUNK)
        value, sl = gelu_parts(dot(nb, win[:, cs]))
        h = value.astype(bf16)
        gpre = (dot_t(go, wout[cs, :]) * sl).astype(bf16)
        out = out + dot(h, wout[cs, :])
        mid = mid + dot_t(h, aout[:, cs])
        gn = gn + dot_t(gpre, win[:, cs])
        gm_in = gm_in + dot_t(gpre, bin_[:, cs])
        grads[:, 512 + c : 512 + c + CHUNK] += t_dot(mid_in, gpre)
        grads[:, 2560 + c : 2560 + c + CHUNK] += t_dot(gm_out, h)
    gm_in = (adapter_scale * gm_in).astype(bf16)
    grads[:, 0:512] += t_dot(gm_in, nb)
    grads[:, 4608:5120] += t_dot(mid.astype(bf16), go)
    result = x[...].reshape(TILE, CHANS).astype(f32) + scale * out
    out_ref[...] = result.reshape(TROWS, COLS, CHANS).astype(bf16)
    u = gn * gain
    standard = xh[...]
    m1 = jnp.mean(u, -1, keepdims=True)
    m2 = jnp.mean(u * standard, -1, keepdims=True)
    inverse = jnp.concatenate([rs[...]] * GROUPS, axis=1)
    result = inverse * (u - m1 - standard * m2)
    gc[...] = result.reshape(TROWS, COLS, CHANS).astype(bf16)
    put_edges(edge, result, edges, step, inner)


def third_kernel(
    flags, cot, cv, w, e, taps, scale, wout, bin_, bout, mid_in, mid_out, nrm_far, hid_far, slope_far,
    grads, he, line, gos, nrm, hid, slope, sems,
):
    step = pl.program_id(0)
    scale = scale[0:1, :]

    def copies(t):
        at = pl.ds(pl.multiple_of(t * TILE, TILE), TILE)
        return [
            pltpu.make_async_copy(far.at[at, :], near.at[t], sems.at[k, t])
            for k, (far, near) in enumerate(((nrm_far, nrm), (hid_far, hid), (slope_far, slope)))
        ]

    @pl.when(step == 0)
    def _():
        for t in range(PIXELS // TILE):
            for copy in copies(t):
                copy.start()
        hold_strips(he, w, e, flags)
        grads[...] = jnp.zeros_like(grads)

    def rows(i, c):
        g = cot[i].astype(f32) + whole_row(cv, he, taps, True, line, step, i)
        gos[row_of(i), :] = (g * scale).astype(bf16)
        return c

    lax.fori_loop(0, TROWS, rows, 0, unroll=8)
    for copy in copies(step):
        copy.wait()
    nb = nrm[step]
    go = gos[...]
    mi = mid_in[...]
    gm_out = (adapter_scale * dot_t(go, bout[...])).astype(bf16)
    gm_in = jnp.zeros((TILE, RANK), f32)
    for c in range(0, HIDDEN, CHUNK):
        cs = slice(c, c + CHUNK)
        gpre = (dot_t(go, wout[cs, :]) * slope[step, :, cs].astype(f32)).astype(bf16)
        gm_in = gm_in + dot_t(gpre, bin_[:, cs])
        grads[:, 512 + c : 512 + c + CHUNK] += t_dot(mi, gpre)
        grads[:, 2560 + c : 2560 + c + CHUNK] += t_dot(gm_out, hid[step, :, cs])
    gm_in = (adapter_scale * gm_in).astype(bf16)
    grads[:, 0:512] += t_dot(gm_in, nb)
    grads[:, 4608:5120] += t_dot(mid_out[...], go)


SMEM = pl.BlockSpec(memory_space=pltpu.SMEM)
ANY = pl.BlockSpec(memory_space=pl.ANY)
HE = pltpu.VMEM((40 * 48, 128), f32)
LINE = pltpu.VMEM((HALF * 8, 128), f32)
EDGE = pltpu.VMEM((TILE, 128), f32)


def fixed(*shape):
    return pl.BlockSpec(shape, lambda *t: (0,) * len(shape), pipeline_mode=pl.Buffered(1))


def layer(l, *shape):
    return pl.BlockSpec((None,) + shape, lambda t: (l,) + (0,) * len(shape), pipeline_mode=pl.Buffered(1))


def tiled(place, *shape):
    return pl.BlockSpec(shape, lambda t: (place(t),) + (0,) * (len(shape) - 1))


def call(kernel, name, grid, ins, outs, scratch, aliases={}, limit=26, far=()):
    return pl.pallas_call(
        kernel,
        grid=grid if isinstance(grid, tuple) else (grid,),
        out_shape=[
            pltpu.HBM(shape, dtype) if k in far else jax.ShapeDtypeStruct(shape, dtype)
            for k, (shape, dtype, _) in enumerate(outs)
        ],
        in_specs=[spec for _, spec in ins],
        out_specs=[spec for _, _, spec in outs],
        scratch_shapes=scratch,
        input_output_aliases=aliases,
        name=name,
        compiler_params=pltpu.CompilerParams(vmem_limit_bytes=limit * 2**20),
    )(*[array for array, _ in ins])


def conv(arrays, sources, n, s, taps, l, flip, flags):
    return call(
        functools.partial(conv_kernel, sources, flip),
        "conv",
        4,
        [(flags, SMEM)]
        + [(a, fixed(*a.shape)) for a in arrays]
        + [(n, fixed(3, COLS, CHANS)), (s, fixed(3, COLS, CHANS))]
        + [(taps, layer(l, 49, 8, 128))],
        [((PIXELS * 4, 128), f32, tiled(lambda t: t, TILE * 4, 128))],
        [
            pltpu.VMEM((40, COLS, CHANS), bf16),
            pltpu.VMEM((SPAN * 8, 128), f32),
            pltpu.VMEM((40 * WIDE * 8, 128), f32),
        ],
        limit=12,
    )[0]


def swap(v, axis):
    n = lax.axis_size(axis)
    after = [(i, (i + 1) % n) for i in range(n)]
    before = [(j, i) for i, j in after]
    return lax.ppermute(v[1], axis, after), lax.ppermute(v[0], axis, before)


def strips(columns, north, south):
    sent = call(
        functools.partial(pack_kernel, len(columns) == 4),
        "pack",
        1,
        [(v, fixed(*v.shape)) for v in (*columns, north, south)],
        [((3, STRIP, CHANS), bf16, fixed(3, STRIP, CHANS))] * 2,
        [],
        limit=6,
    )
    return swap(sent, "col")


def total(first, second):
    core = lax.axis_index("col") % 2
    mine = jnp.where(core == 0, first, second)
    other = jnp.where(core == 0, second, first).astype(bf16)
    pair = [(i, i ^ 1) for i in range(16)]
    part = (mine + lax.ppermute(other, "col", pair).astype(f32)).astype(bf16)
    for even, odd in ((32, 4), (64, 8), (4, 1), (8, 16), (1, 32), (16, 64)):
        pairs = [(i, i ^ (odd if i & 2 else even)) for i in range(128)]
        other = lax.ppermute(part, ("row", "col", "rep"), pairs)
        part = (part.astype(f32) + other.astype(f32)).astype(bf16)
    back = lax.ppermute(part, "col", pair)
    return jnp.stack([jnp.where(core == 0, part, back), jnp.where(core == 0, back, part)]).astype(f32)


def normalize(stacked):
    mean = jnp.mean(stacked * stacked, axis=(1, 2), keepdims=True)
    return stacked * lax.rsqrt(mean + step_eps)


def body(
    features,
    cotangent,
    depthwise_filters,
    depthwise_bias_vector,
    layernorm_gain,
    layernorm_shift,
    inner_frozen_weight,
    outer_frozen_weight,
    inner_down_factor,
    inner_up_factor,
    outer_down_factor,
    outer_up_factor,
    branch_channel_scale,
):
    x0 = features.reshape(ROWS, COLS, CHANS)
    cot = cotangent.reshape(ROWS, COLS, CHANS)
    ain, bin_ = inner_down_factor.transpose(0, 2, 1), inner_up_factor
    aout, bout = outer_down_factor.transpose(0, 2, 1), outer_up_factor
    filters = depthwise_filters.transpose(1, 2, 0, 3).reshape(49, 2, CHANS)
    bias, gain, shift, scale = (
        depthwise_bias_vector, layernorm_gain, layernorm_shift, branch_channel_scale
    )
    row, col = lax.axis_index("row"), lax.axis_index("col")
    flags = jnp.stack(
        [row > 0, row < lax.axis_size("row") - 1, col > 0, col < lax.axis_size("col") - 1]
    ).astype(f32)

    west, east = call(
        edge_kernel,
        "edges",
        1,
        [(x0, pl.BlockSpec((ROWS, 8, CHANS), lambda t, k=k: (0, k, 0))) for k in (0, 3)],
        [((3, ROWS, CHANS), bf16, fixed(3, ROWS, CHANS))] * 2,
        [pltpu.VMEM((ROWS * 8, 128), f32)],
        limit=6,
    )
    north, south = swap((x0[:3], x0[-3:]), "row")
    part = HIDDEN // 4
    wide = (None, CHANS, part), lambda l, c: (l, 0, c)
    tall = (None, part, CHANS), lambda l, c: (l, c, 0)
    flat = (None, RANK, part), lambda l, c: (l, 0, c)
    full = (None, RANK, CHANS), lambda l, c: (l, 0, 0)
    win, wout, taps = call(
        fold_kernel,
        "fold",
        (2, 4),
        [
            (inner_frozen_weight, pl.BlockSpec(*wide)),
            (ain, pl.BlockSpec(*full)),
            (bin_, pl.BlockSpec(*flat)),
            (outer_frozen_weight, pl.BlockSpec(*tall)),
            (aout, pl.BlockSpec(*flat)),
            (bout, pl.BlockSpec(*full)),
            (filters, fixed(49, 2, CHANS)),
        ],
        [
            ((2, CHANS, HIDDEN), bf16, pl.BlockSpec(*wide)),
            ((2, HIDDEN, CHANS), bf16, pl.BlockSpec(*tall)),
            ((2, 49, 8, 128), f32, fixed(2, 49, 8, 128)),
        ],
        [],
        limit=12,
    )
    west, east, win, wout = lax.optimization_barrier((west, east, win, wout))
    west, east = strips([west, east], north, south)
    cv = conv([x0], [[(0, 0, 32)]], north, south, taps, 0, False, flags)

    strip_spec = fixed(3, STRIP, CHANS)

    def common(l, place, x, x_place):
        return [
            (flags, SMEM),
            (x, tiled(x_place, TROWS, COLS, CHANS)),
            (cv, tiled(place, TILE * 4, 128)),
            (west, strip_spec),
            (east, strip_spec),
            (taps, layer(l, 49, 8, 128)),
            (bias, fixed(2, CHANS)),
            (gain, fixed(2, CHANS)),
            (shift, fixed(2, CHANS)),
            (scale, fixed(2, CHANS)),
            (win, layer(l, CHANS, HIDDEN)),
            (wout, layer(l, HIDDEN, CHANS)),
            (ain, layer(l, RANK, CHANS)),
            (aout, layer(l, RANK, HIDDEN)),
        ]

    def outer_place(t):
        return 3 * t

    def inner_place(t):
        return t + 1

    def same(t):
        return t

    row_edges = [((3, COLS, CHANS), bf16, fixed(3, COLS, CHANS))] * 2
    col_edges = [((3, 16, CHANS), bf16, fixed(3, 16, CHANS))] * 2
    half = ((16, COLS, CHANS), bf16, tiled(same, TROWS, COLS, CHANS))

    def kept(place):
        return [
            ((PIXELS, width), bf16, tiled(place, TILE, width))
            for width in (CHANS, HIDDEN, HIDDEN, RANK, RANK)
        ]

    *saved, outer, top, bottom, west_a, east_a = call(
        functools.partial(first_kernel, False),
        "first_outer",
        2,
        common(0, outer_place, x0, outer_place),
        kept(outer_place) + [half] + row_edges + col_edges,
        [HE, LINE, EDGE],
        far=(0, 1, 2),
    )
    north, south = swap((top, bottom), "row")
    ins = common(0, inner_place, x0, inner_place)
    *saved, inner, west_b, east_b = call(
        functools.partial(first_kernel, True),
        "first_inner",
        2,
        ins + [(v, ANY) for v in saved],
        kept(inner_place) + [half] + col_edges,
        [HE, LINE, EDGE],
        {len(ins) + i: i for i in range(5)},
        far=(0, 1, 2),
    )
    split = [[(0, 0, 8), (8, 24, 8)], [(0, 8, 16)]]
    west, east = strips([west_a, west_b, east_a, east_b], north, south)
    cv = conv([outer, inner], split, north, south, taps, 1, False, flags)

    def second(place):
        return [
            (bin_, layer(1, RANK, HIDDEN)),
            (bout, layer(1, RANK, CHANS)),
            (cot, tiled(place, TROWS, COLS, CHANS)),
        ]

    def results(place):
        return [
            ((ROWS, COLS, CHANS), bf16, tiled(place, TROWS, COLS, CHANS)),
            ((RANK, GRADS), f32, fixed(RANK, GRADS)),
            half,
        ]

    work = [
        HE,
        LINE,
        EDGE,
        pltpu.VMEM((TILE, CHANS), bf16),
        pltpu.VMEM((TILE, CHANS), f32),
        pltpu.VMEM((TILE, 128), f32),
    ]
    out, grads1, outer_g, top, bottom, west_a, east_a = call(
        functools.partial(second_kernel, False),
        "second_outer",
        2,
        common(1, outer_place, outer, same) + second(outer_place),
        results(outer_place) + row_edges + col_edges,
        work,
    )
    north, south = swap((top, bottom), "row")
    ins = common(1, inner_place, inner, same) + second(inner_place)
    out, grads1, inner_g, west_b, east_b = call(
        functools.partial(second_kernel, True),
        "second_inner",
        2,
        ins + [(out, ANY), (grads1, fixed(RANK, GRADS))],
        results(inner_place) + col_edges,
        work,
        {len(ins): 0},
    )
    west, east = strips([west_a, west_b, east_a, east_b], north, south)
    cv = conv([outer_g, inner_g], split, north, south, taps, 1, True, flags)
    (grads0,) = call(
        third_kernel,
        "third",
        4,
        [
            (flags, SMEM),
            (cot, tiled(same, TROWS, COLS, CHANS)),
            (cv, tiled(same, TILE * 4, 128)),
            (west, strip_spec),
            (east, strip_spec),
            (taps, layer(1, 49, 8, 128)),
            (scale, fixed(2, CHANS)),
            (wout, layer(0, HIDDEN, CHANS)),
            (bin_, layer(0, RANK, HIDDEN)),
            (bout, layer(0, RANK, CHANS)),
        ]
        + [(v, tiled(same, TILE, RANK)) for v in saved[3:]]
        + [(v, pl.BlockSpec(memory_space=pltpu.HBM)) for v in saved[:3]],
        [((RANK, GRADS), f32, fixed(RANK, GRADS))],
        [HE, LINE, pltpu.VMEM((TILE, CHANS), bf16)]
        + [pltpu.VMEM((4, TILE, width), bf16) for width in (CHANS, HIDDEN, HIDDEN)]
        + [pltpu.SemaphoreType.DMA((3, 4))],
    )
    sums = total(grads0, grads1)
    return (
        out[None],
        normalize(sums[:, :, 0:512].transpose(0, 2, 1)),
        normalize(adapter_scale * sums[:, :, 512:2560]),
        normalize(sums[:, :, 2560:4608].transpose(0, 2, 1)),
        normalize(adapter_scale * sums[:, :, 4608:5120]),
    )


def solution(mesh):
    tile = P("rep", "row", "col", None)
    return jax.shard_map(
        body,
        mesh=mesh,
        in_specs=(tile, tile) + (P(),) * 11,
        out_specs=(tile, P(), P(), P(), P()),
        check_vma=False,
    )
```

```python
import functools

import jax
import jax.numpy as jnp
from jax import lax
from jax.experimental import pallas as pl
from jax.experimental.pallas import tpu as pltpu
from jax.sharding import PartitionSpec as P

BLOCK_COUNT = 2
ROWS, COLS, CHANS, HIDDEN, RANK = 32, 32, 512, 2048, 16
PIXELS = ROWS * COLS
GROUPS = CHANS // 128
HALF = COLS // 2
SPAN = 32
OFFSET = 5
WIDE = HALF + 6
TROWS = 8
TILE = TROWS * COLS
CHUNK = 2048
STRIP = 48
GRADS = 2 * (CHANS + HIDDEN)

adapter_scale = 2.0
norm_eps = 1e-06
step_eps = 1e-06
gelu_coef = 0.7978845608
f32, bf16 = jnp.float32, jnp.bfloat16


def dot(a, b):
    return jnp.dot(a, b, preferred_element_type=f32)


def dot_t(a, b):
    return lax.dot_general(a, b, (((1,), (1,)), ((), ())), preferred_element_type=f32)


def t_dot(a, b):
    return lax.dot_general(a, b, (((0,), (0,)), ((), ())), preferred_element_type=f32)


CENTRE = [(k, g, 0, 8 * k + 8) for k in (0, 1, 2) for g in range(GROUPS)] + [
    (k, g, 1, 8 * k - 8) for k in (1, 2, 3) for g in range(GROUPS)
]


def spread(xs, row, values):
    for k, g, half, at in CENTRE:
        start = (row * SPAN + at) * 8 + half * GROUPS + g
        xs[pl.ds(start, 8, stride=8), :] = values[8 * k : 8 * k + 8, 128 * g : 128 * g + 128]


def conv_kernel(sources, flip, flags, *refs):
    xrefs, (n, s, taps, cv, held, spans, lines) = refs[: len(sources)], refs[len(sources) :]
    step = pl.program_id(0)
    zero = jnp.zeros((8, 128), f32)
    left = lax.broadcasted_iota(jnp.int32, (8, 128), 0) < GROUPS

    def take(row):
        spread(spans, 0, held[row].astype(f32))
        base = pl.multiple_of(row * (WIDE * 8), WIDE * 8)
        for k in range(WIDE):
            reg = spans[(OFFSET + k) * 8 : (OFFSET + k) * 8 + 8, :]
            if k < 3:
                reg = jnp.where(left, zero, reg)
            if k >= HALF + 3:
                reg = jnp.where(left, reg, zero)
            lines[pl.ds(base + k * 8, 8), :] = reg

    @pl.when(step == 0)
    def _():
        for ref, pieces in zip(xrefs, sources):
            for at, row, count in pieces:
                held[row + 3 : row + 3 + count] = ref[at : at + count]
        held[0:3] = (n[...].astype(f32) * flags[0]).astype(bf16)
        held[ROWS + 3 : ROWS + 6] = (s[...].astype(f32) * flags[1]).astype(bf16)
        held[ROWS + 6 :] = jnp.zeros((2, COLS, CHANS), bf16)
        lax.fori_loop(0, 38, lambda r, c: (take(r), c)[1], 0)

    def row(i, c):
        at = step * TROWS + i
        totals = [zero] * HALF
        for a in range(7):
            base = pl.multiple_of((at + a) * (WIDE * 8), WIDE * 8)
            line = [lines[pl.ds(base + k * 8, 8), :] for k in range(WIDE)]
            for b in range(7):
                tap = taps[48 - (a * 7 + b) if flip else a * 7 + b]
                for k in range(HALF):
                    totals[k] = totals[k] + line[k + b] * tap
        base = pl.multiple_of(i * (HALF * 8), HALF * 8)
        for k in range(HALF):
            cv[pl.ds(base + k * 8, 8), :] = totals[k]
        return c

    lax.fori_loop(0, TROWS, row, 0)


def hold_strips(he, w, e, flags):
    he[...] = jnp.zeros_like(he)
    for side, ref in ((0, w), (1, e)):
        for c in range(3):
            for block, row in ((4, 0), (5, 35), (0, 3), (2, 11), (3, 19), (1, 27)):
                v = ref[c, 8 * block : 8 * block + 8, :].astype(f32) * flags[2 + side]
                if block >= 4:
                    v = v * flags[block - 4]
                if block == 5:
                    v = v[0:3]
                for g in range(GROUPS):
                    start = (row * 6 + side * 3 + c) * 8 + side * GROUPS + g
                    he[pl.ds(start, v.shape[0], stride=48), :] = v[:, 128 * g : 128 * g + 128]


def whole_row(cv, he, taps, flip, line, tile, i):
    base = pl.multiple_of(i * (HALF * 8), HALF * 8)
    totals = [cv[pl.ds(base + k * 8, 8), :] for k in range(HALF)]
    for a in range(7):
        at = pl.multiple_of((tile * TROWS + i + a) * 48, 48)
        edge = [he[pl.ds(at + 8 * k, 8), :] for k in range(6)]
        pairs = [(k, h, h - k) for k in range(3) for h in range(k, 3)]
        pairs += [(k, 3 + h, 19 + h - k) for k in (13, 14, 15) for h in range(k - 12)]
        for k, h, b in pairs:
            totals[k] = totals[k] + edge[h] * taps[48 - (a * 7 + b) if flip else a * 7 + b]
    for k in range(HALF):
        line[k * 8 : k * 8 + 8, :] = totals[k]
    parts = []
    for k in range(4):
        start = (k % 2) * 64 + (k // 2) * GROUPS
        parts.append(
            jnp.concatenate([line[pl.ds(start + g, 8, stride=8), :] for g in range(GROUPS)], axis=1)
        )
    return jnp.concatenate(parts, axis=0)


def gelu_parts(v):
    square = v * v
    t = jnp.tanh(v * (gelu_coef + (gelu_coef * 0.044715) * square))
    h = 0.5 * t + 0.5
    value = v * h
    slope = h + value * (1.0 - t) * (gelu_coef + (3.0 * 0.044715 * gelu_coef) * square)
    return value, slope


def row_of(i):
    return pl.ds(pl.multiple_of(i * COLS, COLS), COLS)


def norm_rows(cv, he, taps, line, tile, bias, gain, shift, nrm, xh=None, rs=None):
    def body(i, c):
        conv = whole_row(cv, he, taps, False, line, tile, i) + bias
        centred = conv - jnp.mean(conv, -1, keepdims=True)
        inverse = lax.rsqrt(jnp.mean(centred * centred, -1, keepdims=True) + norm_eps)
        standard = centred * inverse
        nrm[row_of(i), :] = (standard * gain + shift).astype(bf16)
        if xh is not None:
            xh[row_of(i), :] = standard
            rs[row_of(i), :] = jnp.broadcast_to(inverse, (COLS, 128))
        return c

    lax.fori_loop(0, TROWS, body, 0, unroll=8)


def put_edges(edge, value, refs, step, inner):
    west, east = refs[-2:]
    if not inner:
        top, bottom = refs[:2]

        @pl.when(step == 0)
        def _():
            top[...] = value[: 3 * COLS].reshape(3, COLS, CHANS).astype(bf16)

        @pl.when(step == 1)
        def _():
            bottom[...] = value[5 * COLS :].reshape(3, COLS, CHANS).astype(bf16)

    for g in range(GROUPS):
        cs = slice(128 * g, 128 * g + 128)
        edge[...] = value[:, cs]
        for c in range(3):
            at = pl.ds(pl.multiple_of(step * 8, 8), 8)
            west[c, at, cs] = edge[pl.ds(c, 8, stride=COLS), :].astype(bf16)
            east[c, at, cs] = edge[pl.ds(COLS - 3 + c, 8, stride=COLS), :].astype(bf16)


def edge_kernel(first, last, west, east, edge):
    for ref, out, at in ((first, west, 0), (last, east, 5)):
        for g in range(GROUPS):
            cs = slice(128 * g, 128 * g + 128)
            edge[...] = ref[:, :, cs].reshape(ROWS * 8, 128).astype(f32)
            for c in range(3):
                out[c, :, cs] = edge[pl.ds(at + c, ROWS, stride=8), :].astype(bf16)


def pack_kernel(split, *refs):
    pieces, (n, s, west, east) = refs[:-4], refs[-4:]
    for side, out in ((0, west), (1, east)):
        if split:
            out[:, 0:16] = pieces[2 * side][...]
            out[:, 16:32] = pieces[2 * side + 1][...]
        else:
            v = pieces[side]
            for block, row in enumerate((0, 24, 8, 16)):
                out[:, 8 * block : 8 * block + 8] = v[:, row : row + 8]
        for at, ref in ((32, n), (40, s)):
            cut = slice(COLS - 8, COLS) if side else slice(0, 8)
            v = [ref[r, cut, :].astype(f32) for r in range(3)]
            for c in range(3):
                k = c + 5 if side else c
                rows = [v[r][k : k + 1] for r in range(3)] + [jnp.zeros((5, CHANS), f32)]
                out[c, at : at + 8] = jnp.concatenate(rows, axis=0).astype(bf16)


def fold_kernel(win, ain, bin_, wout, aout, bout, filters, win_out, wout_out, taps):
    @pl.when((pl.program_id(0) == 0) & (pl.program_id(1) == 0))
    def _():
        for t in range(49):
            v = filters[t]
            for l in range(2):
                for g in range(8):
                    at = 128 * (g % GROUPS)
                    taps[l, t, g : g + 1, :] = v[l : l + 1, at : at + 128]

    win_out[...] = (win[...].astype(f32) + adapter_scale * t_dot(ain[...], bin_[...])).astype(bf16)
    wout_out[...] = (wout[...].astype(f32) + adapter_scale * t_dot(aout[...], bout[...])).astype(bf16)


def first_kernel(inner, flags, x, cv, w, e, taps, bias, gain, shift, scale, win, wout, ain, aout, *refs):
    refs = refs[5 if inner else 0 :]
    bias, gain, shift, scale = (v[0:1, :] for v in (bias, gain, shift, scale))
    nrm, hid, slope, mid_in, mid_out, y = refs[:6]
    edges, (he, line, edge) = refs[6:-3], refs[-3:]
    step = pl.program_id(0)
    tile = step + 1 if inner else 3 * step

    @pl.when(step == 0)
    def _():
        hold_strips(he, w, e, flags)

    norm_rows(cv, he, taps, line, tile, bias, gain, shift, nrm)
    nb = nrm[...]
    mid_in[...] = dot_t(nb, ain[...]).astype(bf16)
    out = jnp.zeros((TILE, CHANS), f32)
    mid = jnp.zeros((TILE, RANK), f32)
    for c in range(0, HIDDEN, CHUNK):
        cs = slice(c, c + CHUNK)
        value, sl = gelu_parts(dot(nb, win[:, cs]))
        h = value.astype(bf16)
        hid[:, cs] = h
        slope[:, cs] = sl.astype(bf16)
        out = out + dot(h, wout[cs, :])
        mid = mid + dot_t(h, aout[:, cs])
    mid_out[...] = mid.astype(bf16)
    result = x[...].reshape(TILE, CHANS).astype(f32) + scale * out
    y[...] = result.reshape(TROWS, COLS, CHANS).astype(bf16)
    put_edges(edge, result, edges, step, inner)


def second_kernel(
    inner, flags, x, cv, w, e, taps, bias, gain, shift, scale, win, wout, ain, aout, bin_, bout, cot, *refs
):
    bias, gain, shift, scale = (v[1:2, :] for v in (bias, gain, shift, scale))
    if inner:
        before, refs = refs[1], refs[2:]
    out_ref, grads, gc = refs[:3]
    edges, (he, line, edge, nrm, xh, rs) = refs[3:-6], refs[-6:]
    step = pl.program_id(0)
    tile = step + 1 if inner else 3 * step

    @pl.when(step == 0)
    def _():
        hold_strips(he, w, e, flags)
        grads[...] = before[...] if inner else jnp.zeros_like(grads)

    norm_rows(cv, he, taps, line, tile, bias, gain, shift, nrm, xh, rs)
    nb = nrm[...]
    go = (cot[...].reshape(TILE, CHANS).astype(f32) * scale).astype(bf16)
    mid_in = dot_t(nb, ain[...]).astype(bf16)
    gm_out = (adapter_scale * dot_t(go, bout[...])).astype(bf16)
    out = jnp.zeros((TILE, CHANS), f32)
    gn = jnp.zeros((TILE, CHANS), f32)
    mid = jnp.zeros((TILE, RANK), f32)
    gm_in = jnp.zeros((TILE, RANK), f32)
    for c in range(0, HIDDEN, CHUNK):
        cs = slice(c, c + CHUNK)
        value, sl = gelu_parts(dot(nb, win[:, cs]))
        h = value.astype(bf16)
        gpre = (dot_t(go, wout[cs, :]) * sl).astype(bf16)
        out = out + dot(h, wout[cs, :])
        mid = mid + dot_t(h, aout[:, cs])
        gn = gn + dot_t(gpre, win[:, cs])
        gm_in = gm_in + dot_t(gpre, bin_[:, cs])
        grads[:, 512 + c : 512 + c + CHUNK] += t_dot(mid_in, gpre)
        grads[:, 2560 + c : 2560 + c + CHUNK] += t_dot(gm_out, h)
    gm_in = (adapter_scale * gm_in).astype(bf16)
    grads[:, 0:512] += t_dot(gm_in, nb)
    grads[:, 4608:5120] += t_dot(mid.astype(bf16), go)
    result = x[...].reshape(TILE, CHANS).astype(f32) + scale * out
    out_ref[...] = result.reshape(TROWS, COLS, CHANS).astype(bf16)
    u = gn * gain
    standard = xh[...]
    m1 = jnp.mean(u, -1, keepdims=True)
    m2 = jnp.mean(u * standard, -1, keepdims=True)
    inverse = jnp.concatenate([rs[...]] * GROUPS, axis=1)
    result = inverse * (u - m1 - standard * m2)
    gc[...] = result.reshape(TROWS, COLS, CHANS).astype(bf16)
    put_edges(edge, result, edges, step, inner)


def third_kernel(
    flags, cot, cv, w, e, taps, scale, wout, bin_, bout, mid_in, mid_out, nrm_far, hid_far, slope_far,
    grads, he, line, gos, nrm, hid, slope, sems,
):
    step = pl.program_id(0)
    scale = scale[0:1, :]

    def copies(t):
        at = pl.ds(pl.multiple_of(t * TILE, TILE), TILE)
        return [
            pltpu.make_async_copy(far.at[at, :], near.at[t], sems.at[k, t])
            for k, (far, near) in enumerate(((nrm_far, nrm), (hid_far, hid), (slope_far, slope)))
        ]

    @pl.when(step == 0)
    def _():
        for t in range(PIXELS // TILE):
            for copy in copies(t):
                copy.start()
        hold_strips(he, w, e, flags)
        grads[...] = jnp.zeros_like(grads)

    def rows(i, c):
        g = cot[i].astype(f32) + whole_row(cv, he, taps, True, line, step, i)
        gos[row_of(i), :] = (g * scale).astype(bf16)
        return c

    lax.fori_loop(0, TROWS, rows, 0, unroll=8)
    for copy in copies(step):
        copy.wait()
    nb = nrm[step]
    go = gos[...]
    mi = mid_in[...]
    gm_out = (adapter_scale * dot_t(go, bout[...])).astype(bf16)
    gm_in = jnp.zeros((TILE, RANK), f32)
    for c in range(0, HIDDEN, CHUNK):
        cs = slice(c, c + CHUNK)
        gpre = (dot_t(go, wout[cs, :]) * slope[step, :, cs].astype(f32)).astype(bf16)
        gm_in = gm_in + dot_t(gpre, bin_[:, cs])
        grads[:, 512 + c : 512 + c + CHUNK] += t_dot(mi, gpre)
        grads[:, 2560 + c : 2560 + c + CHUNK] += t_dot(gm_out, hid[step, :, cs])
    gm_in = (adapter_scale * gm_in).astype(bf16)
    grads[:, 0:512] += t_dot(gm_in, nb)
    grads[:, 4608:5120] += t_dot(mid_out[...], go)


MICROSECONDS = {'conv': 8, 'fold': 5, 'first_outer': 7, 'first_inner': 7, 'second_outer': 10, 'second_inner': 10, 'third': 9, 'edges': 1, 'pack': 1}
SMEM = pl.BlockSpec(memory_space=pltpu.SMEM)
ANY = pl.BlockSpec(memory_space=pl.ANY)
HE = pltpu.VMEM((40 * 48, 128), f32)
LINE = pltpu.VMEM((HALF * 8, 128), f32)
EDGE = pltpu.VMEM((TILE, 128), f32)


def fixed(*shape):
    return pl.BlockSpec(shape, lambda *t: (0,) * len(shape), pipeline_mode=pl.Buffered(1))


def layer(l, *shape):
    return pl.BlockSpec((None,) + shape, lambda t: (l,) + (0,) * len(shape), pipeline_mode=pl.Buffered(1))


def tiled(place, *shape):
    return pl.BlockSpec(shape, lambda t: (place(t),) + (0,) * (len(shape) - 1))


def call(kernel, name, grid, ins, outs, scratch, aliases={}, limit=26, far=()):
    return pl.pallas_call(
        kernel,
        grid=grid if isinstance(grid, tuple) else (grid,),
        out_shape=[
            pltpu.HBM(shape, dtype) if k in far else jax.ShapeDtypeStruct(shape, dtype)
            for k, (shape, dtype, _) in enumerate(outs)
        ],
        in_specs=[spec for _, spec in ins],
        out_specs=[spec for _, _, spec in outs],
        scratch_shapes=scratch,
        input_output_aliases=aliases,
        name=name,
        cost_estimate=pl.CostEstimate(flops=MICROSECONDS[name] * 10**9, bytes_accessed=10**6, transcendentals=0),
        compiler_params=pltpu.CompilerParams(vmem_limit_bytes=limit * 2**20),
    )(*[array for array, _ in ins])


def conv(arrays, sources, n, s, taps, l, flip, flags):
    return call(
        functools.partial(conv_kernel, sources, flip),
        "conv",
        4,
        [(flags, SMEM)]
        + [(a, fixed(*a.shape)) for a in arrays]
        + [(n, fixed(3, COLS, CHANS)), (s, fixed(3, COLS, CHANS))]
        + [(taps, layer(l, 49, 8, 128))],
        [((PIXELS * 4, 128), f32, tiled(lambda t: t, TILE * 4, 128))],
        [
            pltpu.VMEM((40, COLS, CHANS), bf16),
            pltpu.VMEM((SPAN * 8, 128), f32),
            pltpu.VMEM((40 * WIDE * 8, 128), f32),
        ],
        limit=12,
    )[0]


def swap(v, axis):
    n = lax.axis_size(axis)
    after = [(i, (i + 1) % n) for i in range(n)]
    before = [(j, i) for i, j in after]
    return lax.ppermute(v[1], axis, after), lax.ppermute(v[0], axis, before)


def strips(columns, north, south):
    sent = call(
        functools.partial(pack_kernel, len(columns) == 4),
        "pack",
        1,
        [(v, fixed(*v.shape)) for v in (*columns, north, south)],
        [((3, STRIP, CHANS), bf16, fixed(3, STRIP, CHANS))] * 2,
        [],
        limit=6,
    )
    return swap(sent, "col")


def total(first, second):
    core = lax.axis_index("col") % 2
    mine = jnp.where(core == 0, first, second)
    other = jnp.where(core == 0, second, first).astype(bf16)
    pair = [(i, i ^ 1) for i in range(16)]
    part = (mine + lax.ppermute(other, "col", pair).astype(f32)).astype(bf16)
    for even, odd in ((32, 4), (64, 8), (4, 1), (8, 16), (1, 32), (16, 64)):
        pairs = [(i, i ^ (odd if i & 2 else even)) for i in range(128)]
        other = lax.ppermute(part, ("row", "col", "rep"), pairs)
        part = (part.astype(f32) + other.astype(f32)).astype(bf16)
    back = lax.ppermute(part, "col", pair)
    return jnp.stack([jnp.where(core == 0, part, back), jnp.where(core == 0, back, part)]).astype(f32)


def normalize(stacked):
    mean = jnp.mean(stacked * stacked, axis=(1, 2), keepdims=True)
    return stacked * lax.rsqrt(mean + step_eps)


def body(
    features,
    cotangent,
    depthwise_filters,
    depthwise_bias_vector,
    layernorm_gain,
    layernorm_shift,
    inner_frozen_weight,
    outer_frozen_weight,
    inner_down_factor,
    inner_up_factor,
    outer_down_factor,
    outer_up_factor,
    branch_channel_scale,
):
    x0 = features.reshape(ROWS, COLS, CHANS)
    cot = cotangent.reshape(ROWS, COLS, CHANS)
    ain, bin_ = inner_down_factor.transpose(0, 2, 1), inner_up_factor
    aout, bout = outer_down_factor.transpose(0, 2, 1), outer_up_factor
    filters = depthwise_filters.transpose(1, 2, 0, 3).reshape(49, 2, CHANS)
    bias, gain, shift, scale = (
        depthwise_bias_vector, layernorm_gain, layernorm_shift, branch_channel_scale
    )
    row, col = lax.axis_index("row"), lax.axis_index("col")
    flags = jnp.stack(
        [row > 0, row < lax.axis_size("row") - 1, col > 0, col < lax.axis_size("col") - 1]
    ).astype(f32)

    west, east = call(
        edge_kernel,
        "edges",
        1,
        [(x0, pl.BlockSpec((ROWS, 8, CHANS), lambda t, k=k: (0, k, 0))) for k in (0, 3)],
        [((3, ROWS, CHANS), bf16, fixed(3, ROWS, CHANS))] * 2,
        [pltpu.VMEM((ROWS * 8, 128), f32)],
        limit=6,
    )
    north, south = swap((x0[:3], x0[-3:]), "row")
    part = HIDDEN // 4
    wide = (None, CHANS, part), lambda l, c: (l, 0, c)
    tall = (None, part, CHANS), lambda l, c: (l, c, 0)
    flat = (None, RANK, part), lambda l, c: (l, 0, c)
    full = (None, RANK, CHANS), lambda l, c: (l, 0, 0)
    win, wout, taps = call(
        fold_kernel,
        "fold",
        (2, 4),
        [
            (inner_frozen_weight, pl.BlockSpec(*wide)),
            (ain, pl.BlockSpec(*full)),
            (bin_, pl.BlockSpec(*flat)),
            (outer_frozen_weight, pl.BlockSpec(*tall)),
            (aout, pl.BlockSpec(*flat)),
            (bout, pl.BlockSpec(*full)),
            (filters, fixed(49, 2, CHANS)),
        ],
        [
            ((2, CHANS, HIDDEN), bf16, pl.BlockSpec(*wide)),
            ((2, HIDDEN, CHANS), bf16, pl.BlockSpec(*tall)),
            ((2, 49, 8, 128), f32, fixed(2, 49, 8, 128)),
        ],
        [],
        limit=12,
    )
    west, east, win, wout = lax.optimization_barrier((west, east, win, wout))
    west, east = strips([west, east], north, south)
    cv = conv([x0], [[(0, 0, 32)]], north, south, taps, 0, False, flags)

    strip_spec = fixed(3, STRIP, CHANS)

    def common(l, place, x, x_place):
        return [
            (flags, SMEM),
            (x, tiled(x_place, TROWS, COLS, CHANS)),
            (cv, tiled(place, TILE * 4, 128)),
            (west, strip_spec),
            (east, strip_spec),
            (taps, layer(l, 49, 8, 128)),
            (bias, fixed(2, CHANS)),
            (gain, fixed(2, CHANS)),
            (shift, fixed(2, CHANS)),
            (scale, fixed(2, CHANS)),
            (win, layer(l, CHANS, HIDDEN)),
            (wout, layer(l, HIDDEN, CHANS)),
            (ain, layer(l, RANK, CHANS)),
            (aout, layer(l, RANK, HIDDEN)),
        ]

    def outer_place(t):
        return 3 * t

    def inner_place(t):
        return t + 1

    def same(t):
        return t

    row_edges = [((3, COLS, CHANS), bf16, fixed(3, COLS, CHANS))] * 2
    col_edges = [((3, 16, CHANS), bf16, fixed(3, 16, CHANS))] * 2
    half = ((16, COLS, CHANS), bf16, tiled(same, TROWS, COLS, CHANS))

    def kept(place):
        return [
            ((PIXELS, width), bf16, tiled(place, TILE, width))
            for width in (CHANS, HIDDEN, HIDDEN, RANK, RANK)
        ]

    *saved, outer, top, bottom, west_a, east_a = call(
        functools.partial(first_kernel, False),
        "first_outer",
        2,
        common(0, outer_place, x0, outer_place),
        kept(outer_place) + [half] + row_edges + col_edges,
        [HE, LINE, EDGE],
        far=(0, 1, 2),
    )
    north, south = swap((top, bottom), "row")
    ins = common(0, inner_place, x0, inner_place)
    *saved, inner, west_b, east_b = call(
        functools.partial(first_kernel, True),
        "first_inner",
        2,
        ins + [(v, ANY) for v in saved],
        kept(inner_place) + [half] + col_edges,
        [HE, LINE, EDGE],
        {len(ins) + i: i for i in range(5)},
        far=(0, 1, 2),
    )
    split = [[(0, 0, 8), (8, 24, 8)], [(0, 8, 16)]]
    west, east = strips([west_a, west_b, east_a, east_b], north, south)
    cv = conv([outer, inner], split, north, south, taps, 1, False, flags)

    def second(place):
        return [
            (bin_, layer(1, RANK, HIDDEN)),
            (bout, layer(1, RANK, CHANS)),
            (cot, tiled(place, TROWS, COLS, CHANS)),
        ]

    def results(place):
        return [
            ((ROWS, COLS, CHANS), bf16, tiled(place, TROWS, COLS, CHANS)),
            ((RANK, GRADS), f32, fixed(RANK, GRADS)),
            half,
        ]

    work = [
        HE,
        LINE,
        EDGE,
        pltpu.VMEM((TILE, CHANS), bf16),
        pltpu.VMEM((TILE, CHANS), f32),
        pltpu.VMEM((TILE, 128), f32),
    ]
    out, grads1, outer_g, top, bottom, west_a, east_a = call(
        functools.partial(second_kernel, False),
        "second_outer",
        2,
        common(1, outer_place, outer, same) + second(outer_place),
        results(outer_place) + row_edges + col_edges,
        work,
    )
    north, south = swap((top, bottom), "row")
    ins = common(1, inner_place, inner, same) + second(inner_place)
    out, grads1, inner_g, west_b, east_b = call(
        functools.partial(second_kernel, True),
        "second_inner",
        2,
        ins + [(out, ANY), (grads1, fixed(RANK, GRADS))],
        results(inner_place) + col_edges,
        work,
        {len(ins): 0},
    )
    west, east = strips([west_a, west_b, east_a, east_b], north, south)
    cv = conv([outer_g, inner_g], split, north, south, taps, 1, True, flags)
    (grads0,) = call(
        third_kernel,
        "third",
        4,
        [
            (flags, SMEM),
            (cot, tiled(same, TROWS, COLS, CHANS)),
            (cv, tiled(same, TILE * 4, 128)),
            (west, strip_spec),
            (east, strip_spec),
            (taps, layer(1, 49, 8, 128)),
            (scale, fixed(2, CHANS)),
            (wout, layer(0, HIDDEN, CHANS)),
            (bin_, layer(0, RANK, HIDDEN)),
            (bout, layer(0, RANK, CHANS)),
        ]
        + [(v, tiled(same, TILE, RANK)) for v in saved[3:]]
        + [(v, pl.BlockSpec(memory_space=pltpu.HBM)) for v in saved[:3]],
        [((RANK, GRADS), f32, fixed(RANK, GRADS))],
        [HE, LINE, pltpu.VMEM((TILE, CHANS), bf16)]
        + [pltpu.VMEM((4, TILE, width), bf16) for width in (CHANS, HIDDEN, HIDDEN)]
        + [pltpu.SemaphoreType.DMA((3, 4))],
    )
    sums = total(grads0, grads1)
    return (
        out[None],
        normalize(sums[:, :, 0:512].transpose(0, 2, 1)),
        normalize(adapter_scale * sums[:, :, 512:2560]),
        normalize(sums[:, :, 2560:4608].transpose(0, 2, 1)),
        normalize(adapter_scale * sums[:, :, 4608:5120]),
    )


def solution(mesh):
    tile = P("rep", "row", "col", None)
    return jax.shard_map(
        body,
        mesh=mesh,
        in_specs=(tile, tile) + (P(),) * 11,
        out_specs=(tile, P(), P(), P(), P()),
        check_vma=False,
    )
```

```python
import functools

import jax
import jax.numpy as jnp
from jax import lax
from jax.experimental import pallas as pl
from jax.experimental.pallas import tpu as pltpu
from jax.sharding import PartitionSpec as P

BLOCK_COUNT = 2
ROWS, COLS, CHANS, HIDDEN, RANK = 32, 32, 512, 2048, 16
PIXELS = ROWS * COLS
GROUPS = CHANS // 128
HALF = COLS // 2
SPAN = 32
OFFSET = 5
TROWS = 8
TILE = TROWS * COLS
CHUNK = 2048
STRIP = 48
GRADS = 2 * (CHANS + HIDDEN)

adapter_scale = 2.0
norm_eps = 1e-06
step_eps = 1e-06
gelu_coef = 0.7978845608
f32, bf16 = jnp.float32, jnp.bfloat16


def dot(a, b):
    return jnp.dot(a, b, preferred_element_type=f32)


def dot_t(a, b):
    return lax.dot_general(a, b, (((1,), (1,)), ((), ())), preferred_element_type=f32)


def t_dot(a, b):
    return lax.dot_general(a, b, (((0,), (0,)), ((), ())), preferred_element_type=f32)


CENTRE = [(k, g, 0, 8 * k + 8) for k in (0, 1, 2) for g in range(GROUPS)] + [
    (k, g, 1, 8 * k - 8) for k in (1, 2, 3) for g in range(GROUPS)
]


def spread(xs, row, values):
    for k, g, half, at in CENTRE:
        start = (row * SPAN + at) * 8 + half * GROUPS + g
        xs[pl.ds(start, 8, stride=8), :] = values[8 * k : 8 * k + 8, 128 * g : 128 * g + 128]


def conv_kernel(sources, flip, flags, *refs):
    xrefs, (n, s, taps, cv, xs) = refs[: len(sources)], refs[len(sources) :]
    step = pl.program_id(0)

    @pl.when(step == 0)
    def _():
        zero = jnp.zeros((8, 128), f32)
        for ref, pieces in zip(xrefs, sources):
            for at, row, count in pieces:

                def centre(i, c, ref=ref, at=at, row=row):
                    spread(xs, row + 3 + i, ref[at + i].astype(f32))
                    return c

                lax.fori_loop(0, count, centre, 0, unroll=4)
        for i in range(3):
            spread(xs, i, n[i].astype(f32) * flags[0])
            spread(xs, ROWS + 3 + i, s[i].astype(f32) * flags[1])
        left = lax.broadcasted_iota(jnp.int32, (8, 128), 0) < GROUPS

        def edge(r, c):
            for k in (5, 6, 7):
                at = pl.ds(pl.multiple_of((r * SPAN + k) * 8, 8), 8)
                xs[at, :] = jnp.where(left, zero, xs[at, :])
            for k in (24, 25, 26):
                at = pl.ds(pl.multiple_of((r * SPAN + k) * 8, 8), 8)
                xs[at, :] = jnp.where(left, xs[at, :], zero)
            return c

        lax.fori_loop(0, ROWS + 6, edge, 0, unroll=2)

    def row(i, c):
        first = jnp.zeros((8, 128), f32)
        totals = [first] * HALF
        for a in range(7):
            base = pl.multiple_of((step * TROWS + i + a) * (SPAN * 8), SPAN * 8)
            line = [xs[pl.ds(base + (OFFSET + k) * 8, 8), :] for k in range(HALF + 6)]
            for b in range(7):
                tap = taps[48 - (a * 7 + b) if flip else a * 7 + b]
                for k in range(HALF):
                    totals[k] = totals[k] + line[k + b] * tap
        base = pl.multiple_of(i * (HALF * 8), HALF * 8)
        for k in range(HALF):
            cv[pl.ds(base + k * 8, 8), :] = totals[k]
        return c

    lax.fori_loop(0, TROWS, row, 0)


def hold_strips(he, w, e, flags):
    he[...] = jnp.zeros_like(he)
    for side, ref in ((0, w), (1, e)):
        for c in range(3):
            for block, row in ((4, 0), (5, 35), (0, 3), (2, 11), (3, 19), (1, 27)):
                v = ref[c, 8 * block : 8 * block + 8, :].astype(f32) * flags[2 + side]
                if block >= 4:
                    v = v * flags[block - 4]
                if block == 5:
                    v = v[0:3]
                for g in range(GROUPS):
                    start = (row * 6 + side * 3 + c) * 8 + side * GROUPS + g
                    he[pl.ds(start, v.shape[0], stride=48), :] = v[:, 128 * g : 128 * g + 128]


def whole_row(cv, he, taps, flip, line, tile, i):
    base = pl.multiple_of(i * (HALF * 8), HALF * 8)
    totals = [cv[pl.ds(base + k * 8, 8), :] for k in range(HALF)]
    for a in range(7):
        at = pl.multiple_of((tile * TROWS + i + a) * 48, 48)
        edge = [he[pl.ds(at + 8 * k, 8), :] for k in range(6)]
        pairs = [(k, h, h - k) for k in range(3) for h in range(k, 3)]
        pairs += [(k, 3 + h, 19 + h - k) for k in (13, 14, 15) for h in range(k - 12)]
        for k, h, b in pairs:
            totals[k] = totals[k] + edge[h] * taps[48 - (a * 7 + b) if flip else a * 7 + b]
    for k in range(HALF):
        line[k * 8 : k * 8 + 8, :] = totals[k]
    parts = []
    for k in range(4):
        start = (k % 2) * 64 + (k // 2) * GROUPS
        parts.append(
            jnp.concatenate([line[pl.ds(start + g, 8, stride=8), :] for g in range(GROUPS)], axis=1)
        )
    return jnp.concatenate(parts, axis=0)


def gelu_parts(v):
    square = v * v
    t = jnp.tanh(v * (gelu_coef + (gelu_coef * 0.044715) * square))
    h = 0.5 * t + 0.5
    value = v * h
    slope = h + value * (1.0 - t) * (gelu_coef + (3.0 * 0.044715 * gelu_coef) * square)
    return value, slope


def row_of(i):
    return pl.ds(pl.multiple_of(i * COLS, COLS), COLS)


def norm_rows(cv, he, taps, line, tile, bias, gain, shift, nrm, xh=None, rs=None):
    def body(i, c):
        conv = whole_row(cv, he, taps, False, line, tile, i) + bias
        centred = conv - jnp.mean(conv, -1, keepdims=True)
        inverse = lax.rsqrt(jnp.mean(centred * centred, -1, keepdims=True) + norm_eps)
        standard = centred * inverse
        nrm[row_of(i), :] = (standard * gain + shift).astype(bf16)
        if xh is not None:
            xh[row_of(i), :] = standard
            rs[row_of(i), :] = jnp.broadcast_to(inverse, (COLS, 128))
        return c

    lax.fori_loop(0, TROWS, body, 0, unroll=8)


def put_edges(edge, value, refs, step, inner):
    west, east = refs[-2:]
    if not inner:
        top, bottom = refs[:2]

        @pl.when(step == 0)
        def _():
            top[...] = value[: 3 * COLS].reshape(3, COLS, CHANS).astype(bf16)

        @pl.when(step == 1)
        def _():
            bottom[...] = value[5 * COLS :].reshape(3, COLS, CHANS).astype(bf16)

    for g in range(GROUPS):
        cs = slice(128 * g, 128 * g + 128)
        edge[...] = value[:, cs]
        for c in range(3):
            at = pl.ds(pl.multiple_of(step * 8, 8), 8)
            west[c, at, cs] = edge[pl.ds(c, 8, stride=COLS), :].astype(bf16)
            east[c, at, cs] = edge[pl.ds(COLS - 3 + c, 8, stride=COLS), :].astype(bf16)


def edge_kernel(first, last, west, east, edge):
    for ref, out, at in ((first, west, 0), (last, east, 5)):
        for g in range(GROUPS):
            cs = slice(128 * g, 128 * g + 128)
            edge[...] = ref[:, :, cs].reshape(ROWS * 8, 128).astype(f32)
            for c in range(3):
                out[c, :, cs] = edge[pl.ds(at + c, ROWS, stride=8), :].astype(bf16)


def pack_kernel(split, *refs):
    pieces, (n, s, west, east) = refs[:-4], refs[-4:]
    for side, out in ((0, west), (1, east)):
        if split:
            out[:, 0:16] = pieces[2 * side][...]
            out[:, 16:32] = pieces[2 * side + 1][...]
        else:
            v = pieces[side]
            for block, row in enumerate((0, 24, 8, 16)):
                out[:, 8 * block : 8 * block + 8] = v[:, row : row + 8]
        for at, ref in ((32, n), (40, s)):
            cut = slice(COLS - 8, COLS) if side else slice(0, 8)
            v = [ref[r, cut, :].astype(f32) for r in range(3)]
            for c in range(3):
                k = c + 5 if side else c
                rows = [v[r][k : k + 1] for r in range(3)] + [jnp.zeros((5, CHANS), f32)]
                out[c, at : at + 8] = jnp.concatenate(rows, axis=0).astype(bf16)


def fold_kernel(win, ain, bin_, wout, aout, bout, filters, win_out, wout_out, taps):
    @pl.when((pl.program_id(0) == 0) & (pl.program_id(1) == 0))
    def _():
        for t in range(49):
            v = filters[t]
            for l in range(2):
                for g in range(8):
                    at = 128 * (g % GROUPS)
                    taps[l, t, g : g + 1, :] = v[l : l + 1, at : at + 128]

    win_out[...] = (win[...].astype(f32) + adapter_scale * t_dot(ain[...], bin_[...])).astype(bf16)
    wout_out[...] = (wout[...].astype(f32) + adapter_scale * t_dot(aout[...], bout[...])).astype(bf16)


def first_kernel(inner, flags, x, cv, w, e, taps, bias, gain, shift, scale, win, wout, ain, aout, *refs):
    refs = refs[5 if inner else 0 :]
    bias, gain, shift, scale = (v[0:1, :] for v in (bias, gain, shift, scale))
    nrm, hid, slope, mid_in, mid_out, y = refs[:6]
    edges, (he, line, edge) = refs[6:-3], refs[-3:]
    step = pl.program_id(0)
    tile = step + 1 if inner else 3 * step

    @pl.when(step == 0)
    def _():
        hold_strips(he, w, e, flags)

    norm_rows(cv, he, taps, line, tile, bias, gain, shift, nrm)
    nb = nrm[...]
    mid_in[...] = dot_t(nb, ain[...]).astype(bf16)
    out = jnp.zeros((TILE, CHANS), f32)
    mid = jnp.zeros((TILE, RANK), f32)
    for c in range(0, HIDDEN, CHUNK):
        cs = slice(c, c + CHUNK)
        value, sl = gelu_parts(dot(nb, win[:, cs]))
        h = value.astype(bf16)
        hid[:, cs] = h
        slope[:, cs] = sl.astype(bf16)
        out = out + dot(h, wout[cs, :])
        mid = mid + dot_t(h, aout[:, cs])
    mid_out[...] = mid.astype(bf16)
    result = x[...].reshape(TILE, CHANS).astype(f32) + scale * out
    y[...] = result.reshape(TROWS, COLS, CHANS).astype(bf16)
    put_edges(edge, result, edges, step, inner)


def second_kernel(
    inner, flags, x, cv, w, e, taps, bias, gain, shift, scale, win, wout, ain, aout, bin_, bout, cot, *refs
):
    bias, gain, shift, scale = (v[1:2, :] for v in (bias, gain, shift, scale))
    if inner:
        before, refs = refs[1], refs[2:]
    out_ref, grads, gc = refs[:3]
    edges, (he, line, edge, nrm, xh, rs) = refs[3:-6], refs[-6:]
    step = pl.program_id(0)
    tile = step + 1 if inner else 3 * step

    @pl.when(step == 0)
    def _():
        hold_strips(he, w, e, flags)
        grads[...] = before[...] if inner else jnp.zeros_like(grads)

    norm_rows(cv, he, taps, line, tile, bias, gain, shift, nrm, xh, rs)
    nb = nrm[...]
    go = (cot[...].reshape(TILE, CHANS).astype(f32) * scale).astype(bf16)
    mid_in = dot_t(nb, ain[...]).astype(bf16)
    gm_out = (adapter_scale * dot_t(go, bout[...])).astype(bf16)
    out = jnp.zeros((TILE, CHANS), f32)
    gn = jnp.zeros((TILE, CHANS), f32)
    mid = jnp.zeros((TILE, RANK), f32)
    gm_in = jnp.zeros((TILE, RANK), f32)
    for c in range(0, HIDDEN, CHUNK):
        cs = slice(c, c + CHUNK)
        value, sl = gelu_parts(dot(nb, win[:, cs]))
        h = value.astype(bf16)
        gpre = (dot_t(go, wout[cs, :]) * sl).astype(bf16)
        out = out + dot(h, wout[cs, :])
        mid = mid + dot_t(h, aout[:, cs])
        gn = gn + dot_t(gpre, win[:, cs])
        gm_in = gm_in + dot_t(gpre, bin_[:, cs])
        grads[:, 512 + c : 512 + c + CHUNK] += t_dot(mid_in, gpre)
        grads[:, 2560 + c : 2560 + c + CHUNK] += t_dot(gm_out, h)
    gm_in = (adapter_scale * gm_in).astype(bf16)
    grads[:, 0:512] += t_dot(gm_in, nb)
    grads[:, 4608:5120] += t_dot(mid.astype(bf16), go)
    result = x[...].reshape(TILE, CHANS).astype(f32) + scale * out
    out_ref[...] = result.reshape(TROWS, COLS, CHANS).astype(bf16)
    u = gn * gain
    standard = xh[...]
    m1 = jnp.mean(u, -1, keepdims=True)
    m2 = jnp.mean(u * standard, -1, keepdims=True)
    inverse = jnp.concatenate([rs[...]] * GROUPS, axis=1)
    result = inverse * (u - m1 - standard * m2)
    gc[...] = result.reshape(TROWS, COLS, CHANS).astype(bf16)
    put_edges(edge, result, edges, step, inner)


def third_kernel(
    flags, cot, cv, w, e, taps, scale, wout, bin_, bout, mid_in, mid_out, nrm_far, hid_far, slope_far,
    grads, he, line, gos, nrm, hid, slope, sems,
):
    step = pl.program_id(0)
    scale = scale[0:1, :]

    def copies(t):
        at = pl.ds(pl.multiple_of(t * TILE, TILE), TILE)
        return [
            pltpu.make_async_copy(far.at[at, :], near.at[t], sems.at[k, t])
            for k, (far, near) in enumerate(((nrm_far, nrm), (hid_far, hid), (slope_far, slope)))
        ]

    @pl.when(step == 0)
    def _():
        for t in range(PIXELS // TILE):
            for copy in copies(t):
                copy.start()
        hold_strips(he, w, e, flags)
        grads[...] = jnp.zeros_like(grads)

    def rows(i, c):
        g = cot[i].astype(f32) + whole_row(cv, he, taps, True, line, step, i)
        gos[row_of(i), :] = (g * scale).astype(bf16)
        return c

    lax.fori_loop(0, TROWS, rows, 0, unroll=8)
    for copy in copies(step):
        copy.wait()
    nb = nrm[step]
    go = gos[...]
    mi = mid_in[...]
    gm_out = (adapter_scale * dot_t(go, bout[...])).astype(bf16)
    gm_in = jnp.zeros((TILE, RANK), f32)
    for c in range(0, HIDDEN, CHUNK):
        cs = slice(c, c + CHUNK)
        gpre = (dot_t(go, wout[cs, :]) * slope[step, :, cs].astype(f32)).astype(bf16)
        gm_in = gm_in + dot_t(gpre, bin_[:, cs])
        grads[:, 512 + c : 512 + c + CHUNK] += t_dot(mi, gpre)
        grads[:, 2560 + c : 2560 + c + CHUNK] += t_dot(gm_out, hid[step, :, cs])
    gm_in = (adapter_scale * gm_in).astype(bf16)
    grads[:, 0:512] += t_dot(gm_in, nb)
    grads[:, 4608:5120] += t_dot(mid_out[...], go)


MICROSECONDS = {'conv': 8, 'fold': 5, 'first_outer': 7, 'first_inner': 7, 'second_outer': 10, 'second_inner': 10, 'third': 9, 'edges': 1, 'pack': 1}
SMEM = pl.BlockSpec(memory_space=pltpu.SMEM)
ANY = pl.BlockSpec(memory_space=pl.ANY)
HE = pltpu.VMEM((40 * 48, 128), f32)
LINE = pltpu.VMEM((HALF * 8, 128), f32)
EDGE = pltpu.VMEM((TILE, 128), f32)


def fixed(*shape):
    return pl.BlockSpec(shape, lambda *t: (0,) * len(shape), pipeline_mode=pl.Buffered(1))


def layer(l, *shape):
    return pl.BlockSpec((None,) + shape, lambda t: (l,) + (0,) * len(shape), pipeline_mode=pl.Buffered(1))


def tiled(place, *shape):
    return pl.BlockSpec(shape, lambda t: (place(t),) + (0,) * (len(shape) - 1))


def call(kernel, name, grid, ins, outs, scratch, aliases={}, limit=26, far=()):
    return pl.pallas_call(
        kernel,
        grid=grid if isinstance(grid, tuple) else (grid,),
        out_shape=[
            pltpu.HBM(shape, dtype) if k in far else jax.ShapeDtypeStruct(shape, dtype)
            for k, (shape, dtype, _) in enumerate(outs)
        ],
        in_specs=[spec for _, spec in ins],
        out_specs=[spec for _, _, spec in outs],
        scratch_shapes=scratch,
        input_output_aliases=aliases,
        name=name,
        cost_estimate=pl.CostEstimate(flops=MICROSECONDS[name] * 10**9, bytes_accessed=10**6, transcendentals=0),
        compiler_params=pltpu.CompilerParams(vmem_limit_bytes=limit * 2**20),
    )(*[array for array, _ in ins])


def conv(arrays, sources, n, s, taps, l, flip, flags):
    return call(
        functools.partial(conv_kernel, sources, flip),
        "conv",
        4,
        [(flags, SMEM)]
        + [(a, fixed(*a.shape)) for a in arrays]
        + [(n, fixed(3, COLS, CHANS)), (s, fixed(3, COLS, CHANS))]
        + [(taps, layer(l, 49, 8, 128))],
        [((PIXELS * 4, 128), f32, tiled(lambda t: t, TILE * 4, 128))],
        [
            pltpu.VMEM((40 * SPAN * 8, 128), f32),
        ],
        limit=12,
    )[0]


def swap(v, axis):
    n = lax.axis_size(axis)
    after = [(i, (i + 1) % n) for i in range(n)]
    before = [(j, i) for i, j in after]
    return lax.ppermute(v[1], axis, after), lax.ppermute(v[0], axis, before)


def strips(columns, north, south):
    sent = call(
        functools.partial(pack_kernel, len(columns) == 4),
        "pack",
        1,
        [(v, fixed(*v.shape)) for v in (*columns, north, south)],
        [((3, STRIP, CHANS), bf16, fixed(3, STRIP, CHANS))] * 2,
        [],
        limit=6,
    )
    return swap(sent, "col")


def total(first, second):
    core = lax.axis_index("col") % 2
    mine = jnp.where(core == 0, first, second)
    other = jnp.where(core == 0, second, first).astype(bf16)
    pair = [(i, i ^ 1) for i in range(16)]
    part = (mine + lax.ppermute(other, "col", pair).astype(f32)).astype(bf16)
    for even, odd in ((32, 4), (64, 8), (4, 1), (8, 16), (1, 32), (16, 64)):
        pairs = [(i, i ^ (odd if i & 2 else even)) for i in range(128)]
        other = lax.ppermute(part, ("row", "col", "rep"), pairs)
        part = (part.astype(f32) + other.astype(f32)).astype(bf16)
    back = lax.ppermute(part, "col", pair)
    return jnp.stack([jnp.where(core == 0, part, back), jnp.where(core == 0, back, part)]).astype(f32)


def normalize(stacked):
    mean = jnp.mean(stacked * stacked, axis=(1, 2), keepdims=True)
    return stacked * lax.rsqrt(mean + step_eps)


def body(
    features,
    cotangent,
    depthwise_filters,
    depthwise_bias_vector,
    layernorm_gain,
    layernorm_shift,
    inner_frozen_weight,
    outer_frozen_weight,
    inner_down_factor,
    inner_up_factor,
    outer_down_factor,
    outer_up_factor,
    branch_channel_scale,
):
    x0 = features.reshape(ROWS, COLS, CHANS)
    cot = cotangent.reshape(ROWS, COLS, CHANS)
    ain, bin_ = inner_down_factor.transpose(0, 2, 1), inner_up_factor
    aout, bout = outer_down_factor.transpose(0, 2, 1), outer_up_factor
    filters = depthwise_filters.transpose(1, 2, 0, 3).reshape(49, 2, CHANS)
    bias, gain, shift, scale = (
        depthwise_bias_vector, layernorm_gain, layernorm_shift, branch_channel_scale
    )
    row, col = lax.axis_index("row"), lax.axis_index("col")
    flags = jnp.stack(
        [row > 0, row < lax.axis_size("row") - 1, col > 0, col < lax.axis_size("col") - 1]
    ).astype(f32)

    west, east = call(
        edge_kernel,
        "edges",
        1,
        [(x0, pl.BlockSpec((ROWS, 8, CHANS), lambda t, k=k: (0, k, 0))) for k in (0, 3)],
        [((3, ROWS, CHANS), bf16, fixed(3, ROWS, CHANS))] * 2,
        [pltpu.VMEM((ROWS * 8, 128), f32)],
        limit=6,
    )
    north, south = swap((x0[:3], x0[-3:]), "row")
    part = HIDDEN // 4
    wide = (None, CHANS, part), lambda l, c: (l, 0, c)
    tall = (None, part, CHANS), lambda l, c: (l, c, 0)
    flat = (None, RANK, part), lambda l, c: (l, 0, c)
    full = (None, RANK, CHANS), lambda l, c: (l, 0, 0)
    win, wout, taps = call(
        fold_kernel,
        "fold",
        (2, 4),
        [
            (inner_frozen_weight, pl.BlockSpec(*wide)),
            (ain, pl.BlockSpec(*full)),
            (bin_, pl.BlockSpec(*flat)),
            (outer_frozen_weight, pl.BlockSpec(*tall)),
            (aout, pl.BlockSpec(*flat)),
            (bout, pl.BlockSpec(*full)),
            (filters, fixed(49, 2, CHANS)),
        ],
        [
            ((2, CHANS, HIDDEN), bf16, pl.BlockSpec(*wide)),
            ((2, HIDDEN, CHANS), bf16, pl.BlockSpec(*tall)),
            ((2, 49, 8, 128), f32, fixed(2, 49, 8, 128)),
        ],
        [],
        limit=60,
    )
    west, east, win, wout = lax.optimization_barrier((west, east, win, wout))
    west, east = strips([west, east], north, south)
    cv = conv([x0], [[(0, 0, 32)]], north, south, taps, 0, False, flags)

    strip_spec = fixed(3, STRIP, CHANS)

    def common(l, place, x, x_place):
        return [
            (flags, SMEM),
            (x, tiled(x_place, TROWS, COLS, CHANS)),
            (cv, tiled(place, TILE * 4, 128)),
            (west, strip_spec),
            (east, strip_spec),
            (taps, layer(l, 49, 8, 128)),
            (bias, fixed(2, CHANS)),
            (gain, fixed(2, CHANS)),
            (shift, fixed(2, CHANS)),
            (scale, fixed(2, CHANS)),
            (win, layer(l, CHANS, HIDDEN)),
            (wout, layer(l, HIDDEN, CHANS)),
            (ain, layer(l, RANK, CHANS)),
            (aout, layer(l, RANK, HIDDEN)),
        ]

    def outer_place(t):
        return 3 * t

    def inner_place(t):
        return t + 1

    def same(t):
        return t

    row_edges = [((3, COLS, CHANS), bf16, fixed(3, COLS, CHANS))] * 2
    col_edges = [((3, 16, CHANS), bf16, fixed(3, 16, CHANS))] * 2
    half = ((16, COLS, CHANS), bf16, tiled(same, TROWS, COLS, CHANS))

    def kept(place):
        return [
            ((PIXELS, width), bf16, tiled(place, TILE, width))
            for width in (CHANS, HIDDEN, HIDDEN, RANK, RANK)
        ]

    *saved, outer, top, bottom, west_a, east_a = call(
        functools.partial(first_kernel, False),
        "first_outer",
        2,
        common(0, outer_place, x0, outer_place),
        kept(outer_place) + [half] + row_edges + col_edges,
        [HE, LINE, EDGE],
        far=(0, 1, 2),
    )
    north, south = swap((top, bottom), "row")
    ins = common(0, inner_place, x0, inner_place)
    *saved, inner, west_b, east_b = call(
        functools.partial(first_kernel, True),
        "first_inner",
        2,
        ins + [(v, ANY) for v in saved],
        kept(inner_place) + [half] + col_edges,
        [HE, LINE, EDGE],
        {len(ins) + i: i for i in range(5)},
        far=(0, 1, 2),
    )
    split = [[(0, 0, 8), (8, 24, 8)], [(0, 8, 16)]]
    west, east = strips([west_a, west_b, east_a, east_b], north, south)
    cv = conv([outer, inner], split, north, south, taps, 1, False, flags)

    def second(place):
        return [
            (bin_, layer(1, RANK, HIDDEN)),
            (bout, layer(1, RANK, CHANS)),
            (cot, tiled(place, TROWS, COLS, CHANS)),
        ]

    def results(place):
        return [
            ((ROWS, COLS, CHANS), bf16, tiled(place, TROWS, COLS, CHANS)),
            ((RANK, GRADS), f32, fixed(RANK, GRADS)),
            half,
        ]

    work = [
        HE,
        LINE,
        EDGE,
        pltpu.VMEM((TILE, CHANS), bf16),
        pltpu.VMEM((TILE, CHANS), f32),
        pltpu.VMEM((TILE, 128), f32),
    ]
    out, grads1, outer_g, top, bottom, west_a, east_a = call(
        functools.partial(second_kernel, False),
        "second_outer",
        2,
        common(1, outer_place, outer, same) + second(outer_place),
        results(outer_place) + row_edges + col_edges,
        work,
    )
    north, south = swap((top, bottom), "row")
    ins = common(1, inner_place, inner, same) + second(inner_place)
    out, grads1, inner_g, west_b, east_b = call(
        functools.partial(second_kernel, True),
        "second_inner",
        2,
        ins + [(out, ANY), (grads1, fixed(RANK, GRADS))],
        results(inner_place) + col_edges,
        work,
        {len(ins): 0},
    )
    west, east = strips([west_a, west_b, east_a, east_b], north, south)
    cv = conv([outer_g, inner_g], split, north, south, taps, 1, True, flags)
    (grads0,) = call(
        third_kernel,
        "third",
        4,
        [
            (flags, SMEM),
            (cot, tiled(same, TROWS, COLS, CHANS)),
            (cv, tiled(same, TILE * 4, 128)),
            (west, strip_spec),
            (east, strip_spec),
            (taps, layer(1, 49, 8, 128)),
            (scale, fixed(2, CHANS)),
            (wout, layer(0, HIDDEN, CHANS)),
            (bin_, layer(0, RANK, HIDDEN)),
            (bout, layer(0, RANK, CHANS)),
        ]
        + [(v, tiled(same, TILE, RANK)) for v in saved[3:]]
        + [(v, pl.BlockSpec(memory_space=pltpu.HBM)) for v in saved[:3]],
        [((RANK, GRADS), f32, fixed(RANK, GRADS))],
        [HE, LINE, pltpu.VMEM((TILE, CHANS), bf16)]
        + [pltpu.VMEM((4, TILE, width), bf16) for width in (CHANS, HIDDEN, HIDDEN)]
        + [pltpu.SemaphoreType.DMA((3, 4))],
    )
    sums = total(grads0, grads1)
    return (
        out[None],
        normalize(sums[:, :, 0:512].transpose(0, 2, 1)),
        normalize(adapter_scale * sums[:, :, 512:2560]),
        normalize(sums[:, :, 2560:4608].transpose(0, 2, 1)),
        normalize(adapter_scale * sums[:, :, 4608:5120]),
    )


def solution(mesh):
    tile = P("rep", "row", "col", None)
    return jax.shard_map(
        body,
        mesh=mesh,
        in_specs=(tile, tile) + (P(),) * 11,
        out_specs=(tile, P(), P(), P(), P()),
        check_vma=False,
    )
```

```python
import functools

import jax
import jax.numpy as jnp
from jax import lax
from jax.experimental import pallas as pl
from jax.experimental.pallas import tpu as pltpu
from jax.sharding import PartitionSpec as P

BLOCK_COUNT = 2
ROWS, COLS, CHANS, HIDDEN, RANK = 32, 32, 512, 2048, 16
PIXELS = ROWS * COLS
GROUPS = CHANS // 128
HALF = COLS // 2
SPAN = 32
OFFSET = 5
TROWS = 8
TILE = TROWS * COLS
CHUNK = 2048
STRIP = 48
GRADS = 2 * (CHANS + HIDDEN)

adapter_scale = 2.0
norm_eps = 1e-06
step_eps = 1e-06
gelu_coef = 0.7978845608
f32, bf16 = jnp.float32, jnp.bfloat16


def dot(a, b):
    return jnp.dot(a, b, preferred_element_type=f32)


def dot_t(a, b):
    return lax.dot_general(a, b, (((1,), (1,)), ((), ())), preferred_element_type=f32)


def t_dot(a, b):
    return lax.dot_general(a, b, (((0,), (0,)), ((), ())), preferred_element_type=f32)


CENTRE = [(k, g, 0, 8 * k + 8) for k in (0, 1, 2) for g in range(GROUPS)] + [
    (k, g, 1, 8 * k - 8) for k in (1, 2, 3) for g in range(GROUPS)
]


def spread(xs, row, values):
    for k, g, half, at in CENTRE:
        start = (row * SPAN + at) * 8 + half * GROUPS + g
        xs[pl.ds(start, 8, stride=8), :] = values[8 * k : 8 * k + 8, 128 * g : 128 * g + 128]


def conv_kernel(sources, flip, flags, *refs):
    xrefs, (n, s, taps, cv, xs) = refs[: len(sources)], refs[len(sources) :]
    step = pl.program_id(0)

    @pl.when(step == 0)
    def _():
        zero = jnp.zeros((8, 128), f32)
        for ref, pieces in zip(xrefs, sources):
            for at, row, count in pieces:

                def centre(i, c, ref=ref, at=at, row=row):
                    spread(xs, row + 3 + i, ref[at + i].astype(f32))
                    return c

                lax.fori_loop(0, count, centre, 0, unroll=4)
        for i in range(3):
            spread(xs, i, n[i].astype(f32) * flags[0])
            spread(xs, ROWS + 3 + i, s[i].astype(f32) * flags[1])
        left = lax.broadcasted_iota(jnp.int32, (8, 128), 0) < GROUPS

        def edge(r, c):
            for k in (5, 6, 7):
                at = pl.ds(pl.multiple_of((r * SPAN + k) * 8, 8), 8)
                xs[at, :] = jnp.where(left, zero, xs[at, :])
            for k in (24, 25, 26):
                at = pl.ds(pl.multiple_of((r * SPAN + k) * 8, 8), 8)
                xs[at, :] = jnp.where(left, xs[at, :], zero)
            return c

        lax.fori_loop(0, ROWS + 6, edge, 0, unroll=2)

    def row(i, c):
        first = jnp.zeros((8, 128), f32)
        totals = [first] * HALF
        for a in range(7):
            base = pl.multiple_of((step * TROWS + i + a) * (SPAN * 8), SPAN * 8)
            line = [xs[pl.ds(base + (OFFSET + k) * 8, 8), :] for k in range(HALF + 6)]
            for b in range(7):
                tap = taps[48 - (a * 7 + b) if flip else a * 7 + b]
                for k in range(HALF):
                    totals[k] = totals[k] + line[k + b] * tap
        base = pl.multiple_of(i * (HALF * 8), HALF * 8)
        for k in range(HALF):
            cv[pl.ds(base + k * 8, 8), :] = totals[k]
        return c

    lax.fori_loop(0, TROWS, row, 0)


def hold_strips(he, w, e, flags):
    he[...] = jnp.zeros_like(he)
    for side, ref in ((0, w), (1, e)):
        for c in range(3):
            for block, row in ((4, 0), (5, 35), (0, 3), (2, 11), (3, 19), (1, 27)):
                v = ref[c, 8 * block : 8 * block + 8, :].astype(f32) * flags[2 + side]
                if block >= 4:
                    v = v * flags[block - 4]
                if block == 5:
                    v = v[0:3]
                for g in range(GROUPS):
                    start = (row * 6 + side * 3 + c) * 8 + side * GROUPS + g
                    he[pl.ds(start, v.shape[0], stride=48), :] = v[:, 128 * g : 128 * g + 128]


def whole_row(cv, he, taps, flip, line, tile, i):
    base = pl.multiple_of(i * (HALF * 8), HALF * 8)
    totals = [cv[pl.ds(base + k * 8, 8), :] for k in range(HALF)]
    for a in range(7):
        at = pl.multiple_of((tile * TROWS + i + a) * 48, 48)
        edge = [he[pl.ds(at + 8 * k, 8), :] for k in range(6)]
        pairs = [(k, h, h - k) for k in range(3) for h in range(k, 3)]
        pairs += [(k, 3 + h, 19 + h - k) for k in (13, 14, 15) for h in range(k - 12)]
        for k, h, b in pairs:
            totals[k] = totals[k] + edge[h] * taps[48 - (a * 7 + b) if flip else a * 7 + b]
    for k in range(HALF):
        line[k * 8 : k * 8 + 8, :] = totals[k]
    parts = []
    for k in range(4):
        start = (k % 2) * 64 + (k // 2) * GROUPS
        parts.append(
            jnp.concatenate([line[pl.ds(start + g, 8, stride=8), :] for g in range(GROUPS)], axis=1)
        )
    return jnp.concatenate(parts, axis=0)


def gelu_parts(v):
    square = v * v
    t = jnp.tanh(v * (gelu_coef + (gelu_coef * 0.044715) * square))
    h = 0.5 * t + 0.5
    value = v * h
    slope = h + value * (1.0 - t) * (gelu_coef + (3.0 * 0.044715 * gelu_coef) * square)
    return value, slope


def row_of(i):
    return pl.ds(pl.multiple_of(i * COLS, COLS), COLS)


def norm_rows(cv, he, taps, line, tile, bias, gain, shift, nrm, xh=None, rs=None):
    def body(i, c):
        conv = whole_row(cv, he, taps, False, line, tile, i) + bias
        centred = conv - jnp.mean(conv, -1, keepdims=True)
        inverse = lax.rsqrt(jnp.mean(centred * centred, -1, keepdims=True) + norm_eps)
        standard = centred * inverse
        nrm[row_of(i), :] = (standard * gain + shift).astype(bf16)
        if xh is not None:
            xh[row_of(i), :] = standard
            rs[row_of(i), :] = jnp.broadcast_to(inverse, (COLS, 128))
        return c

    lax.fori_loop(0, TROWS, body, 0, unroll=8)


def put_edges(edge, value, refs, step, inner):
    west, east = refs[-2:]
    if not inner:
        top, bottom = refs[:2]

        @pl.when(step == 0)
        def _():
            top[...] = value[: 3 * COLS].reshape(3, COLS, CHANS).astype(bf16)

        @pl.when(step == 1)
        def _():
            bottom[...] = value[5 * COLS :].reshape(3, COLS, CHANS).astype(bf16)

    for g in range(GROUPS):
        cs = slice(128 * g, 128 * g + 128)
        edge[...] = value[:, cs]
        for c in range(3):
            at = pl.ds(pl.multiple_of(step * 8, 8), 8)
            west[c, at, cs] = edge[pl.ds(c, 8, stride=COLS), :].astype(bf16)
            east[c, at, cs] = edge[pl.ds(COLS - 3 + c, 8, stride=COLS), :].astype(bf16)


def edge_kernel(first, last, west, east, edge):
    for ref, out, at in ((first, west, 0), (last, east, 5)):
        for g in range(GROUPS):
            cs = slice(128 * g, 128 * g + 128)
            edge[...] = ref[:, :, cs].reshape(ROWS * 8, 128).astype(f32)
            for c in range(3):
                out[c, :, cs] = edge[pl.ds(at + c, ROWS, stride=8), :].astype(bf16)


def pack_kernel(split, *refs):
    pieces, (n, s, west, east) = refs[:-4], refs[-4:]
    for side, out in ((0, west), (1, east)):
        if split:
            out[:, 0:16] = pieces[2 * side][...]
            out[:, 16:32] = pieces[2 * side + 1][...]
        else:
            v = pieces[side]
            for block, row in enumerate((0, 24, 8, 16)):
                out[:, 8 * block : 8 * block + 8] = v[:, row : row + 8]
        for at, ref in ((32, n), (40, s)):
            cut = slice(COLS - 8, COLS) if side else slice(0, 8)
            v = [ref[r, cut, :].astype(f32) for r in range(3)]
            for c in range(3):
                k = c + 5 if side else c
                rows = [v[r][k : k + 1] for r in range(3)] + [jnp.zeros((5, CHANS), f32)]
                out[c, at : at + 8] = jnp.concatenate(rows, axis=0).astype(bf16)


def fold_kernel(win, ain, bin_, wout, aout, bout, filters, win_out, wout_out, taps):
    @pl.when((pl.program_id(0) == 0) & (pl.program_id(1) == 0))
    def _():
        for t in range(49):
            v = filters[t]
            for l in range(2):
                for g in range(8):
                    at = 128 * (g % GROUPS)
                    taps[l, t, g : g + 1, :] = v[l : l + 1, at : at + 128]

    win_out[...] = (win[...].astype(f32) + adapter_scale * t_dot(ain[...], bin_[...])).astype(bf16)
    wout_out[...] = (wout[...].astype(f32) + adapter_scale * t_dot(aout[...], bout[...])).astype(bf16)


def first_kernel(inner, flags, x, cv, w, e, taps, bias, gain, shift, scale, win, wout, ain, aout, *refs):
    refs = refs[5 if inner else 0 :]
    bias, gain, shift, scale = (v[0:1, :] for v in (bias, gain, shift, scale))
    nrm, hid, slope, mid_in, mid_out, y = refs[:6]
    edges, (he, line, edge) = refs[6:-3], refs[-3:]
    step = pl.program_id(0)
    tile = step + 1 if inner else 3 * step

    @pl.when(step == 0)
    def _():
        hold_strips(he, w, e, flags)

    norm_rows(cv, he, taps, line, tile, bias, gain, shift, nrm)
    nb = nrm[...]
    mid_in[...] = dot_t(nb, ain[...]).astype(bf16)
    out = jnp.zeros((TILE, CHANS), f32)
    mid = jnp.zeros((TILE, RANK), f32)
    for c in range(0, HIDDEN, CHUNK):
        cs = slice(c, c + CHUNK)
        value, sl = gelu_parts(dot(nb, win[:, cs]))
        h = value.astype(bf16)
        hid[:, cs] = h
        slope[:, cs] = sl.astype(bf16)
        out = out + dot(h, wout[cs, :])
        mid = mid + dot_t(h, aout[:, cs])
    mid_out[...] = mid.astype(bf16)
    result = x[...].reshape(TILE, CHANS).astype(f32) + scale * out
    y[...] = result.reshape(TROWS, COLS, CHANS).astype(bf16)
    put_edges(edge, result, edges, step, inner)


def second_kernel(
    inner, flags, x, cv, w, e, taps, bias, gain, shift, scale, win, wout, ain, aout, bin_, bout, cot, *refs
):
    bias, gain, shift, scale = (v[1:2, :] for v in (bias, gain, shift, scale))
    if inner:
        before, refs = refs[1], refs[2:]
    out_ref, grads, gc = refs[:3]
    edges, (he, line, edge, nrm, xh, rs) = refs[3:-6], refs[-6:]
    step = pl.program_id(0)
    tile = step + 1 if inner else 3 * step

    @pl.when(step == 0)
    def _():
        hold_strips(he, w, e, flags)
        grads[...] = before[...] if inner else jnp.zeros_like(grads)

    norm_rows(cv, he, taps, line, tile, bias, gain, shift, nrm, xh, rs)
    nb = nrm[...]
    go = (cot[...].reshape(TILE, CHANS).astype(f32) * scale).astype(bf16)
    mid_in = dot_t(nb, ain[...]).astype(bf16)
    gm_out = (adapter_scale * dot_t(go, bout[...])).astype(bf16)
    out = jnp.zeros((TILE, CHANS), f32)
    gn = jnp.zeros((TILE, CHANS), f32)
    mid = jnp.zeros((TILE, RANK), f32)
    gm_in = jnp.zeros((TILE, RANK), f32)
    for c in range(0, HIDDEN, CHUNK):
        cs = slice(c, c + CHUNK)
        value, sl = gelu_parts(dot(nb, win[:, cs]))
        h = value.astype(bf16)
        gpre = (dot_t(go, wout[cs, :]) * sl).astype(bf16)
        out = out + dot(h, wout[cs, :])
        mid = mid + dot_t(h, aout[:, cs])
        gn = gn + dot_t(gpre, win[:, cs])
        gm_in = gm_in + dot_t(gpre, bin_[:, cs])
        grads[:, 512 + c : 512 + c + CHUNK] += t_dot(mid_in, gpre)
        grads[:, 2560 + c : 2560 + c + CHUNK] += t_dot(gm_out, h)
    gm_in = (adapter_scale * gm_in).astype(bf16)
    grads[:, 0:512] += t_dot(gm_in, nb)
    grads[:, 4608:5120] += t_dot(mid.astype(bf16), go)
    result = x[...].reshape(TILE, CHANS).astype(f32) + scale * out
    out_ref[...] = result.reshape(TROWS, COLS, CHANS).astype(bf16)
    u = gn * gain
    standard = xh[...]
    m1 = jnp.mean(u, -1, keepdims=True)
    m2 = jnp.mean(u * standard, -1, keepdims=True)
    inverse = jnp.concatenate([rs[...]] * GROUPS, axis=1)
    result = inverse * (u - m1 - standard * m2)
    gc[...] = result.reshape(TROWS, COLS, CHANS).astype(bf16)
    put_edges(edge, result, edges, step, inner)


def third_kernel(
    flags, cot, cv, w, e, taps, scale, wout, bin_, bout, mid_in, mid_out, nrm_far, hid_far, slope_far,
    grads, he, line, gos, nrm, hid, slope, sems,
):
    step = pl.program_id(0)
    scale = scale[0:1, :]

    def copies(t):
        at = pl.ds(pl.multiple_of(t * TILE, TILE), TILE)
        return [
            pltpu.make_async_copy(far.at[at, :], near.at[t], sems.at[k, t])
            for k, (far, near) in enumerate(((nrm_far, nrm), (hid_far, hid), (slope_far, slope)))
        ]

    @pl.when(step == 0)
    def _():
        for t in range(PIXELS // TILE):
            for copy in copies(t):
                copy.start()
        hold_strips(he, w, e, flags)
        grads[...] = jnp.zeros_like(grads)

    def rows(i, c):
        g = cot[i].astype(f32) + whole_row(cv, he, taps, True, line, step, i)
        gos[row_of(i), :] = (g * scale).astype(bf16)
        return c

    lax.fori_loop(0, TROWS, rows, 0, unroll=8)
    for copy in copies(step):
        copy.wait()
    nb = nrm[step]
    go = gos[...]
    mi = mid_in[...]
    gm_out = (adapter_scale * dot_t(go, bout[...])).astype(bf16)
    gm_in = jnp.zeros((TILE, RANK), f32)
    for c in range(0, HIDDEN, CHUNK):
        cs = slice(c, c + CHUNK)
        gpre = (dot_t(go, wout[cs, :]) * slope[step, :, cs].astype(f32)).astype(bf16)
        gm_in = gm_in + dot_t(gpre, bin_[:, cs])
        grads[:, 512 + c : 512 + c + CHUNK] += t_dot(mi, gpre)
        grads[:, 2560 + c : 2560 + c + CHUNK] += t_dot(gm_out, hid[step, :, cs])
    gm_in = (adapter_scale * gm_in).astype(bf16)
    grads[:, 0:512] += t_dot(gm_in, nb)
    grads[:, 4608:5120] += t_dot(mid_out[...], go)


MICROSECONDS = {'conv': 8, 'fold': 5, 'first_outer': 7, 'first_inner': 7, 'second_outer': 10, 'second_inner': 10, 'third': 9, 'edges': 1, 'pack': 1}
SMEM = pl.BlockSpec(memory_space=pltpu.SMEM)
ANY = pl.BlockSpec(memory_space=pl.ANY)
HE = pltpu.VMEM((40 * 48, 128), f32)
LINE = pltpu.VMEM((HALF * 8, 128), f32)
EDGE = pltpu.VMEM((TILE, 128), f32)


def fixed(*shape):
    return pl.BlockSpec(shape, lambda *t: (0,) * len(shape), pipeline_mode=pl.Buffered(1))


def layer(l, *shape):
    return pl.BlockSpec((None,) + shape, lambda t: (l,) + (0,) * len(shape), pipeline_mode=pl.Buffered(1))


def tiled(place, *shape):
    return pl.BlockSpec(shape, lambda t: (place(t),) + (0,) * (len(shape) - 1))


def call(kernel, name, grid, ins, outs, scratch, aliases={}, limit=26, far=()):
    return pl.pallas_call(
        kernel,
        grid=grid if isinstance(grid, tuple) else (grid,),
        out_shape=[
            pltpu.HBM(shape, dtype) if k in far else jax.ShapeDtypeStruct(shape, dtype)
            for k, (shape, dtype, _) in enumerate(outs)
        ],
        in_specs=[spec for _, spec in ins],
        out_specs=[spec for _, _, spec in outs],
        scratch_shapes=scratch,
        input_output_aliases=aliases,
        name=name,
        cost_estimate=pl.CostEstimate(flops=MICROSECONDS[name] * 10**9, bytes_accessed=10**6, transcendentals=0),
        compiler_params=pltpu.CompilerParams(vmem_limit_bytes=limit * 2**20),
    )(*[array for array, _ in ins])


def conv(arrays, sources, n, s, taps, l, flip, flags):
    return call(
        functools.partial(conv_kernel, sources, flip),
        "conv",
        4,
        [(flags, SMEM)]
        + [(a, fixed(*a.shape)) for a in arrays]
        + [(n, fixed(3, COLS, CHANS)), (s, fixed(3, COLS, CHANS))]
        + [(taps, layer(l, 49, 8, 128))],
        [((PIXELS * 4, 128), f32, tiled(lambda t: t, TILE * 4, 128))],
        [
            pltpu.VMEM((40 * SPAN * 8, 128), f32),
        ],
        limit=12,
    )[0]


def swap(v, axis):
    n = lax.axis_size(axis)
    after = [(i, (i + 1) % n) for i in range(n)]
    before = [(j, i) for i, j in after]
    return lax.ppermute(v[1], axis, after), lax.ppermute(v[0], axis, before)


def strips(columns, north, south):
    sent = call(
        functools.partial(pack_kernel, len(columns) == 4),
        "pack",
        1,
        [(v, fixed(*v.shape)) for v in (*columns, north, south)],
        [((3, STRIP, CHANS), bf16, fixed(3, STRIP, CHANS))] * 2,
        [],
        limit=6,
    )
    return swap(sent, "col")


def total(first, second):
    core = lax.axis_index("col") % 2
    mine = jnp.where(core == 0, first, second)
    other = jnp.where(core == 0, second, first).astype(bf16)
    pair = [(i, i ^ 1) for i in range(16)]
    part = (mine + lax.ppermute(other, "col", pair).astype(f32)).astype(bf16)
    for even, odd in ((32, 4), (64, 8), (4, 1), (8, 16), (1, 32), (16, 64)):
        pairs = [(i, i ^ (odd if i & 2 else even)) for i in range(128)]
        other = lax.ppermute(part, ("row", "col", "rep"), pairs)
        part = (part.astype(f32) + other.astype(f32)).astype(bf16)
    back = lax.ppermute(part, "col", pair)
    return jnp.stack([jnp.where(core == 0, part, back), jnp.where(core == 0, back, part)]).astype(f32)


def normalize(stacked):
    mean = jnp.mean(stacked * stacked, axis=(1, 2), keepdims=True)
    return stacked * lax.rsqrt(mean + step_eps)


def body(
    features,
    cotangent,
    depthwise_filters,
    depthwise_bias_vector,
    layernorm_gain,
    layernorm_shift,
    inner_frozen_weight,
    outer_frozen_weight,
    inner_down_factor,
    inner_up_factor,
    outer_down_factor,
    outer_up_factor,
    branch_channel_scale,
):
    x0 = features.reshape(ROWS, COLS, CHANS)
    cot = cotangent.reshape(ROWS, COLS, CHANS)
    ain, bin_ = inner_down_factor.transpose(0, 2, 1), inner_up_factor
    aout, bout = outer_down_factor.transpose(0, 2, 1), outer_up_factor
    filters = depthwise_filters.transpose(1, 2, 0, 3).reshape(49, 2, CHANS)
    bias, gain, shift, scale = (
        depthwise_bias_vector, layernorm_gain, layernorm_shift, branch_channel_scale
    )
    row, col = lax.axis_index("row"), lax.axis_index("col")
    flags = jnp.stack(
        [row > 0, row < lax.axis_size("row") - 1, col > 0, col < lax.axis_size("col") - 1]
    ).astype(f32)

    west, east = call(
        edge_kernel,
        "edges",
        1,
        [(x0, pl.BlockSpec((ROWS, 8, CHANS), lambda t, k=k: (0, k, 0))) for k in (0, 3)],
        [((3, ROWS, CHANS), bf16, fixed(3, ROWS, CHANS))] * 2,
        [pltpu.VMEM((ROWS * 8, 128), f32)],
        limit=6,
    )
    north, south = swap((x0[:3], x0[-3:]), "row")
    part = HIDDEN // 4
    wide = (None, CHANS, part), lambda l, c: (l, 0, c)
    tall = (None, part, CHANS), lambda l, c: (l, c, 0)
    flat = (None, RANK, part), lambda l, c: (l, 0, c)
    full = (None, RANK, CHANS), lambda l, c: (l, 0, 0)
    win, wout, taps = call(
        fold_kernel,
        "fold",
        (2, 4),
        [
            (inner_frozen_weight, pl.BlockSpec(*wide)),
            (ain, pl.BlockSpec(*full)),
            (bin_, pl.BlockSpec(*flat)),
            (outer_frozen_weight, pl.BlockSpec(*tall)),
            (aout, pl.BlockSpec(*flat)),
            (bout, pl.BlockSpec(*full)),
            (filters, fixed(49, 2, CHANS)),
        ],
        [
            ((2, CHANS, HIDDEN), bf16, pl.BlockSpec(*wide)),
            ((2, HIDDEN, CHANS), bf16, pl.BlockSpec(*tall)),
            ((2, 49, 8, 128), f32, fixed(2, 49, 8, 128)),
        ],
        [],
        limit=60,
    )
    west, east, win, wout = lax.optimization_barrier((west, east, win, wout))
    west, east = strips([west, east], north, south)
    cv = conv([x0], [[(0, 0, 32)]], north, south, taps, 0, False, flags)

    strip_spec = fixed(3, STRIP, CHANS)

    def common(l, place, x, x_place):
        return [
            (flags, SMEM),
            (x, tiled(x_place, TROWS, COLS, CHANS)),
            (cv, tiled(place, TILE * 4, 128)),
            (west, strip_spec),
            (east, strip_spec),
            (taps, layer(l, 49, 8, 128)),
            (bias, fixed(2, CHANS)),
            (gain, fixed(2, CHANS)),
            (shift, fixed(2, CHANS)),
            (scale, fixed(2, CHANS)),
            (win, layer(l, CHANS, HIDDEN)),
            (wout, layer(l, HIDDEN, CHANS)),
            (ain, layer(l, RANK, CHANS)),
            (aout, layer(l, RANK, HIDDEN)),
        ]

    def outer_place(t):
        return 3 * t

    def inner_place(t):
        return t + 1

    def same(t):
        return t

    row_edges = [((3, COLS, CHANS), bf16, fixed(3, COLS, CHANS))] * 2
    col_edges = [((3, 16, CHANS), bf16, fixed(3, 16, CHANS))] * 2
    half = ((16, COLS, CHANS), bf16, tiled(same, TROWS, COLS, CHANS))

    def kept(place):
        return [
            ((PIXELS, width), bf16, tiled(place, TILE, width))
            for width in (CHANS, HIDDEN, HIDDEN, RANK, RANK)
        ]

    *saved, outer, top, bottom, west_a, east_a = call(
        functools.partial(first_kernel, False),
        "first_outer",
        2,
        common(0, outer_place, x0, outer_place),
        kept(outer_place) + [half] + row_edges + col_edges,
        [HE, LINE, EDGE],
        far=(1,),
    )
    north, south = swap((top, bottom), "row")
    ins = common(0, inner_place, x0, inner_place)
    *saved, inner, west_b, east_b = call(
        functools.partial(first_kernel, True),
        "first_inner",
        2,
        ins + [(v, ANY) for v in saved],
        kept(inner_place) + [half] + col_edges,
        [HE, LINE, EDGE],
        {len(ins) + i: i for i in range(5)},
        far=(1,),
    )
    split = [[(0, 0, 8), (8, 24, 8)], [(0, 8, 16)]]
    west, east = strips([west_a, west_b, east_a, east_b], north, south)
    cv = conv([outer, inner], split, north, south, taps, 1, False, flags)

    def second(place):
        return [
            (bin_, layer(1, RANK, HIDDEN)),
            (bout, layer(1, RANK, CHANS)),
            (cot, tiled(place, TROWS, COLS, CHANS)),
        ]

    def results(place):
        return [
            ((ROWS, COLS, CHANS), bf16, tiled(place, TROWS, COLS, CHANS)),
            ((RANK, GRADS), f32, fixed(RANK, GRADS)),
            half,
        ]

    work = [
        HE,
        LINE,
        EDGE,
        pltpu.VMEM((TILE, CHANS), bf16),
        pltpu.VMEM((TILE, CHANS), f32),
        pltpu.VMEM((TILE, 128), f32),
    ]
    out, grads1, outer_g, top, bottom, west_a, east_a = call(
        functools.partial(second_kernel, False),
        "second_outer",
        2,
        common(1, outer_place, outer, same) + second(outer_place),
        results(outer_place) + row_edges + col_edges,
        work,
    )
    north, south = swap((top, bottom), "row")
    ins = common(1, inner_place, inner, same) + second(inner_place)
    out, grads1, inner_g, west_b, east_b = call(
        functools.partial(second_kernel, True),
        "second_inner",
        2,
        ins + [(out, ANY), (grads1, fixed(RANK, GRADS))],
        results(inner_place) + col_edges,
        work,
        {len(ins): 0},
    )
    west, east = strips([west_a, west_b, east_a, east_b], north, south)
    cv = conv([outer_g, inner_g], split, north, south, taps, 1, True, flags)
    (grads0,) = call(
        third_kernel,
        "third",
        4,
        [
            (flags, SMEM),
            (cot, tiled(same, TROWS, COLS, CHANS)),
            (cv, tiled(same, TILE * 4, 128)),
            (west, strip_spec),
            (east, strip_spec),
            (taps, layer(1, 49, 8, 128)),
            (scale, fixed(2, CHANS)),
            (wout, layer(0, HIDDEN, CHANS)),
            (bin_, layer(0, RANK, HIDDEN)),
            (bout, layer(0, RANK, CHANS)),
        ]
        + [(v, tiled(same, TILE, RANK)) for v in saved[3:]]
        + [(v, pl.BlockSpec(memory_space=pltpu.HBM)) for v in saved[:3]],
        [((RANK, GRADS), f32, fixed(RANK, GRADS))],
        [HE, LINE, pltpu.VMEM((TILE, CHANS), bf16)]
        + [pltpu.VMEM((4, TILE, width), bf16) for width in (CHANS, HIDDEN, HIDDEN)]
        + [pltpu.SemaphoreType.DMA((3, 4))],
    )
    sums = total(grads0, grads1)
    return (
        out[None],
        normalize(sums[:, :, 0:512].transpose(0, 2, 1)),
        normalize(adapter_scale * sums[:, :, 512:2560]),
        normalize(sums[:, :, 2560:4608].transpose(0, 2, 1)),
        normalize(adapter_scale * sums[:, :, 4608:5120]),
    )


def solution(mesh):
    tile = P("rep", "row", "col", None)
    return jax.shard_map(
        body,
        mesh=mesh,
        in_specs=(tile, tile) + (P(),) * 11,
        out_specs=(tile, P(), P(), P(), P()),
        check_vma=False,
    )
```
